32 devices in a mesh: dp: 8 (over y, x, core), seq: 4 (over z).
Axes of the slice: x: 2, y: 2, z: 4, core: 2. Of those that a mesh axis runs over, the one named last changes fastest.
Arguments:
- inputs: bfloat16 [24, 1024, 768], P('dp', 'seq'), may hold values from -6 to 6
- segment_ids: int32 [24, 1024], P('dp', 'seq'), may hold values from 0 to 3, never falling along the last dimension, each value on 1 to 512 neighbouring positions
- norm1_gain: bfloat16 [768], P('dp'), may hold values from 0.5 to 1.5
- norm1_shift: bfloat16 [768], P('dp'), may hold values from -1.5 to 1.5
- query_weight: bfloat16 [768, 768], P('dp'), may hold values from -0.4375 to 0.4375
- query_bias: bfloat16 [768], P('dp'), may hold values from -2.5 to 2.5
- key_weight: bfloat16 [768, 768], P('dp'), may hold values from -0.21875 to 0.21875
- value_weight: bfloat16 [768, 768], P('dp'), may hold values from -0.21875 to 0.21875
- value_bias: bfloat16 [768], P('dp'), may hold values from -1.5 to 1.5
- out_weight: bfloat16 [768, 768], P('dp'), may hold values from -0.625 to 0.625
- out_bias: bfloat16 [768], P('dp'), may hold values from -1.5 to 1.5
- norm2_gain: bfloat16 [768], P('dp'), may hold values from 0.5 to 1.5
- norm2_shift: bfloat16 [768], P('dp'), may hold values from -1.5 to 1.5
- fc1_weight: bfloat16 [768, 3072], P('dp'), may hold values from -0.21875 to 0.21875
- fc1_bias: bfloat16 [3072], P('dp'), may hold values from -1.5 to 1.5
- fc2_weight: bfloat16 [3072, 768], P('dp'), may hold values from -0.15625 to 0.15625
- fc2_bias: bfloat16 [768], P('dp'), may hold values from -1.5 to 1.5
- grad_output: bfloat16 [24, 1024, 768], P('dp', 'seq'), may hold values from -6 to 6
Outputs:
- output: bfloat16 [24, 1024, 768], P('dp', 'seq')
- grad_inputs: bfloat16 [24, 1024, 768], P('dp', 'seq')
- grad_norm1_gain: float32 [768], P('dp')
- grad_norm1_shift: float32 [768], P('dp')
- grad_query_weight: float32 [768, 768], P('dp')
- grad_query_bias: float32 [768], P('dp')
- grad_key_weight: float32 [768, 768], P('dp')
- grad_value_weight: float32 [768, 768], P('dp')
- grad_value_bias: float32 [768], P('dp')
- grad_out_weight: float32 [768, 768], P('dp')
- grad_out_bias: float32 [768], P('dp')
- grad_norm2_gain: float32 [768], P('dp')
- grad_norm2_shift: float32 [768], P('dp')
- grad_fc1_weight: float32 [768, 3072], P('dp')
- grad_fc1_bias: float32 [3072], P('dp')
- grad_fc2_weight: float32 [3072, 768], P('dp')
- grad_fc2_bias: float32 [768], P('dp')
The draws below stay inside these ranges and needn't reach their ends.
Inputs may be any that keep to these rules, and one draw needn't show every extreme that they name: `segment_ids`: within each sequence, segment numbers never fall along the positions; each segment is a run of 1 to 512 positions.
All inputs are finite; a program needn't handle non-finite values.
Results may differ from the reference program's by a relative error of at most 0.017.
Values may be sent and summed in bfloat16 or wider, within the bound.
No kernel may reach another device: no remote copies, remote signals or barrier semaphores. Data moves between devices by JAX's collectives and lax.ppermute only.
A program may use at most 192 MiB of HBM per device.

```python
import math
import jax
import jax.numpy as jnp
import numpy as np
from jax import lax

D = 768
H = 12
HD = 64
FF = 3072
SEGS = 4
L = 1024
SEQS = 24


def steps_of(key, dims, cuts, least, top_value):
    def one(axis_at, parts):
        heights = jax.random.uniform(jax.random.fold_in(jax.random.fold_in(key, 6), axis_at), (parts,), jnp.float32, least / len(cuts), top_value / len(cuts))
        return jnp.repeat(jnp.exp(heights), dims[axis_at] // parts).reshape((-1,) + (1,) * (len(dims) - axis_at - 1))

    level = one(*cuts[0])
    for cut in cuts[1:]:
        level = level * one(*cut)
    return level


def length_profile(number_of, total, reach, slope):
    loads = [(1 << 20) // math.isqrt(rank ** slope) + 1 for rank in range(2, number_of + 1)]
    spare, holding = total - reach - (number_of - 1), [1] * (number_of - 1)
    while spare > 0:
        movable = [i for i in range(number_of - 1) if holding[i] < reach]
        whole, left = sum([loads[i] for i in movable]), spare
        for i in movable:
            addition = min(reach - holding[i], max(1, left * loads[i] // whole), spare)
            holding[i] = holding[i] + addition
            spare = spare - addition
    return np.array([reach] + holding)


def uneven_parts(own_key, amount, total, bound, slope):
    if amount == 2:
        one = jax.random.randint(own_key, (), max(1, total - bound), min(bound, total - 1) + 1)
        return jnp.stack([one, total - one])
    lengths = jnp.asarray(length_profile(amount, total, bound, slope), jnp.int32)
    twos = (amount - 1) // 2
    source_of, sink = lengths[1:1 + 2 * twos:2], lengths[2:2 + 2 * twos:2]
    room = jnp.minimum(source_of - 1, bound - sink)
    passed = jax.random.randint(jax.random.fold_in(own_key, 1), (twos,), 0, 1 << 20) % (room + 1)
    lengths = lengths.at[1:1 + 2 * twos:2].set(source_of - passed).at[2:2 + 2 * twos:2].set(sink + passed)
    return lengths[jax.random.permutation(jax.random.fold_in(own_key, 2), amount)]


def bell_draw(own_key, dims, width, limit, split=(), dtype=jnp.bfloat16):
    array = jax.random.normal(own_key, dims, jnp.float32) * width
    if len(split) > 0:
        array = steps_of(own_key, dims, split, -0.22, 0.18) * array
    return jnp.clip(array, min=-limit, max=limit).astype(dtype)


def setup_inputs(seed: int = 0) -> dict:
    seeds = jax.random.split(jax.random.key(seed), 19)
    return {
        "inputs": bell_draw(seeds[0], (SEQS, L, D), 1.0, 6.0, ((0, 8), (1, 4))),
        "segment_ids": jax.vmap(lambda own: jnp.searchsorted(jnp.cumsum(uneven_parts(own, SEGS, L, L // 2, 0)), jnp.arange(L), side="right"))(jax.random.split(seeds[1], SEQS)).reshape((SEQS, L)).astype(jnp.int32),
        "norm1_gain": jnp.clip(1.0 + 0.1 * jax.random.normal(seeds[2], (D,), jnp.float32), 0.5, 1.5).astype(jnp.bfloat16),
        "norm1_shift": bell_draw(seeds[3], (D,), 0.3, 1.5, ((0, 8),)),
        "query_weight": bell_draw(seeds[4], (D, D), (D // 4) ** -0.5, 0.4375, ((0, 8),)),
        "query_bias": bell_draw(seeds[5], (D,), 0.5, 2.5, ((0, 8),)),
        "key_weight": bell_draw(seeds[6], (D, D), D ** -0.5, 0.21875, ((0, 8),)),
        "value_weight": bell_draw(seeds[7], (D, D), D ** -0.5, 0.21875, ((0, 8),)),
        "value_bias": bell_draw(seeds[8], (D,), 0.3, 1.5, ((0, 8),)),
        "out_weight": bell_draw(seeds[9], (D, D), (D // 8) ** -0.5, 0.625, ((0, 8),)),
        "out_bias": bell_draw(seeds[10], (D,), 0.3, 1.5, ((0, 8),)),
        "norm2_gain": jnp.clip(1.0 + 0.1 * jax.random.normal(seeds[11], (D,), jnp.float32), 0.5, 1.5).astype(jnp.bfloat16),
        "norm2_shift": bell_draw(seeds[12], (D,), 0.3, 1.5, ((0, 8),)),
        "fc1_weight": bell_draw(seeds[13], (D, FF), D ** -0.5, 0.21875, ((0, 8),)),
        "fc1_bias": bell_draw(seeds[14], (FF,), 0.3, 1.5, ((0, 8),)),
        "fc2_weight": bell_draw(seeds[15], (FF, D), (FF // 2) ** -0.5, 0.15625, ((0, 8),)),
        "fc2_bias": bell_draw(seeds[16], (D,), 0.3, 1.5, ((0, 8),)),
        "grad_output": bell_draw(seeds[17], (SEQS, L, D), 1.0, 6.0, ((0, 8), (1, 4))),
    }


@jax.custom_vjp
def low(v):
    return lax.optimization_barrier(v.astype(jnp.bfloat16)).astype(jnp.float32)

@jax.custom_vjp
def low_back(v):
    return v

def low_keep(v):
    return (low(v), None)

def low_pass(kept, grad):
    return (grad,)

def back_keep(v):
    return (v, None)

def back_low(kept, grad):
    return (low(grad),)
low.defvjp(low_keep, low_pass)
low_back.defvjp(back_keep, back_low)

def dense(left, right):
    return jnp.dot(left, right, precision=lax.Precision.HIGHEST, preferred_element_type=jnp.float32)

def layer_norm(values, gain, shift):
    center = values - lax.optimization_barrier(jnp.mean(values, axis=-1, keepdims=True))
    inverse = lax.rsqrt(lax.optimization_barrier(jnp.mean(center * center, axis=-1, keepdims=True)) + 1e-05)
    return center * inverse * gain + shift

def rounded_both(values):
    return low_back(low(values))

def attend_one(packed):
    query_seq, key_seq, value_seq, segment_row = packed
    scores = jnp.einsum('qhd,khd->hqk', query_seq, key_seq, precision=lax.Precision.HIGHEST) * HD ** (-0.5)
    scores = low_back(scores)
    same_segment = segment_row[:, None] == segment_row[None, :]
    scores = jnp.where(same_segment[None, :, :], scores, -1e+30)
    highest = lax.optimization_barrier(jnp.max(scores, axis=-1, keepdims=True))
    expon = jnp.exp(scores - highest)
    probs = expon / lax.optimization_barrier(jnp.sum(expon, axis=-1, keepdims=True))
    return jnp.einsum('hqk,khd->qhd', low(probs), value_seq, precision=lax.Precision.HIGHEST)

def forward(values, segments, params):
    first_gain, first_shift, w_query, b_query, w_key, w_value, b_value, w_out, b_out, second_gain, second_shift, w_up, b_up, w_down, b_down = params
    group = values.shape[0]
    act_one = low(layer_norm(values, first_gain, first_shift))
    query = rounded_both(dense(act_one, w_query) + b_query).reshape(group, L, H, HD)
    key = rounded_both(dense(act_one, w_key)).reshape(group, L, H, HD)
    value = rounded_both(dense(act_one, w_value) + b_value).reshape(group, L, H, HD)
    attn = lax.map(jax.checkpoint(attend_one), (query, key, value, segments))
    attn = rounded_both(attn.reshape(group, L, D))
    middle = values + low_back(dense(attn, w_out) + b_out)
    act_two = low(layer_norm(middle, second_gain, second_shift))
    pre_act = low_back(dense(act_two, w_up) + b_up)
    hidden = low(jax.nn.gelu(pre_act, approximate=False))
    return middle + low_back(dense(hidden, w_down) + b_down)

def reference(inputs, segment_ids, norm1_gain, norm1_shift, query_weight, query_bias, key_weight, value_weight, value_bias, out_weight, out_bias, norm2_gain, norm2_shift, fc1_weight, fc1_bias, fc2_weight, fc2_bias, grad_output):
    params = tuple((item.astype(jnp.float32) for item in (norm1_gain, norm1_shift, query_weight, query_bias, key_weight, value_weight, value_bias, out_weight, out_bias, norm2_gain, norm2_shift, fc1_weight, fc1_bias, fc2_weight, fc2_bias)))
    group = math.gcd(SEQS, 4)
    blocks = SEQS // group
    values_all = inputs.astype(jnp.float32).reshape(blocks, group, L, D)
    segments_all = segment_ids.reshape(blocks, group, L)
    cotangent_all = grad_output.astype(jnp.float32).reshape(blocks, group, L, D)

    def step(totals, block):
        values, segments, cotangent = block
        result, pullback = jax.vjp(lambda vals, prm: forward(vals, segments, prm), values, params)
        grad_values, grad_params = pullback(cotangent)
        totals = tuple((left + right for left, right in zip(totals, grad_params)))
        return (totals, (result.astype(jnp.bfloat16), grad_values.astype(jnp.bfloat16)))
    zeros = tuple((jnp.zeros_like(item) for item in params))
    totals, (results, grads) = lax.scan(step, zeros, (values_all, segments_all, cotangent_all))
    return (results.reshape(SEQS, L, D), grads.reshape(SEQS, L, D), totals[0], totals[1], totals[2], totals[3], totals[4], totals[5], totals[6], totals[7], totals[8], totals[9], totals[10], totals[11], totals[12], totals[13], totals[14])
```

```python
import functools

import jax
import jax.numpy as jnp
from jax import lax
from jax.experimental import pallas as pl
from jax.experimental.pallas import tpu as pltpu
from jax.sharding import PartitionSpec as P

F32 = jnp.float32
BF16 = jnp.bfloat16
HD = 64
LANES = 128
BIG = 1e30
EPSILON = 1e-05
MIB = 1 << 20

ANY = pl.BlockSpec(memory_space=pl.ANY)
VMEM = pl.BlockSpec(memory_space=pltpu.VMEM)


def nn(left, right):
    return lax.dot_general(left, right, (((1,), (0,)), ((), ())), preferred_element_type=F32)


def nt(left, right):
    return lax.dot_general(left, right, (((1,), (1,)), ((), ())), preferred_element_type=F32)


def tn(left, right):
    return lax.dot_general(left, right, (((0,), (0,)), ((), ())), preferred_element_type=F32)


def unit_of(values):
    center = values - jnp.mean(values, axis=-1, keepdims=True)
    inverse = lax.rsqrt(jnp.mean(center * center, axis=-1, keepdims=True) + EPSILON)
    return center * inverse, inverse


def norm_back(scaled, unit, inverse):
    return inverse * (
        scaled
        - jnp.mean(scaled, axis=-1, keepdims=True)
        - unit * jnp.mean(scaled * unit, axis=-1, keepdims=True)
    )


def column_sum(values):
    return jnp.sum(values, axis=0, keepdims=True)


def needed(scal, block, rows):
    low, high = scal[0], scal[0] + scal[1] * rows
    return (block * rows < high) & ((block + 1) * rows > low)


def cost(flops, moved, transcendentals=0):
    return pl.CostEstimate(flops=int(flops), bytes_accessed=int(moved), transcendentals=int(transcendentals))


def qkv_kernel(seq, scal, x0, xl, xr, xll, xrr, weights, vec, q_out, k_out, v_out, buf, sems):
    i = pl.program_id(0)
    place = scal[2]
    rows, width = buf.shape[1:]
    share = width // weights.shape[0]

    def each(block, slot, act):
        for delta, ref in ((0, x0.at[seq]), (-1, xl), (1, xr), (-2, xll), (2, xrr)):

            @pl.when(needed(scal, block, rows) & (block - place == delta))
            def _():
                act(pltpu.make_async_copy(ref, buf.at[slot], sems.at[slot]))

    @pl.when(i == 0)
    def _():
        each(i, 0, lambda copy: copy.start())

    @pl.when(i + 1 < pl.num_programs(0))
    def _():
        each(i + 1, (i + 1) % 2, lambda copy: copy.start())

    each(i, i % 2, lambda copy: copy.wait())

    @pl.when(needed(scal, i, rows))
    def _():
        unit, _ = unit_of(buf[i % 2].astype(F32))
        act = (unit * vec[0:1] + vec[1:2]).astype(BF16)
        for j, out in enumerate((q_out, k_out, v_out)):
            weight = weights[:, j * share : (j + 1) * share, :].reshape(width, width)
            result = nn(act, weight)
            if j == 0:
                result = (result + vec[2:3]).astype(BF16) * jnp.asarray(HD**-0.5, BF16)
            if j == 2:
                result = result + vec[3:4]
            out[...] = result.astype(BF16)


def qkv_call(seq, scal, x, others, weights, vec):
    _, rows, width = x.shape
    blocks = 4
    out = jax.ShapeDtypeStruct((blocks * rows, width), BF16)
    spec = pl.BlockSpec((rows, width), lambda i, s: (i, 0))
    return pl.pallas_call(
        functools.partial(qkv_kernel, seq),
        out_shape=(out, out, out),
        grid_spec=pltpu.PrefetchScalarGridSpec(
            num_scalar_prefetch=1,
            grid=(blocks,),
            in_specs=[ANY] * 5
            + [
                pl.BlockSpec(weights.shape, lambda i, s: (0, 0, 0), pipeline_mode=pl.Buffered(1)),
                pl.BlockSpec(vec.shape, lambda i, s: (0, 0), pipeline_mode=pl.Buffered(1)),
            ],
            out_specs=[spec] * 3,
            scratch_shapes=[pltpu.VMEM((2, rows, width), BF16), pltpu.SemaphoreType.DMA((2,))],
        ),
        compiler_params=pltpu.CompilerParams(
            dimension_semantics=("arbitrary",), vmem_limit_bytes=24 * MIB
        ),
        cost_estimate=cost(6 * blocks * rows * width * width, 12e6),
        name="qkv",
    )(scal, x, *others, weights, vec)


def lane_is(*wanted):
    lane = lax.broadcasted_iota(jnp.int32, (1, LANES), 1)
    hit = lane == wanted[0]
    for other in wanted[1:]:
        hit = hit | (lane == other)
    return hit


def head_mask(which):
    lane = lax.broadcasted_iota(jnp.int32, (1, LANES), 1)
    return (lane < HD) if which == 0 else (lane >= HD)


def half(pair, which):
    return jnp.where(head_mask(which), pair, jnp.zeros_like(pair))


def window(scal, chunks, rows):
    return pl.ds(pl.multiple_of(scal[0], LANES), chunks * rows)


def by_chunks(scal, body):
    for chunks in range(1, 5):

        @pl.when(scal[1] == chunks)
        def _():
            body(chunks)


def attend_kernel(scal, q, k, v, seg, qf, o_out, qf_out, feats):
    pair = pl.program_id(0)
    rows = q.shape[0]

    @pl.when(pair == 0)
    def _():
        feats[...] = qf[...].astype(F32)

    def body(chunks):
        keys = window(scal, chunks, rows)
        k_aug = jnp.concatenate([k[keys, :], seg[keys, :]], axis=1)
        v_aug = jnp.concatenate([v[keys, :], jnp.ones((chunks * rows, LANES), BF16)], axis=1)
        parts = []
        for which in range(2):
            q_aug = jnp.concatenate([half(q[...], which), qf[...]], axis=1)
            scores = nt(q_aug, k_aug)
            highest = jnp.max(scores, axis=-1, keepdims=True)
            expon = jnp.exp(scores - highest).astype(BF16)
            both = nn(expon, v_aug)
            totals = both[:, LANES:]
            parts.append(both[:, :LANES] / totals)
            lse = highest + jnp.log(totals)
            top = lse.astype(BF16).astype(F32)
            lane = 16 + 4 * (2 * pair + which)
            feats[...] = jnp.where(
                lane_is(lane), -top, jnp.where(lane_is(lane + 1), top - lse, feats[...])
            )
        o_out[...] = jnp.where(head_mask(0), parts[0], parts[1]).astype(BF16)

    by_chunks(scal, body)

    @pl.when(pair == pl.num_programs(0) - 1)
    def _():
        qf_out[...] = feats[...].astype(BF16)


def attend_call(scal, q, k, v, seg, qf, rows):
    total, width = q.shape
    pairs = width // LANES
    own = pl.BlockSpec((rows, LANES), lambda p, s: (s[2], p))
    every = pl.BlockSpec((total, LANES), lambda p, s: (0, p))
    return pl.pallas_call(
        attend_kernel,
        out_shape=(
            jax.ShapeDtypeStruct((rows, width), BF16),
            jax.ShapeDtypeStruct((rows, LANES), BF16),
        ),
        grid_spec=pltpu.PrefetchScalarGridSpec(
            num_scalar_prefetch=1,
            grid=(pairs,),
            in_specs=[
                own,
                every,
                every,
                pl.BlockSpec((total, LANES), lambda p, s: (0, 0)),
                pl.BlockSpec((rows, LANES), lambda p, s: (0, 0)),
            ],
            out_specs=[
                pl.BlockSpec((rows, LANES), lambda p, s: (0, p)),
                pl.BlockSpec((rows, LANES), lambda p, s: (0, 0)),
            ],
            scratch_shapes=[pltpu.VMEM((rows, LANES), F32)],
        ),
        compiler_params=pltpu.CompilerParams(
            dimension_semantics=("arbitrary",), vmem_limit_bytes=24 * MIB
        ),
        cost_estimate=cost(16 * rows * total * width, 5e6, rows * total * width // HD),
        name="attend",
    )(scal, q, k, v, seg, qf)


def middle_kernel(
    seq, x, attn, grad, qf, weights, vec, out, msg, hid, gpre, act2, branch, gmid, sums,
    wo, up, down, hid_s, gpre_s, sems, out_sems,
):
    parts, share, width = wo.shape
    rows = attn.shape[0]
    loads = [pltpu.make_async_copy(weights.at[:, 0:share, :], wo, sems.at[0])]
    for c in range(4):
        loads.append(
            pltpu.make_async_copy(
                weights.at[:, (1 + c) * share : (2 + c) * share, :], up.at[c], sems.at[1 + c]
            )
        )
    loads.append(
        pltpu.make_async_copy(weights.at[:, 5 * share : 9 * share, :], down, sems.at[5])
    )
    for load in (loads[0], loads[1], loads[5], loads[2], loads[3], loads[4]):
        load.start()
    loads[0].wait()
    w_out = wo[...].reshape(width, width)
    middle = x[seq].astype(F32) + nn(attn[...], w_out) + vec[4:5]
    unit, inverse = unit_of(middle)
    normed = (unit * vec[5:6] + vec[6:7]).astype(BF16)
    act2[...] = normed
    g = grad[seq]
    g_full = g.astype(F32)
    result = middle + vec[7:8]
    grad_two = jnp.zeros((rows, width), F32)
    stores = []
    for c in range(4):
        loads[1 + c].wait()
        if c == 0:
            loads[5].wait()
        w_up = up[c].reshape(width, width)
        if parts >= 4:
            step = parts // 4
            w_down = down[c * step : (c + 1) * step].reshape(width, width)
        else:
            w_down = down[0, c * width : (c + 1) * width]
        pre = nn(normed, w_up) + vec[8 + c : 9 + c]
        whole = 0.5 * (1.0 + lax.erf(pre * 0.7071067811865476))
        slope = whole + pre * jnp.exp(-0.5 * pre * pre) * 0.3989422804014327
        hidden = (pre * whole).astype(BF16)
        hid_s[c] = hidden
        result = result + nn(hidden, w_down)
        grad_pre = (nt(g, w_down) * slope).astype(BF16)
        gpre_s[c] = grad_pre
        grad_two = grad_two + nt(grad_pre, w_up)
        sums[4 + c : 5 + c] = column_sum(grad_pre.astype(F32))
        stores.append(pltpu.make_async_copy(hid_s.at[c], hid.at[c], out_sems.at[0, c]))
        stores.append(pltpu.make_async_copy(gpre_s.at[c], gpre.at[c], out_sems.at[1, c]))
        stores[-1].start()
        stores[-2].start()
    out[...] = result.astype(BF16)
    sums[0:1] = column_sum(grad_two * unit)
    sums[1:2] = column_sum(grad_two)
    grad_middle = g_full + norm_back(grad_two * vec[5:6], unit, inverse)
    gmid[...] = grad_middle
    grad_branch = grad_middle.astype(BF16)
    branch[...] = grad_branch
    sums[2:3] = column_sum(grad_branch.astype(F32))
    sums[3:4] = column_sum(g_full)
    sums[8:16] = jnp.zeros((8, width), F32)
    grad_attn = nt(grad_branch, w_out).astype(BF16)
    msg[:, :width] = grad_attn
    product = grad_attn.astype(F32) * attn[...].astype(F32)
    high = product.astype(BF16)
    low = (product - high.astype(F32)).astype(BF16)
    head = lax.broadcasted_iota(jnp.int32, (width, LANES), 0) // HD
    lane = lax.broadcasted_iota(jnp.int32, (width, LANES), 1) - 16 - 4 * head
    pick = jnp.where((lane == 2) | (lane == 3), 1.0, 0.0).astype(BF16)
    delta = nn(high, pick) + nn(low, pick)
    top = delta.astype(BF16).astype(F32)
    column = lax.broadcasted_iota(jnp.int32, (1, LANES), 1)
    heads = width // HD
    in_heads = (column >= 16) & (column < 16 + 4 * heads)
    features = jnp.where(
        in_heads & (column % 4 == 2),
        -top,
        jnp.where(in_heads & (column % 4 == 3), top - delta, qf[...].astype(F32)),
    )
    msg[:, width:] = features.astype(BF16)
    for store in stores:
        store.wait()


def middle_call(seq, x, attn, grad, qf, weights, vec):
    _, rows, width = x.shape
    parts = weights.shape[0]
    share = width // parts
    flat = jax.ShapeDtypeStruct((rows, width), BF16)
    chunked = jax.ShapeDtypeStruct((4, rows, width), BF16)
    return pl.pallas_call(
        functools.partial(middle_kernel, seq),
        out_shape=(
            flat,
            jax.ShapeDtypeStruct((rows, width + LANES), BF16),
            chunked,
            chunked,
            flat,
            flat,
            jax.ShapeDtypeStruct((rows, width), F32),
            jax.ShapeDtypeStruct((16, width), F32),
        ),
        in_specs=[VMEM, VMEM, VMEM, VMEM, ANY, VMEM],
        out_specs=[VMEM, VMEM, ANY, ANY, VMEM, VMEM, VMEM, VMEM],
        scratch_shapes=[
            pltpu.VMEM((parts, share, width), BF16),
            pltpu.VMEM((4, parts, share, width), BF16),
            pltpu.VMEM((parts, 4 * share, width), BF16),
            pltpu.VMEM((4, rows, width), BF16),
            pltpu.VMEM((4, rows, width), BF16),
            pltpu.SemaphoreType.DMA((6,)),
            pltpu.SemaphoreType.DMA((2, 4)),
        ],
        compiler_params=pltpu.CompilerParams(vmem_limit_bytes=48 * MIB),
        cost_estimate=cost(2 * 18 * rows * width * width, 20e6, 2 * rows * 4 * width),
        name="middle",
    )(x, attn, grad, qf, weights, vec)


def ffn_grads_kernel(count, *refs):
    hid, gpre, act2, attn, branch = (refs[count * k : count * (k + 1)] for k in range(5))
    grad, first, second = refs[5 * count :]
    i = pl.program_id(0)

    @pl.when(i == 0)
    def _():
        total = sum(tn(attn[s][...], branch[s][...]) for s in range(count))
        first[...] = total.astype(BF16).reshape(first.shape)

    @pl.when(i > 0)
    def _():
        total = sum(tn(act2[s][...], gpre[s][0]) for s in range(count))
        first[...] = total.astype(BF16).reshape(first.shape)
        total = sum(tn(hid[s][0], grad[s]) for s in range(count))
        second[...] = total.astype(BF16).reshape(second.shape)


def ffn_grads_call(parts, hid, gpre, act2, attn, branch, grad):
    count, rows, width = grad.shape
    share = width // parts
    chunk = pl.BlockSpec((1, rows, width), lambda i: (jnp.maximum(i - 1, 0), 0, 0))
    whole = pl.BlockSpec((rows, width), lambda i: (0, 0))
    step = parts // 4 if parts >= 4 else 1
    depth = 4 * share if parts >= 4 else width
    second_map = (
        (lambda i: (jnp.maximum(i - 1, 0), 0, 0))
        if parts >= 4
        else (lambda i: (0, jnp.maximum(i - 1, 0), 0))
    )
    return pl.pallas_call(
        functools.partial(ffn_grads_kernel, count),
        out_shape=(
            jax.ShapeDtypeStruct((parts, 5 * share, width), BF16),
            jax.ShapeDtypeStruct((parts, 4 * share, width), BF16),
        ),
        grid=(5,),
        in_specs=[chunk] * (2 * count)
        + [whole] * (3 * count)
        + [pl.BlockSpec(grad.shape, lambda i: (0, 0, 0))],
        out_specs=[
            pl.BlockSpec((parts, share, width), lambda i: (0, i, 0)),
            pl.BlockSpec((step, depth, width), second_map),
        ],
        compiler_params=pltpu.CompilerParams(
            dimension_semantics=("arbitrary",), vmem_limit_bytes=40 * MIB
        ),
        cost_estimate=cost(18 * count * rows * width * width, 25e6),
        name="ffn_grads",
    )(*hid, *gpre, *act2, *attn, *branch, grad)


def ones_at(rows, *wanted):
    return jnp.broadcast_to(jnp.where(lane_is(*wanted), 1.0, 0.0).astype(BF16), (rows, LANES))


def query_grads_kernel(scal, q, k, v, grad, qf, seg, dq_out):
    pair = pl.program_id(0)
    rows = q.shape[0]

    def body(chunks):
        keys = window(scal, chunks, rows)
        size = chunks * rows
        k_pair, v_pair, features = k[keys, :], v[keys, :], seg[keys, :]
        total = None
        for which in range(2):
            lane = 16 + 4 * (2 * pair + which)
            q_aug = jnp.concatenate([half(q[...], which), qf[...]], axis=1)
            k_aug = jnp.concatenate([k_pair, features + ones_at(size, lane, lane + 1)], axis=1)
            probs = jnp.exp(nt(q_aug, k_aug))
            g_aug = jnp.concatenate([half(grad[...], which), qf[...]], axis=1)
            v_aug = jnp.concatenate([v_pair, ones_at(size, lane + 2, lane + 3)], axis=1)
            grad_scores = (probs * nt(g_aug, v_aug)).astype(BF16)
            part = nn(grad_scores, half(k_pair, which))
            total = part if total is None else total + part
        dq_out[...] = (total * HD**-0.5).astype(BF16)

    by_chunks(scal, body)


def query_grads_call(scal, q, k, v, msg, seg):
    total, width = q.shape
    rows = msg.shape[0]
    pairs = width // LANES
    every = pl.BlockSpec((total, LANES), lambda p, s: (0, p))
    return pl.pallas_call(
        query_grads_kernel,
        out_shape=jax.ShapeDtypeStruct((rows, width), BF16),
        grid_spec=pltpu.PrefetchScalarGridSpec(
            num_scalar_prefetch=1,
            grid=(pairs,),
            in_specs=[
                pl.BlockSpec((rows, LANES), lambda p, s: (s[2], p)),
                every,
                every,
                pl.BlockSpec((rows, LANES), lambda p, s: (0, p)),
                pl.BlockSpec((rows, LANES), lambda p, s: (0, pairs)),
                pl.BlockSpec((total, LANES), lambda p, s: (0, 0)),
            ],
            out_specs=pl.BlockSpec((rows, LANES), lambda p, s: (0, p)),
        ),
        compiler_params=pltpu.CompilerParams(
            dimension_semantics=("arbitrary",), vmem_limit_bytes=24 * MIB
        ),
        cost_estimate=cost(24 * rows * total * width, 5e6, rows * total * width // HD),
        name="query_grads",
    )(scal, q, k, v, msg, msg, seg)


def key_grads_kernel(scal, q, k, v, seg, g0, gl, gr, gll, grr, dk_out, dv_out, grads, sems):
    pair = pl.program_id(0)
    rows = k.shape[0]
    width = grads.shape[1] - LANES

    @pl.when(pair == 0)
    def _():
        for act in (lambda copy: copy.start(), lambda copy: copy.wait()):
            for block in range(4):
                for delta, ref in ((0, g0), (-1, gl), (1, gr), (-2, gll), (2, grr)):

                    @pl.when(needed(scal, block, rows) & (block - scal[2] == delta))
                    def _():
                        target = grads.at[pl.ds(block * rows, rows)]
                        act(pltpu.make_async_copy(ref, target, sems.at[block]))

    def body(chunks):
        queries = window(scal, chunks, rows)
        q_pair = q[queries, :]
        g_pair = grads[queries, pl.ds(pl.multiple_of(pair * LANES, LANES), LANES)]
        features = grads[queries, width:]
        dk, dv = None, None
        for which in range(2):
            lane = 16 + 4 * (2 * pair + which)
            q_half, g_half = half(q_pair, which), half(g_pair, which)
            k_aug = jnp.concatenate([k[...], seg[...] + ones_at(rows, lane, lane + 1)], axis=1)
            v_aug = jnp.concatenate([v[...], ones_at(rows, lane + 2, lane + 3)], axis=1)
            probs = jnp.exp(nt(k_aug, jnp.concatenate([q_half, features], axis=1)))
            grad_probs = nt(v_aug, jnp.concatenate([g_half, features], axis=1))
            grad_scores = (probs * grad_probs).astype(BF16)
            dv_part, dk_part = nn(probs.astype(BF16), g_half), nn(grad_scores, q_half)
            dk = dk_part if dk is None else dk + dk_part
            dv = dv_part if dv is None else dv + dv_part
        dk_out[...] = dk.astype(BF16)
        dv_out[...] = dv.astype(BF16)

    by_chunks(scal, body)


def key_grads_call(scal, q, k, v, seg, msgs):
    total, width = q.shape
    rows = msgs[0].shape[0]
    pairs = width // LANES
    own = pl.BlockSpec((rows, LANES), lambda p, s: (s[2], p))
    out = pl.BlockSpec((rows, LANES), lambda p, s: (0, p))
    return pl.pallas_call(
        key_grads_kernel,
        out_shape=(jax.ShapeDtypeStruct((rows, width), BF16),) * 2,
        grid_spec=pltpu.PrefetchScalarGridSpec(
            num_scalar_prefetch=1,
            grid=(pairs,),
            in_specs=[
                pl.BlockSpec((total, LANES), lambda p, s: (0, p)),
                own,
                own,
                pl.BlockSpec((rows, LANES), lambda p, s: (s[2], 0)),
            ]
            + [ANY] * 5,
            out_specs=[out, out],
            scratch_shapes=[
                pltpu.VMEM((total, width + LANES), BF16),
                pltpu.SemaphoreType.DMA((4,)),
            ],
        ),
        compiler_params=pltpu.CompilerParams(
            dimension_semantics=("arbitrary",), vmem_limit_bytes=28 * MIB
        ),
        cost_estimate=cost(32 * rows * total * width, 6e6, rows * total * width // HD),
        name="key_grads",
    )(scal, q, k, v, seg, *msgs)


def last_kernel(count, x, gmid, dq, dk, dv, weights, vec, sums, gin, grads, acc_q, acc_k, acc_v, acc_s):
    i = pl.program_id(0)
    parts, _, width = weights.shape
    share = width // parts
    unit, inverse = unit_of(x[0].astype(F32))
    act = (unit * vec[0:1] + vec[1:2]).astype(BF16)
    given = [dq[0], dk[0], dv[0]]
    accs = (acc_q, acc_k, acc_v)
    grad_one = jnp.zeros(unit.shape, F32)
    for j in range(3):
        weight = weights[:, j * share : (j + 1) * share, :].reshape(width, width)
        grad_one = grad_one + nt(given[j], weight)
        part = tn(act, given[j])

        @pl.when(i == 0)
        def _():
            accs[j][...] = part

        @pl.when(i > 0)
        def _():
            accs[j][...] += part

    gin[0] = (gmid[0] + norm_back(grad_one * vec[0:1], unit, inverse)).astype(BF16)
    rows_now = [
        column_sum(grad_one * unit),
        column_sum(grad_one),
        column_sum(given[0].astype(F32)),
        column_sum(given[2].astype(F32)),
    ]

    @pl.when(i == 0)
    def _():
        acc_s[...] = jnp.zeros(acc_s.shape, F32)

    acc_s[0:8] += sums[0, 0:8]
    for j, row in enumerate(rows_now):
        acc_s[8 + j : 9 + j] += row

    @pl.when(i == count - 1)
    def _():
        for j in range(3):
            grads[:, j * share : (j + 1) * share, :] = (
                accs[j][...].astype(BF16).reshape(parts, share, width)
            )
        total = acc_s[...].astype(BF16)
        for part in range(parts):
            grads[part, 3 * share : 3 * share + 16, :] = total


def last_call(x, gmid, dq, dk, dv, weights, vec, sums):
    count, rows, width = x.shape
    parts, depth, _ = weights.shape
    block = pl.BlockSpec((1, rows, width), lambda i: (i, 0, 0))
    fixed3 = lambda i: (0, 0, 0)
    return pl.pallas_call(
        functools.partial(last_kernel, count),
        out_shape=(
            jax.ShapeDtypeStruct(x.shape, BF16),
            jax.ShapeDtypeStruct((parts, depth, width), BF16),
        ),
        grid=(count,),
        in_specs=[
            block,
            block,
            block,
            block,
            block,
            pl.BlockSpec(weights.shape, fixed3, pipeline_mode=pl.Buffered(1)),
            pl.BlockSpec(vec.shape, lambda i: (0, 0)),
            pl.BlockSpec((1, 16, width), lambda i: (i, 0, 0)),
        ],
        out_specs=[block, pl.BlockSpec((parts, depth, width), fixed3)],
        scratch_shapes=[pltpu.VMEM((width, width), F32)] * 3 + [pltpu.VMEM((16, width), F32)],
        compiler_params=pltpu.CompilerParams(
            dimension_semantics=("arbitrary",), vmem_limit_bytes=48 * MIB
        ),
        cost_estimate=cost(12 * count * rows * width * width, 20e6),
        name="last",
    )(x, gmid, dq, dk, dv, weights, vec, sums)


def shifted(array, pairs):
    return lax.ppermute(array, "seq", pairs)


RIGHT = [(0, 1), (1, 2), (2, 3)]
LEFT = [(1, 0), (2, 1), (3, 2)]
RIGHT_AGAIN = [(1, 2), (2, 3)]
LEFT_AGAIN = [(2, 1), (1, 0)]


def neighbours(array):
    left, right = shifted(array, RIGHT), shifted(array, LEFT)
    return left, right, shifted(left, RIGHT_AGAIN), shifted(right, LEFT_AGAIN)


def whole_segments(segments, place):
    seqs, rows = segments.shape
    left, right = shifted(segments, RIGHT), shifted(segments, LEFT)
    far = shifted(segments, [(0, 2), (1, 3), (2, 0), (3, 1)])
    blocks = []
    for i in range(4):
        delta = i - place
        value = jnp.where(delta == 0, segments, jnp.where(delta == -1, left, right))
        value = jnp.where(jnp.abs(delta) == 2, far, value)
        value = jnp.where(delta == -3, -1, jnp.where(delta == 3, 99, value))
        blocks.append(value)
    return jnp.stack(blocks, axis=1).reshape(seqs, 4 * rows)


def windows(whole, segments, place, me, rows):
    first, last = segments[:, :1], segments[:, -1:]
    low = jnp.sum((whole < first).astype(jnp.int32), axis=1)
    high = jnp.sum((whole <= last).astype(jnp.int32), axis=1)
    start = (low // LANES) * LANES
    chunks = (high - start + rows - 1) // rows
    end = jnp.where(place == 0, 3 * rows, 4 * rows)
    start = jnp.minimum(start, end - chunks * rows)
    other = jnp.zeros_like(start)
    return jnp.stack([start, chunks, other + place, other + me], axis=1)


def per_device(
    inputs,
    segment_ids,
    norm1_gain,
    norm1_shift,
    query_weight,
    query_bias,
    key_weight,
    value_weight,
    value_bias,
    out_weight,
    out_bias,
    norm2_gain,
    norm2_shift,
    fc1_weight,
    fc1_bias,
    fc2_weight,
    fc2_bias,
    grad_output,
):
    seqs, rows, width = inputs.shape
    devices = lax.axis_size("dp")
    share = query_weight.shape[0]
    place, me = lax.axis_index("seq"), lax.axis_index("dp")
    direct = share % 16 == 0

    small = jnp.concatenate(
        [
            norm1_gain, norm1_shift, query_bias, value_bias,
            out_bias, norm2_gain, norm2_shift, fc2_bias, fc1_bias,
        ]
    )
    small = jnp.pad(small, (0, 16 * width - small.shape[0])).reshape(16, width)
    first_part = jnp.concatenate([query_weight, key_weight, value_weight, small])
    up_part = fc1_weight.reshape(share, 4, width).transpose(1, 0, 2).reshape(4 * share, width)
    second_part = jnp.concatenate([out_weight, up_part, fc2_weight])
    others = [neighbours(inputs[s]) for s in range(seqs)]
    whole = whole_segments(segment_ids, place)

    first = lax.all_gather(first_part, "dp", axis=0)
    second = lax.all_gather(second_part, "dp", axis=0)

    small_all = first[:, 3 * share :, :].reshape(devices, -1)
    eight = small_all[:, : 8 * share].reshape(devices, 8, share).transpose(1, 0, 2).reshape(8, width)
    four = small_all[:, 8 * share : 12 * share].reshape(4, width)
    vec = jnp.concatenate([eight, four, four]).astype(F32)
    if not direct:
        first = jnp.concatenate(
            [first[:, j * share : (j + 1) * share].reshape(width, width) for j in range(3)]
            + [jnp.zeros((16, width), BF16)]
        )[None]
        second = jnp.concatenate(
            [second[:, j * share : (j + 1) * share].reshape(width, width) for j in range(5)]
            + [second[:, 5 * share :].reshape(4 * width, width)]
        )[None]
    parts = first.shape[0]

    scal = windows(whole, segment_ids, place, me, rows)
    lane = lax.broadcasted_iota(jnp.int32, (1, 1, LANES), 2)
    seg = (whole[:, :, None] == lane).astype(BF16)
    qf = jnp.where((lane < 4) & (lane != segment_ids[:, :, None]), -BIG, 0.0).astype(BF16)

    saved, outs = [], []
    for s in range(seqs):
        q, k, v = qkv_call(s, scal[s], inputs, others[s], first, vec)
        attn, qf_s = attend_call(scal[s], q, k, v, seg[s], qf[s], rows)
        saved.append((q, k, v, attn))
        outs.append(middle_call(s, inputs, attn, grad_output, qf_s, second, vec))
    out, msg, hid, gpre, act2, branch, gmid, sums = zip(*outs)
    grads = [neighbours(msg[s]) for s in range(seqs)]
    attn = [saved[s][3] for s in range(seqs)]
    ffn_one, ffn_two = ffn_grads_call(parts, hid, gpre, act2, attn, branch, grad_output)
    dq = [query_grads_call(scal[s], *saved[s][:3], msg[s], seg[s]) for s in range(seqs)]
    dkv = [
        key_grads_call(scal[s], *saved[s][:3], seg[s], (msg[s], *grads[s])) for s in range(seqs)
    ]
    grad_inputs, proj = last_call(
        inputs,
        jnp.stack(gmid),
        jnp.stack(dq),
        jnp.stack([pair[0] for pair in dkv]),
        jnp.stack([pair[1] for pair in dkv]),
        first,
        vec,
        jnp.stack(sums),
    )
    if direct:
        ffn_all = jnp.concatenate([ffn_one, ffn_two], axis=1)
    else:
        ffn_all = jnp.concatenate(
            [ffn_one[0].reshape(5, devices, share, width).transpose(1, 0, 2, 3).reshape(devices, 5 * share, width),
             ffn_two[0].reshape(devices, 4 * share, width)], axis=1)
        total = proj[0, 3 * width :]
        proj = jnp.concatenate(
            [proj[0, : 3 * width].reshape(3, devices, share, width).transpose(1, 0, 2, 3).reshape(devices, 3 * share, width),
             jnp.broadcast_to(total[None], (devices, 16, width))], axis=1)

    def reduced(array):
        part = lax.psum_scatter(array, "dp", scatter_dimension=0, tiled=True)[0]
        return lax.psum(part, "seq").astype(F32)

    ffn_done = reduced(ffn_all)
    proj_done = reduced(proj)
    vectors = proj_done[3 * share :]
    mine = lax.dynamic_slice(vectors, (0, me * share), (16, share))
    up_grad = ffn_done[share : 5 * share].reshape(4, share, width).transpose(1, 0, 2)
    up_bias = lax.dynamic_slice(vectors[4:8].reshape(4 * width), (me * 4 * share,), (4 * share,))
    return (
        jnp.stack(out),
        grad_inputs,
        mine[8],
        mine[9],
        proj_done[:share],
        mine[10],
        proj_done[share : 2 * share],
        proj_done[2 * share : 3 * share],
        mine[11],
        ffn_done[:share],
        mine[2],
        mine[0],
        mine[1],
        up_grad.reshape(share, 4 * width),
        up_bias,
        ffn_done[5 * share :],
        mine[3],
    )


def solution(mesh):
    token, matrix, vector = P("dp", "seq", None), P("dp", None), P("dp")
    return jax.shard_map(
        per_device,
        mesh=mesh,
        in_specs=(
            token, P("dp", "seq"), vector, vector, matrix, vector, matrix, matrix, vector,
            matrix, vector, vector, vector, matrix, vector, matrix, vector, token,
        ),
        out_specs=(
            token, token, vector, vector, matrix, vector, matrix, matrix, vector,
            matrix, vector, vector, vector, matrix, vector, matrix, vector,
        ),
        check_vma=False,
    )
```

```python
import functools

import jax
import jax.numpy as jnp
from jax import lax
from jax.experimental import pallas as pl
from jax.experimental.pallas import tpu as pltpu
from jax.sharding import PartitionSpec as P

F32 = jnp.float32
BF16 = jnp.bfloat16
HD = 64
LANES = 128
BIG = 1e30
EPSILON = 1e-05
MIB = 1 << 20

ANY = pl.BlockSpec(memory_space=pl.ANY)
VMEM = pl.BlockSpec(memory_space=pltpu.VMEM)


def nn(left, right):
    return lax.dot_general(left, right, (((1,), (0,)), ((), ())), preferred_element_type=F32)


def nt(left, right):
    return lax.dot_general(left, right, (((1,), (1,)), ((), ())), preferred_element_type=F32)


def tn(left, right):
    return lax.dot_general(left, right, (((0,), (0,)), ((), ())), preferred_element_type=F32)


def unit_of(values):
    center = values - jnp.mean(values, axis=-1, keepdims=True)
    inverse = lax.rsqrt(jnp.mean(center * center, axis=-1, keepdims=True) + EPSILON)
    return center * inverse, inverse


def norm_back(scaled, unit, inverse):
    return inverse * (
        scaled
        - jnp.mean(scaled, axis=-1, keepdims=True)
        - unit * jnp.mean(scaled * unit, axis=-1, keepdims=True)
    )


def column_sum(values):
    return jnp.sum(values, axis=0, keepdims=True)


def cost(flops, moved, transcendentals=0):
    return pl.CostEstimate(flops=int(flops / 4), bytes_accessed=int(moved / 4), transcendentals=0)


def params(limit=56, grid=1):
    return pltpu.CompilerParams(dimension_semantics=("arbitrary",) * grid, vmem_limit_bytes=limit * MIB)


def bits(rel):
    return (rel >> 1) & 1, (rel >> 2) & 1


def pack_kernel(wq, wk, wv, wo, up, down, x, seg, *rest):
    *vectors, first, second, tokens = rest
    share, width = wq.shape
    rows = x.shape[1]
    first[0:share] = wq[...]
    first[share : 2 * share] = wk[...]
    first[2 * share : 3 * share] = wv[...]
    first[3 * share :] = jnp.zeros((16, width), BF16)
    for j, vector in enumerate(vectors):
        size = vector.shape[1]
        first[3 * share + j : 3 * share + j + 1, 0:size] = vector[...]
    second[0:share] = wo[...]
    for c in range(4):
        second[(1 + c) * share : (2 + c) * share] = up[:, c * width : (c + 1) * width]
    second[5 * share :] = down[...]
    tokens[:, 0:rows] = x[...]
    tokens[:, rows:] = jnp.zeros((x.shape[0], 16, width), BF16)
    for s in range(x.shape[0]):
        tokens[s, rows : rows + 1, 0:rows] = seg[s : s + 1].astype(F32).astype(BF16)


def whole_spec(array):
    zeros = (0,) * len(array.shape)
    return pl.BlockSpec(array.shape, lambda i: zeros)


def pack_call(matrices, vectors, x, seg):
    share, width = matrices[0].shape
    args = (*matrices, x, seg, *[v.reshape(1, -1) for v in vectors])
    outs = (
        jax.ShapeDtypeStruct((3 * share + 16, width), BF16),
        jax.ShapeDtypeStruct((9 * share, width), BF16),
        jax.ShapeDtypeStruct((x.shape[0], x.shape[1] + 16, width), BF16),
    )
    return pl.pallas_call(
        pack_kernel,
        out_shape=outs,
        grid=(1,),
        in_specs=[whole_spec(a) for a in args],
        out_specs=[whole_spec(a) for a in outs],
        compiler_params=params(),
        cost_estimate=cost(0, 6e6),
        name="pack",
    )(*args)


def piece_copies(scal, pieces, low, size, target, sems):
    if len(pieces) == 1:
        return [pltpu.make_async_copy(pieces[0][0].at[:, pl.ds(low, size)], target, sems.at[0])]
    me, copies = scal[0, 3], []
    for ref, index, rel, start, stop in pieces:
        if start <= low and low + size <= stop:
            source = ref if index is None else ref.at[index]
            copies.append(
                pltpu.make_async_copy(
                    source.at[pl.ds(low - start, size)], target.at[me ^ rel], sems.at[rel]
                )
            )
    return copies


def first_pieces(refs):
    if len(refs) == 1:
        return [(refs[0],)]
    near, far = refs
    return [(near, j, 2 * j, 0, near.shape[1]) for j in range(4)] + [
        (far, j, 2 * j + 1, 0, far.shape[1]) for j in range(4)
    ]


def second_pieces(refs):
    if len(refs) == 1:
        return [(refs[0],)]
    full = refs[0].shape[0]
    split = refs[3].shape[0]
    pieces = []
    for core in range(2):
        own, x, y, xy_low, xy_high = refs[5 * core : 5 * core + 5]
        pieces += [(own, None, core, 0, full), (x, None, 2 + core, 0, full), (y, None, 4 + core, 0, full)]
        pieces += [(xy_low, None, 6 + core, 0, split), (xy_high, None, 6 + core, split, full)]
    return pieces


def start(copies):
    for copy in copies:
        copy.start()


def wait(copies):
    for copy in copies:
        copy.wait()


def unpack_kernel(near, far, scal, vec):
    me = scal[0, 3]
    share = 96
    width = vec.shape[1]
    low = near.shape[1] - 16
    total = jnp.zeros((16, width), F32)
    row = lax.broadcasted_iota(jnp.int32, (LANES, width), 0)
    column = lax.broadcasted_iota(jnp.int32, (LANES, width), 1)
    for rel in range(8):
        device = me ^ rel
        block = (near if rel % 2 == 0 else far)[rel // 2, low:, :]
        pick = jnp.where((row < share) & (column == row + device * share), 1.0, 0.0).astype(BF16)
        total = total + nn(block[:, 0:LANES], pick)
        bias = block[8:9, 0 : 4 * share].astype(F32)
        vec[pl.ds(8 + device // 2, 1), pl.ds(pl.multiple_of((device % 2) * 4 * share, LANES), 4 * share)] = bias
    vec[0:8] = total[0:8]
    vec[12:16] = jnp.zeros((4, width), F32)


def unpack_call(near, far, ids):
    width = near.shape[2]
    out = jax.ShapeDtypeStruct((16, width), F32)
    return pl.pallas_call(
        unpack_kernel,
        out_shape=out,
        grid=(1,),
        in_specs=[whole_spec(near), whole_spec(far), pl.BlockSpec(memory_space=pltpu.SMEM)],
        out_specs=whole_spec(out),
        compiler_params=params(),
        cost_estimate=cost(1e6, 4e6),
        name="unpack",
    )(near, far, ids)


def needed(scal, seq, slot, rows):
    low, high = scal[seq, 0], scal[seq, 0] + scal[seq, 1] * rows
    return (slot * rows < high) & ((slot + 1) * rows > low)


def project_kernel(far, pieces, scal, vec, *rest):
    sources = rest[: 2 if far else 3]
    rest = rest[len(sources) :]
    refs, (*outs, buf, weights, made, sems, wsems, out_sems) = rest[:pieces], rest[-9:]
    i = pl.program_id(0)
    steps = 1 if far else 3
    count, rows, width = buf.shape[1:]
    share = width // weights.shape[0]
    after = scal[0, 2] >= 2
    copies = piece_copies(scal, first_pieces(refs), 0, weights.shape[1], weights, wsems)
    if far:
        slot = jnp.where(after, 0, 4)
        used = needed(scal, 0, slot, rows)
        for s in range(1, count):
            used = used | needed(scal, s, slot, rows)
    else:
        slot = jnp.where(i == 0, 2, jnp.where(i == 1, 1, 3))
        used = True

    def load(step, act):
        for j, ref in enumerate(sources):
            when = (after == (j == 0)) if far else (step == j)

            @pl.when(when)
            def _():
                source = ref.at[:, pl.ds(0, rows)]
                act(pltpu.make_async_copy(source, buf.at[step % 2], sems.at[step % 2]))

    def stores(step, where):
        return [
            pltpu.make_async_copy(
                made.at[step % 2, t], outs[t].at[:, pl.ds(where * rows, rows)], out_sems.at[step % 2, t]
            )
            for t in range(3)
        ]

    @pl.when(i == 0)
    def _():
        load(0, lambda copy: copy.start())
        start(copies)

    @pl.when(i + 1 < steps)
    def _():
        load(i + 1, lambda copy: copy.start())

    load(i, lambda copy: copy.wait())

    @pl.when(i == 0)
    def _():
        wait(copies)

    @pl.when(i >= 2)
    def _():
        wait(stores(i, 0))

    def work():
        unit, _ = unit_of(buf[i % 2].reshape(count * rows, width).astype(F32))
        act = (unit * vec[0:1] + vec[1:2]).astype(BF16)
        for t in range(3):
            weight = weights[:, t * share : (t + 1) * share, :].reshape(width, width)
            result = nn(act, weight)
            if t == 0:
                result = (result + vec[2:3]).astype(BF16) * jnp.asarray(HD**-0.5, BF16)
            if t == 2:
                result = result + vec[3:4]
            made[i % 2, t] = result.astype(BF16).reshape(count, rows, width)
        start(stores(i, slot))

    if far:

        @pl.when(used)
        def _():
            work()
            wait(stores(0, 0))
    else:
        work()

        @pl.when(i == steps - 1)
        def _():
            wait(stores(i, 0))
            wait(stores(i - 1, 0))


def project_call(scal, sources, vec, first, before, seqs, rows):
    far = before is not None
    width = vec.shape[1]
    out = jax.ShapeDtypeStruct((seqs, 5 * rows, width), BF16)
    parts, depth = (8, first[0].shape[1]) if len(first) > 1 else first[0].shape[:2]
    steps = 1 if far else 3
    at = 2 + len(sources) + len(first)
    return pl.pallas_call(
        functools.partial(project_kernel, far, len(first)),
        out_shape=(out, out, out),
        grid=(steps,),
        in_specs=[pl.BlockSpec(memory_space=pltpu.SMEM), whole_spec(vec)]
        + [ANY] * (len(sources) + len(first) + (3 if far else 0)),
        out_specs=[ANY] * 3,
        scratch_shapes=[
            pltpu.VMEM((2, seqs, rows, width), BF16),
            pltpu.VMEM((parts, depth, width), BF16),
            pltpu.VMEM((2, 3, seqs, rows, width), BF16),
            pltpu.SemaphoreType.DMA((2,)),
            pltpu.SemaphoreType.DMA((8,)),
            pltpu.SemaphoreType.DMA((2, 3)),
        ],
        input_output_aliases={at: 0, at + 1: 1, at + 2: 2} if far else {},
        compiler_params=params(),
        cost_estimate=cost(6 * steps * seqs * rows * width * width, 8e6 * steps),
        name="far" if far else "near",
    )(scal, vec, *sources, *first, *(before or ()))


def lane_is(*wanted):
    lane = lax.broadcasted_iota(jnp.int32, (1, LANES), 1)
    hit = lane == wanted[0]
    for other in wanted[1:]:
        hit = hit | (lane == other)
    return hit


def head_mask(which):
    lane = lax.broadcasted_iota(jnp.int32, (1, LANES), 1)
    return (lane < HD) if which == 0 else (lane >= HD)


def half(pair, which):
    return jnp.where(head_mask(which), pair, jnp.zeros_like(pair))


def by_chunks(scal, seq, rows, body):
    for chunks in range(1, 5):

        @pl.when(scal[seq, 1] == chunks)
        def _():
            body(chunks * rows, pl.ds(pl.multiple_of(scal[seq, 0], LANES), chunks * rows))


def attend_kernel(at, scal, q, k, v, seg, qf, *rest):
    o_out, qf_out, feats = rest[-3:]
    seq, pair = at + pl.program_id(0), pl.program_id(1)
    rows = q.shape[1]

    @pl.when(pair == 0)
    def _():
        feats[...] = qf[0].astype(F32)

    def body(size, keys):
        k_aug = jnp.concatenate([k[0, keys, :], seg[0, keys, :]], axis=1)
        v_aug = jnp.concatenate([v[0, keys, :], jnp.ones((size, LANES), BF16)], axis=1)
        parts = []
        for which in range(2):
            q_aug = jnp.concatenate([half(q[0], which), qf[0]], axis=1)
            scores = nt(q_aug, k_aug)
            highest = jnp.max(scores, axis=-1, keepdims=True)
            expon = jnp.exp(scores - highest).astype(BF16)
            both = nn(expon, v_aug)
            totals = both[:, LANES:]
            parts.append(both[:, :LANES] / totals)
            lse = highest + jnp.log(totals)
            top = lse.astype(BF16).astype(F32)
            lane = 16 + 4 * (2 * pair + which)
            feats[...] = jnp.where(
                lane_is(lane), -top, jnp.where(lane_is(lane + 1), top - lse, feats[...])
            )
        o_out[0] = jnp.where(head_mask(0), parts[0], parts[1]).astype(BF16)

    by_chunks(scal, seq, rows, body)

    @pl.when(pair == pl.num_programs(1) - 1)
    def _():
        qf_out[0] = feats[...].astype(BF16)


def attend_call(at, count, scal, q, k, v, seg, qf, before):
    seqs, total, width = q.shape
    rows = qf.shape[1]
    pairs = width // LANES
    own = pl.BlockSpec((1, rows, LANES), lambda s, p, c: (at + s, 2, p))
    every = pl.BlockSpec((1, total, LANES), lambda s, p, c: (at + s, 0, p))
    return pl.pallas_call(
        functools.partial(attend_kernel, at),
        out_shape=(
            jax.ShapeDtypeStruct((seqs, rows, width), BF16),
            jax.ShapeDtypeStruct((seqs, rows, LANES), BF16),
        ),
        grid_spec=pltpu.PrefetchScalarGridSpec(
            num_scalar_prefetch=1,
            grid=(count, pairs),
            in_specs=[
                own,
                every,
                every,
                pl.BlockSpec((1, total, LANES), lambda s, p, c: (at + s, 0, 0)),
                pl.BlockSpec((1, rows, LANES), lambda s, p, c: (at + s, 0, 0)),
            ]
            + ([ANY] * 2 if before else []),
            out_specs=[
                pl.BlockSpec((1, rows, LANES), lambda s, p, c: (at + s, 0, p)),
                pl.BlockSpec((1, rows, LANES), lambda s, p, c: (at + s, 0, 0)),
            ],
            scratch_shapes=[pltpu.VMEM((rows, LANES), F32)],
        ),
        input_output_aliases={6: 0, 7: 1} if before else {},
        compiler_params=params(grid=2),
        cost_estimate=cost(16 * count * rows * total * width, 15e6, count * rows * total * width // HD),
        name="attend",
    )(scal, q, k, v, seg, qf, *(before or ()))


def middle_kernel(at, count, carried, pieces, scal, x, attn, grad, qf, vec, *rest):
    refs = rest[:pieces]
    outs = rest[pieces + (7 if carried else 0) :]
    out, hid, gpre, act2, branch, gmid, sums, msg = outs[:8]
    x_s, attn_s, grad_s, qf_s, wo, up, down = outs[8:15]
    out_s, hid_s, gpre_s, act2_s, branch_s, gmid_s, sums_s, msg_s = outs[15:23]
    in_sems, w_sems, sems = outs[23:]
    parts, share, width = wo.shape
    rows = count * x.shape[1]
    group = pl.ds(at, count)
    second = second_pieces(refs)
    loads_out = piece_copies(scal, second, 0, share, wo, w_sems.at[0])
    loads_up = piece_copies(scal, second, share, 4 * share, up, w_sems.at[1])
    loads_down = piece_copies(scal, second, 5 * share, 4 * share, down, w_sems.at[2])
    inputs = [
        pltpu.make_async_copy(ref.at[group], buf, in_sems.at[j])
        for j, (ref, buf) in enumerate(((attn, attn_s), (x, x_s), (grad, grad_s), (qf, qf_s)))
    ]
    start(inputs[:2])
    start(loads_out)
    start(loads_up)
    start(loads_down)
    start(inputs[2:])
    wait(inputs[:2])
    wait(loads_out)
    w_out = wo[...].reshape(width, width)
    attended = attn_s[...].reshape(rows, width)
    middle = x_s[...].reshape(rows, width).astype(F32) + nn(attended, w_out) + vec[4:5]
    unit, inverse = unit_of(middle)
    normed = (unit * vec[5:6] + vec[6:7]).astype(BF16)
    stores = []

    def store(j, value, buf, ref):
        buf[...] = value.reshape(buf.shape)
        stores.append(pltpu.make_async_copy(buf, ref, sems.at[j]))
        stores[-1].start()

    store(0, normed, act2_s, act2.at[group])
    wait(inputs[2:])
    g = grad_s[...].reshape(rows, width)
    g_full = g.astype(F32)
    result = middle + vec[7:8]
    grad_two = jnp.zeros((rows, width), F32)
    wait(loads_up)
    wait(loads_down)
    for c in range(4):
        w_up = up[:, c * share : (c + 1) * share, :].reshape(width, width)
        if parts >= 4:
            step = parts // 4
            w_down = down[c * step : (c + 1) * step].reshape(width, width)
        else:
            w_down = down[0, c * width : (c + 1) * width]
        pre = nn(normed, w_up) + vec[8 + c : 9 + c]
        whole = 0.5 * (1.0 + lax.erf(pre * 0.7071067811865476))
        slope = whole + pre * jnp.exp(-0.5 * pre * pre) * 0.3989422804014327
        hidden = (pre * whole).astype(BF16)
        store(8 + c, hidden, hid_s.at[:, c], hid.at[group, c])
        result = result + nn(hidden, w_down)
        grad_pre = (nt(g, w_down) * slope).astype(BF16)
        store(12 + c, grad_pre, gpre_s.at[:, c], gpre.at[group, c])
        grad_two = grad_two + nt(grad_pre, w_up)
        sums_s[4 + c : 5 + c] = column_sum(grad_pre.astype(F32))
    store(1, result.astype(BF16), out_s, out.at[group])
    sums_s[0:1] = column_sum(grad_two * unit)
    sums_s[1:2] = column_sum(grad_two)
    grad_middle = g_full + norm_back(grad_two * vec[5:6], unit, inverse)
    store(2, grad_middle, gmid_s, gmid.at[group])
    grad_branch = grad_middle.astype(BF16)
    store(3, grad_branch, branch_s, branch.at[group])
    sums_s[2:3] = column_sum(grad_branch.astype(F32))
    sums_s[3:4] = column_sum(g_full)
    stores.append(pltpu.make_async_copy(sums_s, sums.at[1 if carried else 0], sems.at[4]))
    stores[-1].start()
    grad_attn = nt(grad_branch, w_out).astype(BF16)
    product = grad_attn.astype(F32) * attended.astype(F32)
    high = product.astype(BF16)
    low = (product - high.astype(F32)).astype(BF16)
    head = lax.broadcasted_iota(jnp.int32, (width, LANES), 0) // HD
    lane = lax.broadcasted_iota(jnp.int32, (width, LANES), 1) - 16 - 4 * head
    pick = jnp.where((lane == 2) | (lane == 3), 1.0, 0.0).astype(BF16)
    delta = nn(high, pick) + nn(low, pick)
    top = delta.astype(BF16).astype(F32)
    column = lax.broadcasted_iota(jnp.int32, (1, LANES), 1)
    in_heads = (column >= 16) & (column < 16 + 4 * (width // HD))
    features = jnp.where(
        in_heads & (column % 4 == 2),
        -top,
        jnp.where(
            in_heads & (column % 4 == 3),
            top - delta,
            qf_s[...].reshape(rows, LANES).astype(F32),
        ),
    )
    msg_s[:, :, :width] = grad_attn.reshape(count, rows // count, width)
    msg_s[:, :, width:] = features.astype(BF16).reshape(count, rows // count, LANES)
    stores.append(pltpu.make_async_copy(msg_s, msg, sems.at[5]))
    stores[-1].start()
    wait(stores)


def middle_call(at, count, scal, x, attn, grad, qf, second, vec, before):
    seqs, rows, width = x.shape
    parts = 8 if len(second) > 1 else 1
    share = width // parts
    flat = jax.ShapeDtypeStruct((seqs, rows, width), BF16)
    chunked = jax.ShapeDtypeStruct((seqs, 4, rows, width), BF16)
    outs = (
        flat,
        chunked,
        chunked,
        flat,
        flat,
        jax.ShapeDtypeStruct((seqs, rows, width), F32),
        jax.ShapeDtypeStruct((2, 8, width), F32),
    )
    base = 6 + len(second)
    return pl.pallas_call(
        functools.partial(middle_kernel, at, count, before is not None, len(second)),
        out_shape=outs + (jax.ShapeDtypeStruct((count, rows, width + LANES), BF16),),
        in_specs=[pl.BlockSpec(memory_space=pltpu.SMEM)]
        + [ANY] * 4
        + [VMEM]
        + [ANY] * (len(second) + (7 if before else 0)),
        out_specs=[ANY] * 8,
        scratch_shapes=[
            pltpu.VMEM((count, rows, width), BF16),
            pltpu.VMEM((count, rows, width), BF16),
            pltpu.VMEM((count, rows, width), BF16),
            pltpu.VMEM((count, rows, LANES), BF16),
            pltpu.VMEM((parts, share, width), BF16),
            pltpu.VMEM((parts, 4 * share, width), BF16),
            pltpu.VMEM((parts, 4 * share, width), BF16),
            pltpu.VMEM((count, rows, width), BF16),
            pltpu.VMEM((count, 4, rows, width), BF16),
            pltpu.VMEM((count, 4, rows, width), BF16),
            pltpu.VMEM((count, rows, width), BF16),
            pltpu.VMEM((count, rows, width), BF16),
            pltpu.VMEM((count, rows, width), F32),
            pltpu.VMEM((8, width), F32),
            pltpu.VMEM((count, rows, width + LANES), BF16),
            pltpu.SemaphoreType.DMA((4,)),
            pltpu.SemaphoreType.DMA((3, 8)),
            pltpu.SemaphoreType.DMA((16,)),
        ],
        input_output_aliases={base + j: j for j in range(7)} if before else {},
        compiler_params=pltpu.CompilerParams(vmem_limit_bytes=60 * MIB),
        cost_estimate=cost(36 * count * rows * width * width, 12e6 + 8e6 * count, 8 * count * rows * width),
        name="middle",
    )(scal, x, attn, grad, qf, vec, *second, *(before or ()))


def spread_copies(scal, source, row, keep, send, sems):
    share = source.shape[0] // 8
    copies = []
    for rel in range(8):
        x, y = bits(rel)
        ref = send if rel & 1 else keep
        block = source.at[pl.ds(pl.multiple_of((scal[0, 3] ^ rel) * share, 16), share)]
        copies.append(
            pltpu.make_async_copy(block, ref.at[2 * x + y, pl.ds(row, share)], sems.at[rel])
        )
    return copies


def ffn_grads_kernel(parts, scal, hid, gpre, act2, attn, branch, grad, *rest):
    outs, (one, two, sems_one, sems_two) = rest[:2], rest[-4:]
    i = pl.program_id(0)
    slot = i % 2
    count, rows, width = grad.shape
    tokens = count * rows
    share = width // parts

    def flat(ref):
        return ref[...].reshape(tokens, width)

    def copies_one(step):
        source = one.at[step % 2]
        if parts == 1:
            return [pltpu.make_async_copy(source, outs[0].at[pl.ds(step * width, width)], sems_one.at[step % 2, 0])]
        row = pl.multiple_of(step * share, 16)
        return spread_copies(scal, source, row, *outs, sems_one.at[step % 2])

    def copies_two(step):
        c = step - 1
        source = two.at[step % 2]
        if parts == 1:
            target = outs[1].at[pl.ds(c * width, width)]
            return [pltpu.make_async_copy(source, target, sems_two.at[step % 2, 0])]
        core, size = scal[0, 3] & 1, 4 * share
        where = c ^ (scal[0, 3] >> 1)
        where = 2 * (where & 1) + (where >> 1)
        return [
            pltpu.make_async_copy(
                source.at[pl.ds(pl.multiple_of(half_at * size, 16), size)],
                ref.at[where, pl.ds(5 * share, size)],
                sems_two.at[step % 2, j],
            )
            for j, (half_at, ref) in enumerate(((core, outs[0]), (1 - core, outs[1])))
        ]

    @pl.when(i >= 2)
    def _():
        wait(copies_one(i - 2))

    @pl.when(i >= 3)
    def _():
        wait(copies_two(i - 2))

    @pl.when(i == 0)
    def _():
        one[slot] = tn(flat(attn), flat(branch)).astype(BF16)

    @pl.when(i > 0)
    def _():
        one[slot] = tn(flat(act2), flat(gpre)).astype(BF16)
        two[slot] = tn(flat(hid), flat(grad)).astype(BF16)
        start(copies_two(i))

    start(copies_one(i))

    @pl.when(i == 4)
    def _():
        for step in (3, 4):
            wait(copies_one(step))
            wait(copies_two(step))


def ffn_grads_call(scal, parts, hid, gpre, act2, attn, branch, grad):
    count, rows, width = grad.shape
    share = width // parts
    chunk = pl.BlockSpec((count, 1, rows, width), lambda i: (0, jnp.maximum(i - 1, 0), 0, 0))
    if parts == 8:
        outs = (jax.ShapeDtypeStruct((4, 9 * share, width), BF16),) * 2
    else:
        outs = (
            jax.ShapeDtypeStruct((5 * width, width), BF16),
            jax.ShapeDtypeStruct((4 * width, width), BF16),
        )
    return pl.pallas_call(
        functools.partial(ffn_grads_kernel, parts),
        out_shape=outs,
        grid=(5,),
        in_specs=[pl.BlockSpec(memory_space=pltpu.SMEM), chunk, chunk]
        + [whole_spec(a) for a in (act2, attn, branch, grad)],
        out_specs=[ANY, ANY],
        scratch_shapes=[
            pltpu.VMEM((2, width, width), BF16),
            pltpu.VMEM((2, width, width), BF16),
            pltpu.SemaphoreType.DMA((2, 8)),
            pltpu.SemaphoreType.DMA((2, 2)),
        ],
        compiler_params=params(),
        cost_estimate=cost(18 * count * rows * width * width, 25e6),
        name="ffn_grads",
    )(scal, hid, gpre, act2, attn, branch, grad)


def ones_at(rows, *wanted):
    return jnp.broadcast_to(jnp.where(lane_is(*wanted), 1.0, 0.0).astype(BF16), (rows, LANES))


def query_grads_kernel(at, scal, q, k, v, grad, qf, seg, *rest):
    dq_out = rest[-1]
    seq, pair = at + pl.program_id(0), pl.program_id(1)
    rows = q.shape[1]

    def body(size, keys):
        k_pair, v_pair, features = k[0, keys, :], v[0, keys, :], seg[0, keys, :]
        total = None
        for which in range(2):
            lane = 16 + 4 * (2 * pair + which)
            q_aug = jnp.concatenate([half(q[0], which), qf[0]], axis=1)
            k_aug = jnp.concatenate([k_pair, features + ones_at(size, lane, lane + 1)], axis=1)
            probs = jnp.exp(nt(q_aug, k_aug))
            g_aug = jnp.concatenate([half(grad[0], which), qf[0]], axis=1)
            v_aug = jnp.concatenate([v_pair, ones_at(size, lane + 2, lane + 3)], axis=1)
            grad_scores = (probs * nt(g_aug, v_aug)).astype(BF16)
            part = nn(grad_scores, half(k_pair, which))
            total = part if total is None else total + part
        dq_out[0] = (total * HD**-0.5).astype(BF16)

    by_chunks(scal, seq, rows, body)


def query_grads_call(at, scal, q, k, v, msg, seg, before):
    seqs, total, width = q.shape
    count, rows = msg.shape[:2]
    pairs = width // LANES
    every = pl.BlockSpec((1, total, LANES), lambda s, p, c: (at + s, 0, p))
    return pl.pallas_call(
        functools.partial(query_grads_kernel, at),
        out_shape=jax.ShapeDtypeStruct((seqs, rows, width), BF16),
        grid_spec=pltpu.PrefetchScalarGridSpec(
            num_scalar_prefetch=1,
            grid=(count, pairs),
            in_specs=[
                pl.BlockSpec((1, rows, LANES), lambda s, p, c: (at + s, 2, p)),
                every,
                every,
                pl.BlockSpec((1, rows, LANES), lambda s, p, c: (s, 0, p)),
                pl.BlockSpec((1, rows, LANES), lambda s, p, c: (s, 0, pairs)),
                pl.BlockSpec((1, total, LANES), lambda s, p, c: (at + s, 0, 0)),
            ]
            + ([] if before is None else [ANY]),
            out_specs=pl.BlockSpec((1, rows, LANES), lambda s, p, c: (at + s, 0, p)),
        ),
        input_output_aliases={} if before is None else {7: 0},
        compiler_params=params(grid=2),
        cost_estimate=cost(24 * count * rows * total * width, 5e6 * count, count * rows * total * width // HD),
        name="query_grads",
    )(scal, q, k, v, msg, msg, seg, *(() if before is None else (before,)))


def key_grads_kernel(at, scal, q, k, v, seg, g0, gl, gr, gll, grr, *rest):
    dk_out, dv_out, grads, sems = rest[-4:]
    local, pair = pl.program_id(0), pl.program_id(1)
    seq = at + local
    rows = k.shape[1]
    width = grads.shape[1] - LANES

    @pl.when(pair == 0)
    def _():
        for act in (lambda copy: copy.start(), lambda copy: copy.wait()):
            for slot, ref in enumerate((gll, gl, g0, gr, grr)):

                @pl.when(needed(scal, seq, slot, rows))
                def _():
                    target = grads.at[pl.ds(slot * rows, rows)]
                    act(pltpu.make_async_copy(ref.at[local], target, sems.at[slot]))

    def body(size, queries):
        q_pair = q[0, queries, :]
        g_pair = grads[queries, pl.ds(pl.multiple_of(pair * LANES, LANES), LANES)]
        features = grads[queries, width:]
        dk, dv = None, None
        for which in range(2):
            lane = 16 + 4 * (2 * pair + which)
            q_half, g_half = half(q_pair, which), half(g_pair, which)
            k_aug = jnp.concatenate([k[0], seg[0] + ones_at(rows, lane, lane + 1)], axis=1)
            v_aug = jnp.concatenate([v[0], ones_at(rows, lane + 2, lane + 3)], axis=1)
            probs = jnp.exp(nt(k_aug, jnp.concatenate([q_half, features], axis=1)))
            grad_probs = nt(v_aug, jnp.concatenate([g_half, features], axis=1))
            grad_scores = (probs * grad_probs).astype(BF16)
            dv_part, dk_part = nn(probs.astype(BF16), g_half), nn(grad_scores, q_half)
            dk = dk_part if dk is None else dk + dk_part
            dv = dv_part if dv is None else dv + dv_part
        dk_out[0] = dk.astype(BF16)
        dv_out[0] = dv.astype(BF16)

    by_chunks(scal, seq, rows, body)


def key_grads_call(at, scal, q, k, v, seg, msgs, before):
    seqs, total, width = q.shape
    count, rows = msgs[0].shape[:2]
    pairs = width // LANES
    own = pl.BlockSpec((1, rows, LANES), lambda s, p, c: (at + s, 2, p))
    out = pl.BlockSpec((1, rows, LANES), lambda s, p, c: (at + s, 0, p))
    return pl.pallas_call(
        functools.partial(key_grads_kernel, at),
        out_shape=(jax.ShapeDtypeStruct((seqs, rows, width), BF16),) * 2,
        grid_spec=pltpu.PrefetchScalarGridSpec(
            num_scalar_prefetch=1,
            grid=(count, pairs),
            in_specs=[
                pl.BlockSpec((1, total, LANES), lambda s, p, c: (at + s, 0, p)),
                own,
                own,
                pl.BlockSpec((1, rows, LANES), lambda s, p, c: (at + s, 2, 0)),
            ]
            + [ANY] * (5 + (2 if before else 0)),
            out_specs=[out, out],
            scratch_shapes=[
                pltpu.VMEM((total, width + LANES), BF16),
                pltpu.SemaphoreType.DMA((5,)),
            ],
        ),
        input_output_aliases={10: 0, 11: 1} if before else {},
        compiler_params=params(grid=2),
        cost_estimate=cost(32 * count * rows * total * width, 6e6 * count, count * rows * total * width // HD),
        name="key_grads",
    )(scal, q, k, v, seg, *msgs, *(before or ()))


def last_kernel(parts, pieces, scal, x, gmid, dq, dk, dv, vec, sums, *rest):
    refs, rest = rest[:pieces], rest[pieces:]
    gin, outs = rest[0], rest[1:-5]
    weights, work, total, wsems, sems = rest[-5:]
    count, rows, width = x.shape
    tokens = count * rows
    depth = weights.shape[1]
    share = width // parts
    copies = piece_copies(scal, first_pieces(refs), 0, depth, weights, wsems)
    start(copies)
    unit, inverse = unit_of(x[...].reshape(tokens, width).astype(F32))
    act = (unit * vec[0:1] + vec[1:2]).astype(BF16)
    given = [ref[...].reshape(tokens, width) for ref in (dq, dk, dv)]
    stores = []
    for j in range(3):
        work[j] = tn(act, given[j]).astype(BF16)
        if parts == 1:
            target = outs[0].at[pl.ds(j * width, width)]
            stores.append(pltpu.make_async_copy(work.at[j], target, sems.at[j, 0]))
            stores[-1].start()
        else:
            stores += spread_copies(scal, work.at[j], j * share, *outs, sems.at[j])
            start(stores[-8:])
    wait(copies)
    grad_one = jnp.zeros(unit.shape, F32)
    for j in range(3):
        weight = weights[:, j * share : (j + 1) * share, :].reshape(width, width)
        grad_one = grad_one + nt(given[j], weight)
    back = norm_back(grad_one * vec[0:1], unit, inverse)
    gin[...] = (gmid[...].reshape(tokens, width) + back).astype(BF16).reshape(gin.shape)
    total[0:8] = (sums[0] + sums[1]).astype(BF16)
    total[8:32] = jnp.zeros((24, width), BF16)
    rows_now = [
        column_sum(grad_one * unit),
        column_sum(grad_one),
        column_sum(given[0].astype(F32)),
        column_sum(given[2].astype(F32)),
    ]
    for j, row in enumerate(rows_now):
        total[8 + j : 9 + j] = row.astype(BF16)
    if parts == 1:
        stores.append(
            pltpu.make_async_copy(total, outs[0].at[pl.ds(3 * width, 32)], sems.at[3, 0])
        )
        stores[-1].start()
    else:
        for rel in range(8):
            x_bit, y_bit = bits(rel)
            target = outs[rel & 1].at[2 * x_bit + y_bit, pl.ds(3 * share, 32)]
            stores.append(pltpu.make_async_copy(total, target, sems.at[3, rel]))
            stores[-1].start()
    wait(stores)


def last_call(scal, x, gmid, dq, dk, dv, vec, sums, first):
    parts, depth = (8, first[0].shape[1]) if len(first) > 1 else first[0].shape[:2]
    width = x.shape[2]
    share = width // parts
    gin = jax.ShapeDtypeStruct(x.shape, BF16)
    if parts == 1:
        outs = (jax.ShapeDtypeStruct((3 * width + 32, width), BF16),)
    else:
        outs = (jax.ShapeDtypeStruct((4, 3 * share + 32, width), BF16),) * 2
    return pl.pallas_call(
        functools.partial(last_kernel, parts, len(first)),
        out_shape=(gin, *outs),
        grid=(1,),
        in_specs=[pl.BlockSpec(memory_space=pltpu.SMEM)]
        + [whole_spec(a) for a in (x, gmid, dq, dk, dv, vec, sums)]
        + [ANY] * len(first),
        out_specs=[whole_spec(gin)] + [ANY] * len(outs),
        scratch_shapes=[
            pltpu.VMEM((parts, depth, width), BF16),
            pltpu.VMEM((3, width, width), BF16),
            pltpu.VMEM((32, width), BF16),
            pltpu.SemaphoreType.DMA((8,)),
            pltpu.SemaphoreType.DMA((4, 8)),
        ],
        compiler_params=params(),
        cost_estimate=cost(12 * x.shape[0] * x.shape[1] * width * width, 20e6),
        name="last",
    )(scal, x, gmid, dq, dk, dv, vec, sums, *first)


def outer(ids):
    return (ids[0, 2] == 0) | (ids[0, 2] == 3)


def halves(ids, mine, got):
    swap = outer(ids)
    return jnp.where(swap, mine[...], got[...]).astype(F32), jnp.where(swap, got[...], mine[...]).astype(F32)


def finish_ffn_kernel(ids, mine, got, out_w, up_w, down_w, both):
    share, width = out_w.shape
    size = mine.shape[0]
    both[0:size], both[size:] = halves(ids, mine, got)
    out_w[...] = both[0:share]
    for c in range(4):
        up_w[:, c * width : (c + 1) * width] = both[(1 + c) * share : (2 + c) * share]
    down_w[...] = both[5 * share :]


def finish_ffn_call(ids, mine, got, share):
    width = mine.shape[1]
    outs = (
        jax.ShapeDtypeStruct((share, width), F32),
        jax.ShapeDtypeStruct((share, 4 * width), F32),
        jax.ShapeDtypeStruct((4 * share, width), F32),
    )
    return pl.pallas_call(
        finish_ffn_kernel,
        out_shape=outs,
        grid=(1,),
        in_specs=[pl.BlockSpec(memory_space=pltpu.SMEM), whole_spec(mine), whole_spec(got)],
        out_specs=[whole_spec(a) for a in outs],
        scratch_shapes=[pltpu.VMEM((2 * mine.shape[0], width), F32)],
        compiler_params=params(),
        cost_estimate=cost(0, 6e6),
        name="finish_ffn",
    )(ids, mine, got)


def finish_proj_kernel(ids, mine, got, q_w, k_w, v_w, *rest):
    *vectors, bias, both = rest
    share, width = q_w.shape
    size = mine.shape[0]
    both[0:size], both[size:] = halves(ids, mine, got)
    for j, out in enumerate((q_w, k_w, v_w)):
        out[...] = both[j * share : (j + 1) * share]
    me = ids[0, 3]
    row = lax.broadcasted_iota(jnp.int32, (width, LANES), 0)
    column = lax.broadcasted_iota(jnp.int32, (width, LANES), 1)
    pick = jnp.where(row == column + me * share, 1.0, 0.0).astype(BF16)
    picked = nn(both[3 * share : 3 * share + 16].astype(BF16), pick)
    for out, j in zip(vectors, (8, 9, 10, 11, 2, 0, 1, 3)):
        out[...] = picked[j : j + 1, 0:share]
    line = both[pl.ds(3 * share + 4 + me // 2, 1), :]
    bias[...] = jnp.where(me % 2 == 0, line[:, 0 : 4 * share], line[:, 4 * share :])


def finish_proj_call(ids, mine, got, share):
    width = mine.shape[1]
    outs = (
        [jax.ShapeDtypeStruct((share, width), F32)] * 3
        + [jax.ShapeDtypeStruct((1, share), F32)] * 8
        + [jax.ShapeDtypeStruct((1, 4 * share), F32)]
    )
    return pl.pallas_call(
        finish_proj_kernel,
        out_shape=outs,
        grid=(1,),
        in_specs=[pl.BlockSpec(memory_space=pltpu.SMEM), whole_spec(mine), whole_spec(got)],
        out_specs=[whole_spec(a) for a in outs],
        scratch_shapes=[pltpu.VMEM((2 * mine.shape[0], width), F32)],
        compiler_params=params(),
        cost_estimate=cost(0, 2e6),
        name="finish_proj",
    )(ids, mine, got)


RIGHT = [(0, 1), (1, 2), (2, 3)]
LEFT = [(1, 0), (2, 1), (3, 2)]
RIGHT_AGAIN = [(1, 2), (2, 3)]
LEFT_AGAIN = [(2, 1), (1, 0)]


def shifted(array, pairs):
    return lax.ppermute(array, "seq", pairs)


def crossed(array, distance):
    return lax.ppermute(array, "dp", [(i, i ^ distance) for i in range(8)])


def neighbours(array):
    left, right = shifted(array, RIGHT), shifted(array, LEFT)
    return left, right, shifted(left, RIGHT_AGAIN), shifted(right, LEFT_AGAIN)


def after(value, *others):
    return lax.optimization_barrier((value, *others))[0]


def add(*arrays):
    return sum(array.astype(F32) for array in arrays).astype(BF16)


PAIRS = [(0, 1), (1, 0), (2, 3), (3, 2)]
ACROSS = [(0, 3), (3, 0), (1, 2), (2, 1)]


class Reduction:
    def __init__(self, keep, send, place):
        self.keep, self.place, self.cut = keep, place, keep.shape[1] // 2
        self.got = crossed(send, 1)

    def second(self, *order):
        keep, got, cut = self.keep, after(self.got, *order), self.cut
        self.got = got
        one = add(keep[2:4, :cut], got[2:4, :cut])
        two = add(keep[1::2, cut:], got[1::2, cut:])
        self.more = crossed(one, 2), crossed(two, 4)
        return one, two

    def third(self, *order):
        keep, got, cut = self.keep, self.got, self.cut
        more = self.more = tuple(after(m, *order) for m in self.more)
        one = add(keep[1, :cut], got[1, :cut], more[0][1])
        two = add(keep[2, cut:], got[2, cut:], more[1][1])
        self.last = crossed(one, 4), crossed(two, 2)
        return one, two

    def fourth(self, *order):
        keep, got, cut = self.keep, self.got, self.cut
        last = tuple(after(m, *order) for m in self.last)
        one = add(keep[0, :cut], got[0, :cut], self.more[0][0], last[0])
        two = add(keep[0, cut:], got[0, cut:], self.more[1][0], last[1])
        return self.over_seq(one, two)

    def over_seq(self, one, two):
        outside = (self.place == 0) | (self.place == 3)
        self.mine = jnp.where(outside, one, two)
        other = jnp.where(outside, two, one)
        self.got = shifted(other, PAIRS)
        return self.mine, other

    def fifth(self, *order):
        self.mine = add(self.mine, after(self.got, *order))
        self.got = shifted(self.mine, ACROSS)
        return (self.mine,)

    def sixth(self, *order):
        self.mine = add(self.mine, after(self.got, *order))
        self.got = shifted(self.mine, PAIRS)
        return (self.mine,)

    def result(self):
        return self.mine, self.got


def windows(slots, place, me):
    seqs, _, rows = slots.shape
    whole = slots.reshape(seqs, 5 * rows)
    first, last = slots[:, 2, :1], slots[:, 2, -1:]
    low = jnp.sum((whole < first).astype(jnp.int32), axis=1)
    high = jnp.sum((whole <= last).astype(jnp.int32), axis=1)
    begin = (low // LANES) * LANES
    chunks = (high - begin + rows - 1) // rows
    begin = jnp.minimum(begin, rows * (jnp.minimum(5, 6 - place) - chunks))
    other = jnp.zeros_like(begin)
    return jnp.stack([begin, chunks, other + place, other + me], axis=1)


def per_device(
    inputs,
    segment_ids,
    norm1_gain,
    norm1_shift,
    query_weight,
    query_bias,
    key_weight,
    value_weight,
    value_bias,
    out_weight,
    out_bias,
    norm2_gain,
    norm2_shift,
    fc1_weight,
    fc1_bias,
    fc2_weight,
    fc2_bias,
    grad_output,
):
    seqs, rows, width = inputs.shape
    devices = lax.axis_size("dp")
    share = query_weight.shape[0]
    place, me = lax.axis_index("seq"), lax.axis_index("dp")
    direct = devices == 8
    parts = 8 if direct else 1
    zero = jnp.zeros((), jnp.int32)
    ids = jnp.stack([zero, zero, place, me])[None]

    vectors = (
        norm1_gain, norm1_shift, query_bias, value_bias,
        out_bias, norm2_gain, norm2_shift, fc2_bias, fc1_bias,
    )
    packed_one, packed_two, tokens = pack_call(
        (query_weight, key_weight, value_weight, out_weight, fc1_weight, fc2_weight),
        vectors,
        inputs,
        segment_ids,
    )
    left, right = shifted(tokens, RIGHT), shifted(tokens, LEFT)
    if direct:
        near = jnp.stack(
            [after(packed_one, left, right)] + [crossed(packed_one, d) for d in (2, 4, 6)]
        )
        first = near, crossed(near, 1)
        later = after(packed_two, near)
        x2, y2 = crossed(later, 2), crossed(later, 4)
        vec = unpack_call(*first, ids)
    else:
        one = lax.all_gather(packed_one, "dp", axis=0)
        two = lax.all_gather(packed_two, "dp", axis=0)
        small = one[:, 3 * share :]
        vec = jnp.concatenate(
            [
                small[:, :8, :share].transpose(1, 0, 2).reshape(8, width),
                small[:, 8, : 4 * share].reshape(4, width),
                jnp.zeros((4, width), BF16),
            ]
        ).astype(F32)
        first = (
            jnp.concatenate(
                [one[:, j * share : (j + 1) * share].reshape(width, width) for j in range(3)]
                + [jnp.zeros((16, width), BF16)]
            )[None],
        )
        second = (
            jnp.concatenate(
                [two[:, j * share : (j + 1) * share].reshape(width, width) for j in range(5)]
                + [two[:, 5 * share :].reshape(4 * width, width)]
            )[None],
        )
    far_left, far_right = shifted(left, RIGHT_AGAIN), shifted(right, LEFT_AGAIN)

    qkv = project_call(ids, (inputs, left, right), vec, first, None, seqs, rows)
    if direct:
        cut = 5 * share
        own = crossed(after(packed_two, left, right), 1)
        far_left, far_right, x2, y2, own, *qkv = lax.optimization_barrier(
            (far_left, far_right, x2, y2, own, *qkv)
        )
        low, high = crossed(y2[:cut], 2), crossed(x2[cut:], 4)
        x3, y3 = crossed(x2, 1), crossed(y2, 1)

    def ids_of(message):
        return message[:, rows, :rows].astype(jnp.int32)

    before, beyond = jnp.full_like(segment_ids, -1), jnp.full_like(segment_ids, 99)
    slots = jnp.stack(
        [
            jnp.where(place >= 2, ids_of(far_left), before),
            jnp.where(place >= 1, ids_of(left), before),
            segment_ids,
            jnp.where(place <= 2, ids_of(right), beyond),
            jnp.where(place <= 1, ids_of(far_right), beyond),
        ],
        axis=1,
    )
    scal = windows(slots, place, me)
    lane = lax.broadcasted_iota(jnp.int32, (1, 1, LANES), 2)
    seg = (slots.reshape(seqs, 5 * rows)[:, :, None] == lane).astype(BF16)
    qf = jnp.where((lane < 4) & (lane != segment_ids[:, :, None]), -BIG, 0.0).astype(BF16)
    qkv = project_call(scal, (far_left, far_right), vec, first, qkv, seqs, rows)

    attended = list(attend_call(0, 1, scal, *qkv, seg, qf, None))
    if direct:
        low, high = after(low, attended[0]), after(high, attended[0])
        low2, high2 = crossed(low, 1), crossed(high, 1)
        attended[0], low, high = lax.optimization_barrier((attended[0], low, high))
        second = (packed_two, x2, y2, low, high, own, x3, y3, low2, high2)
    attn, features = attend_call(1, seqs - 1, scal, *qkv, seg, qf, tuple(attended))

    split = ((0, 1), (1, seqs - 1))

    def middle(at, count, before):
        *shared, msg = middle_call(
            at, count, scal, inputs, attn, grad_output, features, second, vec, before
        )
        return shared, msg

    shared, msg_a = middle(*split[0], None)
    left_a, right_a = shifted(msg_a, RIGHT), shifted(msg_a, LEFT)
    shared, msg_b = middle(*split[1], shared)
    left_a, right_a, msg_b = lax.optimization_barrier((left_a, right_a, msg_b))
    far_left_a, far_right_a = shifted(left_a, RIGHT_AGAIN), shifted(right_a, LEFT_AGAIN)
    left_b, right_b = shifted(msg_b, RIGHT), shifted(msg_b, LEFT)
    out, hid, gpre, act2, branch, gmid, sums = shared
    ffn = ffn_grads_call(after(scal, left_a), parts, hid, gpre, act2, attn, branch, grad_output)
    ffn = list(ffn)
    ffn[1], far_left_a, far_right_a = lax.optimization_barrier((ffn[1], far_left_a, far_right_a))
    dq = query_grads_call(split[0][0], after(scal, ffn[1]), *qkv, msg_a, seg, None)
    left_b, right_b, dq = lax.optimization_barrier((left_b, right_b, dq))
    far_left_b, far_right_b = shifted(left_b, RIGHT_AGAIN), shifted(right_b, LEFT_AGAIN)
    all_a = msg_a, left_a, right_a, far_left_a, far_right_a
    all_b = msg_b, left_b, right_b, far_left_b, far_right_b
    if direct:
        reduction = Reduction(*ffn, place)
        order = reduction.second(dq)
        dq = query_grads_call(split[1][0], after(scal, *order), *qkv, msg_b, seg, dq)
        dkv = key_grads_call(split[0][0], after(scal, dq), *qkv, seg, all_a, None)
        order = reduction.third(dkv[0])
        dkv = key_grads_call(split[1][0], after(scal, *order), *qkv, seg, all_b, tuple(dkv))
        order = reduction.fourth(dkv[0])
        grad_inputs, *proj = last_call(
            after(scal, *order), inputs, gmid, dq, *dkv, vec, sums, first
        )
        order = reduction.fifth(grad_inputs)
        tail = Reduction(proj[0], after(proj[1], *order), place)
        order = tail.second()
        order = tail.third(*reduction.sixth(*order))
        tail.fourth()
        tail.fifth()
        tail.sixth()
        out_w, up_w, down_w = finish_ffn_call(ids, *reduction.result(), share)
        q_w, k_w, v_w, *small, up_b = finish_proj_call(ids, *tail.result(), share)
        small = [s.reshape(share) for s in small]
        return (
            out, grad_inputs, small[0], small[1], q_w, small[2], k_w, v_w, small[3], out_w,
            small[4], small[5], small[6], up_w, up_b.reshape(4 * share), down_w, small[7],
        )

    dq = query_grads_call(split[1][0], scal, *qkv, msg_b, seg, dq)
    dkv = key_grads_call(split[0][0], scal, *qkv, seg, all_a, None)
    dkv = key_grads_call(split[1][0], scal, *qkv, seg, all_b, tuple(dkv))
    grad_inputs, proj = last_call(scal, inputs, gmid, dq, *dkv, vec, sums, first)

    def reduced(array, count):
        cut = array.reshape(count, devices, -1, width).transpose(1, 0, 2, 3)
        cut = cut.reshape(devices, -1, width)
        part = lax.psum_scatter(cut, "dp", scatter_dimension=0, tiled=True)[0]
        return lax.psum(part, "seq").astype(F32)

    ffn_one, ffn_two = reduced(ffn[0], 5), reduced(ffn[1], 1)
    proj_w = reduced(proj[: 3 * width], 3)
    vectors = lax.psum(proj[3 * width : 3 * width + 16].astype(F32), ("dp", "seq"))
    mine = lax.dynamic_slice(vectors, (0, me * share), (16, share))
    up_grad = ffn_one[share:].reshape(4, share, width).transpose(1, 0, 2)
    up_bias = lax.dynamic_slice(vectors[4:8].reshape(4 * width), (me * 4 * share,), (4 * share,))
    return (
        out, grad_inputs, mine[8], mine[9], proj_w[:share], mine[10], proj_w[share : 2 * share],
        proj_w[2 * share :], mine[11], ffn_one[:share], mine[2], mine[0], mine[1],
        up_grad.reshape(share, 4 * width), up_bias, ffn_two, mine[3],
    )


def solution(mesh):
    token, matrix, vector = P("dp", "seq", None), P("dp", None), P("dp")
    return jax.shard_map(
        per_device,
        mesh=mesh,
        in_specs=(
            token, P("dp", "seq"), vector, vector, matrix, vector, matrix, matrix, vector,
            matrix, vector, vector, vector, matrix, vector, matrix, vector, token,
        ),
        out_specs=(
            token, token, vector, vector, matrix, vector, matrix, matrix, vector,
            matrix, vector, vector, vector, matrix, vector, matrix, vector,
        ),
        check_vma=False,
    )
```

```python
import functools

import jax
import jax.numpy as jnp
from jax import lax
from jax.experimental import pallas as pl
from jax.experimental.pallas import tpu as pltpu
from jax.sharding import PartitionSpec as P

F32 = jnp.float32
BF16 = jnp.bfloat16
HD = 64
LANES = 128
BIG = 1e30
EPSILON = 1e-05
MIB = 1 << 20

ANY = pl.BlockSpec(memory_space=pl.ANY)
VMEM = pl.BlockSpec(memory_space=pltpu.VMEM)


def nn(left, right):
    return lax.dot_general(left, right, (((1,), (0,)), ((), ())), preferred_element_type=F32)


def nt(left, right):
    return lax.dot_general(left, right, (((1,), (1,)), ((), ())), preferred_element_type=F32)


def tn(left, right):
    return lax.dot_general(left, right, (((0,), (0,)), ((), ())), preferred_element_type=F32)


def unit_of(values):
    center = values - jnp.mean(values, axis=-1, keepdims=True)
    inverse = lax.rsqrt(jnp.mean(center * center, axis=-1, keepdims=True) + EPSILON)
    return center * inverse, inverse


def norm_back(scaled, unit, inverse):
    return inverse * (
        scaled
        - jnp.mean(scaled, axis=-1, keepdims=True)
        - unit * jnp.mean(scaled * unit, axis=-1, keepdims=True)
    )


def column_sum(values):
    return jnp.sum(values, axis=0, keepdims=True)


def cost(flops, moved, transcendentals=0):
    return pl.CostEstimate(flops=int(flops / 4), bytes_accessed=int(moved / 4), transcendentals=0)


def params(limit=56, grid=1):
    return pltpu.CompilerParams(dimension_semantics=("arbitrary",) * grid, vmem_limit_bytes=limit * MIB)


def bits(rel):
    return (rel >> 1) & 1, (rel >> 2) & 1


def tokens_kernel(x, seg, tokens):
    count, rows, width = x.shape
    tokens[:, 0:rows] = x[...]
    tokens[:, rows:] = jnp.zeros((count, 16, width), BF16)
    for s in range(count):
        tokens[s, rows : rows + 1, 0:rows] = seg[s : s + 1].astype(F32).astype(BF16)


def tokens_call(x, seg):
    out = jax.ShapeDtypeStruct((x.shape[0], x.shape[1] + 16, x.shape[2]), BF16)
    return pl.pallas_call(
        tokens_kernel,
        out_shape=out,
        grid=(1,),
        in_specs=[whole_spec(x), whole_spec(seg)],
        out_specs=whole_spec(out),
        compiler_params=params(),
        cost_estimate=cost(0, 3e6),
        name="tokens",
    )(x, seg)


def pack_kernel(wq, wk, wv, wo, up, down, *rest):
    *vectors, first, second = rest
    share, width = wq.shape
    first[0:share] = wq[...]
    first[share : 2 * share] = wk[...]
    first[2 * share : 3 * share] = wv[...]
    first[3 * share :] = jnp.zeros((16, width), BF16)
    for j, vector in enumerate(vectors):
        size = vector.shape[1]
        first[3 * share + j : 3 * share + j + 1, 0:size] = vector[...]
    second[0:share] = wo[...]
    for c in range(4):
        second[(1 + c) * share : (2 + c) * share] = up[:, c * width : (c + 1) * width]
    second[5 * share :] = down[...]


def whole_spec(array):
    zeros = (0,) * len(array.shape)
    return pl.BlockSpec(array.shape, lambda i: zeros)


def pack_call(matrices, vectors):
    share, width = matrices[0].shape
    args = (*matrices, *[v.reshape(1, -1) for v in vectors])
    outs = (
        jax.ShapeDtypeStruct((3 * share + 16, width), BF16),
        jax.ShapeDtypeStruct((9 * share, width), BF16),
    )
    return pl.pallas_call(
        pack_kernel,
        out_shape=outs,
        grid=(1,),
        in_specs=[whole_spec(a) for a in args],
        out_specs=[whole_spec(a) for a in outs],
        compiler_params=params(),
        cost_estimate=cost(0, 6e6),
        name="pack",
    )(*args)


def piece_copies(scal, pieces, low, size, target, sems):
    if len(pieces) == 1:
        return [pltpu.make_async_copy(pieces[0][0].at[:, pl.ds(low, size)], target, sems.at[0])]
    me, copies = scal[0, 3], []
    for ref, index, rel, start, stop in pieces:
        if start <= low and low + size <= stop:
            source = ref if index is None else ref.at[index]
            copies.append(
                pltpu.make_async_copy(
                    source.at[pl.ds(low - start, size)], target.at[me ^ rel], sems.at[rel]
                )
            )
    return copies


def first_pieces(refs):
    if len(refs) == 1:
        return [(refs[0],)]
    near, far = refs
    return [(near, j, 2 * j, 0, near.shape[1]) for j in range(4)] + [
        (far, j, 2 * j + 1, 0, far.shape[1]) for j in range(4)
    ]


def second_pieces(refs):
    if len(refs) == 1:
        return [(refs[0],)]
    full = refs[0].shape[0]
    split = refs[3].shape[0]
    pieces = []
    for core in range(2):
        own, x, y, xy_low, xy_high = refs[5 * core : 5 * core + 5]
        pieces += [(own, None, core, 0, full), (x, None, 2 + core, 0, full), (y, None, 4 + core, 0, full)]
        pieces += [(xy_low, None, 6 + core, 0, split), (xy_high, None, 6 + core, split, full)]
    return pieces


def start(copies):
    for copy in copies:
        copy.start()


def wait(copies):
    for copy in copies:
        copy.wait()


def unpack_kernel(near, far, scal, vec):
    me = scal[0, 3]
    share = 96
    width = vec.shape[1]
    total = jnp.zeros((16, width), F32)
    row = lax.broadcasted_iota(jnp.int32, (LANES, width), 0)
    column = lax.broadcasted_iota(jnp.int32, (LANES, width), 1)
    for rel in range(8):
        device = me ^ rel
        block = (near if rel % 2 == 0 else far)[rel // 2]
        pick = jnp.where((row < share) & (column == row + device * share), 1.0, 0.0).astype(BF16)
        total = total + nn(block[:, 0:LANES], pick)
        bias = block[8:9, 0 : 4 * share].astype(F32)
        vec[pl.ds(8 + device // 2, 1), pl.ds(pl.multiple_of((device % 2) * 4 * share, LANES), 4 * share)] = bias
    vec[0:8] = total[0:8]
    vec[12:16] = jnp.zeros((4, width), F32)


def unpack_call(near, far, ids):
    width = near.shape[2]
    out = jax.ShapeDtypeStruct((16, width), F32)
    tail = pl.BlockSpec((4, 16, width), lambda i: (0, near.shape[1] // 16 - 1, 0))
    return pl.pallas_call(
        unpack_kernel,
        out_shape=out,
        grid=(1,),
        in_specs=[tail, tail, pl.BlockSpec(memory_space=pltpu.SMEM)],
        out_specs=whole_spec(out),
        compiler_params=params(),
        cost_estimate=cost(1e6, 4e6),
        name="unpack",
    )(near, far, ids)


def needed(scal, seq, slot, rows):
    low, high = scal[seq, 0], scal[seq, 0] + scal[seq, 1] * rows
    return (slot * rows < high) & ((slot + 1) * rows > low)


def project_kernel(far, pieces, scal, vec, *rest):
    sources = rest[: 2 if far else 3]
    rest = rest[len(sources) :]
    refs, (*outs, buf, weights, made, sems, wsems, out_sems) = rest[:pieces], rest[-9:]
    i = pl.program_id(0)
    steps = 1 if far else 3
    count, rows, width = buf.shape[1:]
    share = width // weights.shape[0]
    after = scal[0, 2] >= 2
    copies = piece_copies(scal, first_pieces(refs), 0, weights.shape[1], weights, wsems)
    if far:
        slot = jnp.where(after, 0, 4)
        used = needed(scal, 0, slot, rows)
        for s in range(1, count):
            used = used | needed(scal, s, slot, rows)
    else:
        slot = jnp.where(i == 0, 2, jnp.where(i == 1, 1, 3))
        used = True

    def load(step, act):
        for j, ref in enumerate(sources):
            when = (after == (j == 0)) if far else (step == j)

            @pl.when(when)
            def _():
                source = ref.at[:, pl.ds(0, rows)]
                act(pltpu.make_async_copy(source, buf.at[step % 2], sems.at[step % 2]))

    def stores(step, where):
        return [
            pltpu.make_async_copy(
                made.at[step % 2, t], outs[t].at[:, pl.ds(where * rows, rows)], out_sems.at[step % 2, t]
            )
            for t in range(3)
        ]

    @pl.when(i == 0)
    def _():
        load(0, lambda copy: copy.start())
        start(copies)

    @pl.when(i + 1 < steps)
    def _():
        load(i + 1, lambda copy: copy.start())

    load(i, lambda copy: copy.wait())

    @pl.when(i == 0)
    def _():
        wait(copies)

    @pl.when(i >= 2)
    def _():
        wait(stores(i, 0))

    def work():
        unit, _ = unit_of(buf[i % 2].reshape(count * rows, width).astype(F32))
        act = (unit * vec[0:1] + vec[1:2]).astype(BF16)
        for t in range(3):
            weight = weights[:, t * share : (t + 1) * share, :].reshape(width, width)
            result = nn(act, weight)
            if t == 0:
                result = (result + vec[2:3]).astype(BF16) * jnp.asarray(HD**-0.5, BF16)
            if t == 2:
                result = result + vec[3:4]
            made[i % 2, t] = result.astype(BF16).reshape(count, rows, width)
        start(stores(i, slot))

    if far:

        @pl.when(used)
        def _():
            work()
            wait(stores(0, 0))
    else:
        work()

        @pl.when(i == steps - 1)
        def _():
            wait(stores(i, 0))
            wait(stores(i - 1, 0))


def project_call(scal, sources, vec, first, before, seqs, rows):
    far = before is not None
    width = vec.shape[1]
    out = jax.ShapeDtypeStruct((seqs, 5 * rows, width), BF16)
    parts, depth = (8, first[0].shape[1]) if len(first) > 1 else first[0].shape[:2]
    steps = 1 if far else 3
    at = 2 + len(sources) + len(first)
    return pl.pallas_call(
        functools.partial(project_kernel, far, len(first)),
        out_shape=(out, out, out),
        grid=(steps,),
        in_specs=[pl.BlockSpec(memory_space=pltpu.SMEM), whole_spec(vec)]
        + [ANY] * (len(sources) + len(first) + (3 if far else 0)),
        out_specs=[ANY] * 3,
        scratch_shapes=[
            pltpu.VMEM((2, seqs, rows, width), BF16),
            pltpu.VMEM((parts, depth, width), BF16),
            pltpu.VMEM((2, 3, seqs, rows, width), BF16),
            pltpu.SemaphoreType.DMA((2,)),
            pltpu.SemaphoreType.DMA((8,)),
            pltpu.SemaphoreType.DMA((2, 3)),
        ],
        input_output_aliases={at: 0, at + 1: 1, at + 2: 2} if far else {},
        compiler_params=params(),
        cost_estimate=cost(6 * steps * seqs * rows * width * width, 8e6 * steps),
        name="far" if far else "near",
    )(scal, vec, *sources, *first, *(before or ()))


def lane_is(*wanted):
    lane = lax.broadcasted_iota(jnp.int32, (1, LANES), 1)
    hit = lane == wanted[0]
    for other in wanted[1:]:
        hit = hit | (lane == other)
    return hit


def head_mask(which):
    lane = lax.broadcasted_iota(jnp.int32, (1, LANES), 1)
    return (lane < HD) if which == 0 else (lane >= HD)


def half(pair, which):
    return jnp.where(head_mask(which), pair, jnp.zeros_like(pair))


def ones_at(rows, *wanted):
    return jnp.broadcast_to(jnp.where(lane_is(*wanted), 1.0, 0.0).astype(BF16), (rows, LANES))


def lanes(pair):
    return pl.ds(pl.multiple_of(pair * LANES, LANES), LANES)


def windowed(at, count, scal, arrays, rows):
    i = pl.program_id(0)

    def each(step, act):
        for c in range(4):

            @pl.when(c < scal[at + step, 1])
            def _():
                begin = pl.multiple_of(scal[at + step, 0] + c * rows, LANES)
                for ref, buf, sems in arrays:
                    source = ref.at[at + step, pl.ds(begin, rows)]
                    target = buf.at[step % 2, pl.ds(c * rows, rows)]
                    act(pltpu.make_async_copy(source, target, sems.at[step % 2, c]))

    @pl.when(i == 0)
    def _():
        each(i, lambda copy: copy.start())

    @pl.when(i + 1 < count)
    def _():
        each(i + 1, lambda copy: copy.start())

    each(i, lambda copy: copy.wait())


def by_chunks(chunks, pairs, body):
    for c in range(2, 5):

        @pl.when(chunks == c)
        def _():
            lax.fori_loop(0, pairs, lambda p, _: body(c, p), None, unroll=2)


def window_scratch(rows, widths):
    return [pltpu.VMEM((2, 4 * rows, w), BF16) for w in widths] + [
        pltpu.SemaphoreType.DMA((2, 4)) for _ in widths
    ]


def attend_kernel(at, count, scal, q, qf, k, v, seg, *rest):
    o_out, qf_out, kbuf, vbuf, sbuf, ksem, vsem, ssem, feats = rest[-9:]
    i = pl.program_id(0)
    slot = i % 2
    rows, width = q.shape[1:]
    windowed(at, count, scal, ((k, kbuf, ksem), (v, vbuf, vsem), (seg, sbuf, ssem)), rows)
    feats[...] = qf[0].astype(F32)

    def body(chunks, pair):
        size = chunks * rows
        q_pair, features = q[0, :, lanes(pair)], qf[0]
        q_aug = jnp.concatenate(
            [
                jnp.concatenate([half(q_pair, 0), half(q_pair, 1)], axis=0),
                jnp.concatenate([features, features], axis=0),
            ],
            axis=1,
        )
        k_aug = jnp.concatenate([kbuf[slot, :size, lanes(pair)], sbuf[slot, :size, :]], axis=1)
        v_aug = jnp.concatenate(
            [vbuf[slot, :size, lanes(pair)], jnp.ones((size, LANES), BF16)], axis=1
        )
        scores = nt(q_aug, k_aug)
        highest = jnp.max(scores, axis=-1, keepdims=True)
        both = nn(jnp.exp(scores - highest).astype(BF16), v_aug)
        totals = both[:, LANES:]
        result = both[:, :LANES] / totals
        o_out[0, :, lanes(pair)] = jnp.where(head_mask(0), result[:rows], result[rows:]).astype(BF16)
        lse = highest + jnp.log(totals)
        top = lse.astype(BF16).astype(F32)
        rest_of = top - lse
        lane = 16 + 8 * pair
        new = jnp.where(lane_is(lane), -top[:rows], feats[...])
        new = jnp.where(lane_is(lane + 1), rest_of[:rows], new)
        new = jnp.where(lane_is(lane + 4), -top[rows:], new)
        feats[...] = jnp.where(lane_is(lane + 5), rest_of[rows:], new)

    by_chunks(scal[at + i, 1], width // LANES, body)
    qf_out[0] = feats[...].astype(BF16)


def attend_call(at, count, scal, q, k, v, seg, qf, before):
    seqs, total, width = q.shape
    rows = qf.shape[1]
    flat = pl.BlockSpec((1, rows, width), lambda s, c: (at + s, 0, 0))
    narrow = pl.BlockSpec((1, rows, LANES), lambda s, c: (at + s, 0, 0))
    return pl.pallas_call(
        functools.partial(attend_kernel, at, count),
        out_shape=(
            jax.ShapeDtypeStruct((seqs, rows, width), BF16),
            jax.ShapeDtypeStruct((seqs, rows, LANES), BF16),
        ),
        grid_spec=pltpu.PrefetchScalarGridSpec(
            num_scalar_prefetch=1,
            grid=(count,),
            in_specs=[pl.BlockSpec((1, rows, width), lambda s, c: (at + s, 2, 0)), narrow]
            + [ANY] * (5 if before else 3),
            out_specs=[flat, narrow],
            scratch_shapes=window_scratch(rows, (width, width, LANES))
            + [pltpu.VMEM((rows, LANES), F32)],
        ),
        input_output_aliases={6: 0, 7: 1} if before else {},
        compiler_params=params(),
        cost_estimate=cost(16 * count * rows * total * width, 15e6),
        name="attend",
    )(scal, q, qf, k, v, seg, *(before or ()))


def query_grads_kernel(at, count, scal, q, grad, k, v, seg, *rest):
    dq_out, kbuf, vbuf, sbuf, ksem, vsem, ssem = rest[-7:]
    i = pl.program_id(0)
    slot = i % 2
    rows, width = q.shape[1:]
    windowed(at, count, scal, ((k, kbuf, ksem), (v, vbuf, vsem), (seg, sbuf, ssem)), rows)

    def body(chunks, pair):
        size = chunks * rows
        q_pair, g_pair, features = q[0, :, lanes(pair)], grad[0, :, lanes(pair)], grad[0, :, width:]
        k_pair, v_pair = kbuf[slot, :size, lanes(pair)], vbuf[slot, :size, lanes(pair)]
        lane = 16 + 8 * pair
        for_scores, for_probs = [], []
        for which in range(2):
            own = lane + 4 * which
            kept = (lane_is(own, own + 1)) | (lane_is(0, 1, 2, 3))
            masked = jnp.where(kept, features, jnp.zeros_like(features))
            for_scores.append(jnp.concatenate([half(q_pair, which), masked], axis=1))
            masked = jnp.where(lane_is(own + 2, own + 3), features, jnp.zeros_like(features))
            for_probs.append(jnp.concatenate([half(g_pair, which), masked], axis=1))
        q_aug, g_aug = jnp.concatenate(for_scores, axis=0), jnp.concatenate(for_probs, axis=0)
        probs = jnp.exp(nt(q_aug, jnp.concatenate([k_pair, sbuf[slot, :size, :]], axis=1)))
        ones = jnp.ones((size, LANES), BF16)
        grad_probs = nt(g_aug, jnp.concatenate([v_pair, ones], axis=1))
        total = nn((probs * grad_probs).astype(BF16), k_pair)
        total = jnp.where(head_mask(0), total[:rows], total[rows:])
        dq_out[0, :, lanes(pair)] = (total * HD**-0.5).astype(BF16)

    by_chunks(scal[at + i, 1], width // LANES, body)


def query_grads_call(at, count, scal, q, k, v, msg, seg, before, skip=0):
    seqs, total, width = q.shape
    rows = msg.shape[1]
    return pl.pallas_call(
        functools.partial(query_grads_kernel, at, count),
        out_shape=jax.ShapeDtypeStruct((seqs, rows, width), BF16),
        grid_spec=pltpu.PrefetchScalarGridSpec(
            num_scalar_prefetch=1,
            grid=(count,),
            in_specs=[
                pl.BlockSpec((1, rows, width), lambda s, c: (at + s, 2, 0)),
                pl.BlockSpec((1, rows, width + LANES), lambda s, c: (skip + s, 0, 0)),
            ]
            + [ANY] * (3 if before is None else 4),
            out_specs=pl.BlockSpec((1, rows, width), lambda s, c: (at + s, 0, 0)),
            scratch_shapes=window_scratch(rows, (width, width, LANES)),
        ),
        input_output_aliases={} if before is None else {6: 0},
        compiler_params=params(),
        cost_estimate=cost(24 * count * rows * total * width, 5e6 * count),
        name="query_grads",
    )(scal, q, msg, k, v, seg, *(() if before is None else (before,)))


def key_grads_kernel(at, skip, count, scal, k, v, seg, q, g0, gl, gr, gll, grr, *rest):
    dk_out, dv_out, qbuf, qsem, grads, sems = rest[-6:]
    i = pl.program_id(0)
    slot = i % 2
    rows, width = k.shape[1:]

    def each(step, act):
        for place, ref in enumerate((gll, gl, g0, gr, grr)):

            @pl.when(needed(scal, at + step, place, rows))
            def _():
                target = grads.at[step % 2, pl.ds(place * rows, rows)]
                act(pltpu.make_async_copy(ref.at[step + skip], target, sems.at[step % 2, place]))

    @pl.when(i == 0)
    def _():
        each(i, lambda copy: copy.start())

    @pl.when(i + 1 < count)
    def _():
        each(i + 1, lambda copy: copy.start())

    windowed(at, count, scal, ((q, qbuf, qsem),), rows)
    each(i, lambda copy: copy.wait())
    begin = pl.multiple_of(scal[at + i, 0], LANES)

    def body(chunks, pair):
        size = chunks * rows
        queries = pl.ds(begin, size)
        q_pair = qbuf[slot, :size, lanes(pair)]
        g_pair = grads[slot, queries, lanes(pair)]
        features = grads[slot, queries, width:]
        k_pair, v_pair = k[0, :, lanes(pair)], v[0, :, lanes(pair)]
        lane = 16 + 8 * pair
        for_scores, for_probs = [], []
        for which in range(2):
            own = lane + 4 * which
            kept = (lane_is(own, own + 1)) | (lane_is(0, 1, 2, 3))
            masked = jnp.where(kept, seg[0], jnp.zeros_like(seg[0]))
            for_scores.append(jnp.concatenate([half(k_pair, which), masked], axis=1))
            for_probs.append(
                jnp.concatenate([half(v_pair, which), ones_at(rows, own + 2, own + 3)], axis=1)
            )
        k_aug, v_aug = jnp.concatenate(for_scores, axis=0), jnp.concatenate(for_probs, axis=0)
        probs = jnp.exp(nt(k_aug, jnp.concatenate([q_pair, features], axis=1)))
        grad_probs = nt(v_aug, jnp.concatenate([g_pair, features], axis=1))
        grad_scores = (probs * grad_probs).astype(BF16)
        dv, dk = nn(probs.astype(BF16), g_pair), nn(grad_scores, q_pair)
        dk_out[0, :, lanes(pair)] = jnp.where(head_mask(0), dk[:rows], dk[rows:]).astype(BF16)
        dv_out[0, :, lanes(pair)] = jnp.where(head_mask(0), dv[:rows], dv[rows:]).astype(BF16)

    by_chunks(scal[at + i, 1], width // LANES, body)


def key_grads_call(at, count, scal, q, k, v, seg, msgs, before, skip=0):
    seqs, total, width = q.shape
    rows = msgs[0].shape[1]
    own = pl.BlockSpec((1, rows, width), lambda s, c: (at + s, 2, 0))
    out = pl.BlockSpec((1, rows, width), lambda s, c: (at + s, 0, 0))
    return pl.pallas_call(
        functools.partial(key_grads_kernel, at, skip, count),
        out_shape=(jax.ShapeDtypeStruct((seqs, rows, width), BF16),) * 2,
        grid_spec=pltpu.PrefetchScalarGridSpec(
            num_scalar_prefetch=1,
            grid=(count,),
            in_specs=[own, own, pl.BlockSpec((1, rows, LANES), lambda s, c: (at + s, 2, 0))]
            + [ANY] * (6 + (2 if before else 0)),
            out_specs=[out, out],
            scratch_shapes=window_scratch(rows, (width,))
            + [
                pltpu.VMEM((2, total, width + LANES), BF16),
                pltpu.SemaphoreType.DMA((2, 5)),
            ],
        ),
        input_output_aliases={10: 0, 11: 1} if before else {},
        compiler_params=params(),
        cost_estimate=cost(32 * count * rows * total * width, 6e6 * count),
        name="key_grads",
    )(scal, k, v, seg, q, *msgs, *(before or ()))


def middle_kernel(at, count, carried, pieces, scal, x, attn, grad, qf, vec, *rest):
    refs = rest[:pieces]
    outs = rest[pieces + (7 if carried else 0) :]
    out, hid, gpre, act2, branch, gmid, sums, msg = outs[:8]
    x_s, attn_s, grad_s, qf_s, wo, up_first, up_rest, down = outs[8:16]
    out_s, act2_s, branch_s, gmid_s, sums_s, msg_s = outs[16:22]
    hid_s, gpre_s = outs[22:26], outs[26:30]
    in_sems, w_sems, sems = outs[30:]
    parts, share, width = wo.shape
    rows = count * x.shape[1]
    group = pl.ds(at, count)
    second = second_pieces(refs)
    loads_out = piece_copies(scal, second, 0, share, wo, w_sems.at[0])
    loads_up = piece_copies(scal, second, share, share, up_first, w_sems.at[1])
    loads_rest = piece_copies(scal, second, 2 * share, 3 * share, up_rest, w_sems.at[3])
    loads_down = piece_copies(scal, second, 5 * share, 4 * share, down, w_sems.at[2])
    inputs = [
        pltpu.make_async_copy(ref.at[group], buf, in_sems.at[j])
        for j, (ref, buf) in enumerate(((attn, attn_s), (x, x_s), (grad, grad_s), (qf, qf_s)))
    ]
    start(inputs[:2])
    start(loads_out)
    start(inputs[2:])
    start(loads_up)
    start(loads_down)
    start(loads_rest)
    wait(inputs[:2])
    wait(loads_out)
    w_out = wo[...].reshape(width, width)
    attended = attn_s[...].reshape(rows, width)
    middle = x_s[...].reshape(rows, width).astype(F32) + nn(attended, w_out) + vec[4:5]
    unit, inverse = unit_of(middle)
    normed = (unit * vec[5:6] + vec[6:7]).astype(BF16)
    stores = []

    def store(j, value, buf, ref):
        buf[...] = value.reshape(buf.shape)
        stores.append(pltpu.make_async_copy(buf, ref, sems.at[j]))
        stores[-1].start()

    store(0, normed, act2_s, act2.at[group])
    wait(inputs[2:])
    g = grad_s[...].reshape(rows, width)
    g_full = g.astype(F32)
    result = middle + vec[7:8]
    grad_two = jnp.zeros((rows, width), F32)
    wait(loads_up)
    for c in range(4):
        w_up = up_first[...] if c == 0 else up_rest[:, (c - 1) * share : c * share, :]
        w_up = w_up.reshape(width, width)
        pre = nn(normed, w_up) + vec[8 + c : 9 + c]
        if c == 0:
            wait(loads_down)
            wait(loads_rest)
        if parts >= 4:
            step = parts // 4
            w_down = down[c * step : (c + 1) * step].reshape(width, width)
        else:
            w_down = down[0, c * width : (c + 1) * width]
        whole = 0.5 * (1.0 + lax.erf(pre * 0.7071067811865476))
        slope = whole + pre * jnp.exp(-0.5 * pre * pre) * 0.3989422804014327
        hidden = (pre * whole).astype(BF16)
        store(8 + c, hidden, hid_s[c], hid.at[group, c])
        result = result + nn(hidden, w_down)
        grad_pre = (nt(g, w_down) * slope).astype(BF16)
        store(12 + c, grad_pre, gpre_s[c], gpre.at[group, c])
        grad_two = grad_two + nt(grad_pre, w_up)
        sums_s[4 + c : 5 + c] = column_sum(grad_pre.astype(F32))
    store(1, result.astype(BF16), out_s, out.at[group])
    sums_s[0:1] = column_sum(grad_two * unit)
    sums_s[1:2] = column_sum(grad_two)
    grad_middle = g_full + norm_back(grad_two * vec[5:6], unit, inverse)
    store(2, grad_middle, gmid_s, gmid.at[group])
    grad_branch = grad_middle.astype(BF16)
    store(3, grad_branch, branch_s, branch.at[group])
    sums_s[2:3] = column_sum(grad_branch.astype(F32))
    sums_s[3:4] = column_sum(g_full)
    stores.append(pltpu.make_async_copy(sums_s, sums.at[1 if carried else 0], sems.at[4]))
    stores[-1].start()
    grad_attn = nt(grad_branch, w_out).astype(BF16)
    product = grad_attn.astype(F32) * attended.astype(F32)
    high = product.astype(BF16)
    low = (product - high.astype(F32)).astype(BF16)
    head = lax.broadcasted_iota(jnp.int32, (width, LANES), 0) // HD
    lane = lax.broadcasted_iota(jnp.int32, (width, LANES), 1) - 16 - 4 * head
    pick = jnp.where((lane == 2) | (lane == 3), 1.0, 0.0).astype(BF16)
    delta = nn(high, pick) + nn(low, pick)
    top = delta.astype(BF16).astype(F32)
    column = lax.broadcasted_iota(jnp.int32, (1, LANES), 1)
    in_heads = (column >= 16) & (column < 16 + 4 * (width // HD))
    features = jnp.where(
        in_heads & (column % 4 == 2),
        -top,
        jnp.where(
            in_heads & (column % 4 == 3),
            top - delta,
            qf_s[...].reshape(rows, LANES).astype(F32),
        ),
    )
    msg_s[:, :, :width] = grad_attn.reshape(count, rows // count, width)
    msg_s[:, :, width:] = features.astype(BF16).reshape(count, rows // count, LANES)
    stores.append(pltpu.make_async_copy(msg_s, msg, sems.at[5]))
    stores[-1].start()
    wait(stores)


def middle_call(at, count, scal, x, attn, grad, qf, second, vec, before):
    seqs, rows, width = x.shape
    parts = second[0].shape[0]
    share = width // parts
    flat = jax.ShapeDtypeStruct((seqs, rows, width), BF16)
    chunked = jax.ShapeDtypeStruct((seqs, 4, rows, width), BF16)
    outs = (
        flat,
        chunked,
        chunked,
        flat,
        flat,
        jax.ShapeDtypeStruct((seqs, rows, width), F32),
        jax.ShapeDtypeStruct((2, 8, width), F32),
    )
    base = 6 + len(second)
    return pl.pallas_call(
        functools.partial(middle_kernel, at, count, before is not None, len(second)),
        out_shape=outs + (jax.ShapeDtypeStruct((count, rows, width + LANES), BF16),),
        in_specs=[pl.BlockSpec(memory_space=pltpu.SMEM)]
        + [ANY] * 4
        + [VMEM]
        + [ANY] * (len(second) + (7 if before else 0)),
        out_specs=[ANY] * 8,
        scratch_shapes=[
            pltpu.VMEM((count, rows, width), BF16),
            pltpu.VMEM((count, rows, width), BF16),
            pltpu.VMEM((count, rows, width), BF16),
            pltpu.VMEM((count, rows, LANES), BF16),
            pltpu.VMEM((parts, share, width), BF16),
            pltpu.VMEM((parts, share, width), BF16),
            pltpu.VMEM((parts, 3 * share, width), BF16),
            pltpu.VMEM((parts, 4 * share, width), BF16),
            pltpu.VMEM((count, rows, width), BF16),
            pltpu.VMEM((count, rows, width), BF16),
            pltpu.VMEM((count, rows, width), BF16),
            pltpu.VMEM((count, rows, width), F32),
            pltpu.VMEM((8, width), F32),
            pltpu.VMEM((count, rows, width + LANES), BF16),
        ]
        + [pltpu.VMEM((count, rows, width), BF16)] * 8
        + [
            pltpu.SemaphoreType.DMA((4,)),
            pltpu.SemaphoreType.DMA((4, 8)),
            pltpu.SemaphoreType.DMA((16,)),
        ],
        input_output_aliases={base + j: j for j in range(7)} if before else {},
        compiler_params=pltpu.CompilerParams(vmem_limit_bytes=60 * MIB),
        cost_estimate=cost(36 * count * rows * width * width, 12e6 + 8e6 * count, 8 * count * rows * width),
        name="middle",
    )(scal, x, attn, grad, qf, vec, *second, *(before or ()))


def spread_copies(scal, source, row, keep, send, sems):
    share = source.shape[0] // 8
    copies = []
    for rel in range(8):
        x, y = bits(rel)
        ref = send if rel & 1 else keep
        block = source.at[pl.ds(pl.multiple_of((scal[0, 3] ^ rel) * share, 16), share)]
        copies.append(
            pltpu.make_async_copy(block, ref.at[2 * x + y, pl.ds(row, share)], sems.at[rel])
        )
    return copies


def ffn_grads_kernel(parts, scal, hid, gpre, act2, attn, branch, grad, *rest):
    outs, (one, two, sems_one, sems_two) = rest[:2], rest[-4:]
    i = pl.program_id(0)
    slot = i % 2
    count, rows, width = grad.shape
    tokens = count * rows
    share = width // parts

    def flat(ref):
        return ref[...].reshape(tokens, width)

    def copies_one(step):
        source = one.at[step % 2]
        if parts == 1:
            return [pltpu.make_async_copy(source, outs[0].at[pl.ds(step * width, width)], sems_one.at[step % 2, 0])]
        row = pl.multiple_of(step * share, 16)
        return spread_copies(scal, source, row, *outs, sems_one.at[step % 2])

    def copies_two(step):
        c = step - 1
        source = two.at[step % 2]
        if parts == 1:
            target = outs[1].at[pl.ds(c * width, width)]
            return [pltpu.make_async_copy(source, target, sems_two.at[step % 2, 0])]
        core, size = scal[0, 3] & 1, 4 * share
        where = c ^ (scal[0, 3] >> 1)
        where = 2 * (where & 1) + (where >> 1)
        return [
            pltpu.make_async_copy(
                source.at[pl.ds(pl.multiple_of(half_at * size, 16), size)],
                ref.at[where, pl.ds(5 * share, size)],
                sems_two.at[step % 2, j],
            )
            for j, (half_at, ref) in enumerate(((core, outs[0]), (1 - core, outs[1])))
        ]

    @pl.when(i >= 2)
    def _():
        wait(copies_one(i - 2))

    @pl.when(i >= 3)
    def _():
        wait(copies_two(i - 2))

    @pl.when(i == 0)
    def _():
        one[slot] = tn(flat(attn), flat(branch)).astype(BF16)

    @pl.when(i > 0)
    def _():
        one[slot] = tn(flat(act2), flat(gpre)).astype(BF16)
        two[slot] = tn(flat(hid), flat(grad)).astype(BF16)
        start(copies_two(i))

    start(copies_one(i))

    @pl.when(i == 4)
    def _():
        for step in (3, 4):
            wait(copies_one(step))
            wait(copies_two(step))


def ffn_grads_call(scal, parts, hid, gpre, act2, attn, branch, grad):
    count, rows, width = grad.shape
    share = width // parts
    chunk = pl.BlockSpec((count, 1, rows, width), lambda i: (0, jnp.maximum(i - 1, 0), 0, 0))
    if parts == 8:
        outs = (jax.ShapeDtypeStruct((4, 9 * share, width), BF16),) * 2
    else:
        outs = (
            jax.ShapeDtypeStruct((5 * width, width), BF16),
            jax.ShapeDtypeStruct((4 * width, width), BF16),
        )
    return pl.pallas_call(
        functools.partial(ffn_grads_kernel, parts),
        out_shape=outs,
        grid=(5,),
        in_specs=[pl.BlockSpec(memory_space=pltpu.SMEM), chunk, chunk]
        + [whole_spec(a) for a in (act2, attn, branch, grad)],
        out_specs=[ANY, ANY],
        scratch_shapes=[
            pltpu.VMEM((2, width, width), BF16),
            pltpu.VMEM((2, width, width), BF16),
            pltpu.SemaphoreType.DMA((2, 8)),
            pltpu.SemaphoreType.DMA((2, 2)),
        ],
        compiler_params=params(),
        cost_estimate=cost(18 * count * rows * width * width, 25e6),
        name="ffn_grads",
    )(scal, hid, gpre, act2, attn, branch, grad)


def last_kernel(parts, pieces, scal, vec, sums, x_in, gmid_in, dq_in, dk_in, dv_in, *rest):
    refs, rest = rest[:pieces], rest[pieces:]
    gin_out, outs = rest[0], rest[1:-13]
    weights, work, total, wsems, sems, x, gmid, dq, dk, dv, gin, in_sems, gin_sem = rest[-13:]
    count, rows, width = x.shape
    loads = [
        pltpu.make_async_copy(ref, buf, in_sems.at[j])
        for j, (ref, buf) in enumerate(
            ((x_in, x), (dq_in, dq), (dk_in, dk), (dv_in, dv), (gmid_in, gmid))
        )
    ]
    start(loads[:4])
    tokens = count * rows
    depth = weights.shape[1]
    share = width // parts
    copies = piece_copies(scal, first_pieces(refs), 0, depth, weights, wsems)
    start(copies)
    start(loads[4:])
    wait(loads[:1])
    unit, inverse = unit_of(x[...].reshape(tokens, width).astype(F32))
    act = (unit * vec[0:1] + vec[1:2]).astype(BF16)
    given, stores = [], []
    for j, ref in enumerate((dq, dk, dv)):
        wait(loads[1 + j : 2 + j])
        given.append(ref[...].reshape(tokens, width))
        work[j] = tn(act, given[j]).astype(BF16)
        if parts == 1:
            target = outs[0].at[pl.ds(j * width, width)]
            stores.append(pltpu.make_async_copy(work.at[j], target, sems.at[j, 0]))
            stores[-1].start()
        else:
            stores += spread_copies(scal, work.at[j], j * share, *outs, sems.at[j])
            start(stores[-8:])
    wait(copies)
    grad_one = jnp.zeros(unit.shape, F32)
    for j in range(3):
        weight = weights[:, j * share : (j + 1) * share, :].reshape(width, width)
        grad_one = grad_one + nt(given[j], weight)
    back = norm_back(grad_one * vec[0:1], unit, inverse)
    wait(loads[4:])
    gin[...] = (gmid[...].reshape(tokens, width) + back).astype(BF16).reshape(gin.shape)
    stores.append(pltpu.make_async_copy(gin, gin_out, gin_sem.at[0]))
    stores[-1].start()
    total[0:8] = (sums[0] + sums[1]).astype(BF16)
    total[8:32] = jnp.zeros((24, width), BF16)
    rows_now = [
        column_sum(grad_one * unit),
        column_sum(grad_one),
        column_sum(given[0].astype(F32)),
        column_sum(given[2].astype(F32)),
    ]
    for j, row in enumerate(rows_now):
        total[8 + j : 9 + j] = row.astype(BF16)
    if parts == 1:
        stores.append(
            pltpu.make_async_copy(total, outs[0].at[pl.ds(3 * width, 32)], sems.at[3, 0])
        )
        stores[-1].start()
    else:
        for rel in range(8):
            x_bit, y_bit = bits(rel)
            target = outs[rel & 1].at[2 * x_bit + y_bit, pl.ds(3 * share, 32)]
            stores.append(pltpu.make_async_copy(total, target, sems.at[3, rel]))
            stores[-1].start()
    wait(stores)


def last_call(scal, x, gmid, dq, dk, dv, vec, sums, first):
    parts, depth = (8, first[0].shape[1]) if len(first) > 1 else first[0].shape[:2]
    width = x.shape[2]
    share = width // parts
    gin = jax.ShapeDtypeStruct(x.shape, BF16)
    if parts == 1:
        outs = (jax.ShapeDtypeStruct((3 * width + 32, width), BF16),)
    else:
        outs = (jax.ShapeDtypeStruct((4, 3 * share + 32, width), BF16),) * 2
    return pl.pallas_call(
        functools.partial(last_kernel, parts, len(first)),
        out_shape=(gin, *outs),
        grid=(1,),
        in_specs=[pl.BlockSpec(memory_space=pltpu.SMEM), whole_spec(vec), whole_spec(sums)]
        + [ANY] * (5 + len(first)),
        out_specs=[ANY] * (1 + len(outs)),
        scratch_shapes=[
            pltpu.VMEM((parts, depth, width), BF16),
            pltpu.VMEM((3, width, width), BF16),
            pltpu.VMEM((32, width), BF16),
            pltpu.SemaphoreType.DMA((8,)),
            pltpu.SemaphoreType.DMA((4, 8)),
            pltpu.VMEM(x.shape, BF16),
            pltpu.VMEM(x.shape, F32),
            pltpu.VMEM(x.shape, BF16),
            pltpu.VMEM(x.shape, BF16),
            pltpu.VMEM(x.shape, BF16),
            pltpu.VMEM(x.shape, BF16),
            pltpu.SemaphoreType.DMA((5,)),
            pltpu.SemaphoreType.DMA((1,)),
        ],
        compiler_params=params(),
        cost_estimate=cost(12 * x.shape[0] * x.shape[1] * width * width, 20e6),
        name="last",
    )(scal, vec, sums, x, gmid, dq, dk, dv, *first)


def outer(ids):
    return (ids[0, 2] == 0) | (ids[0, 2] == 3)


def halves(ids, mine, got):
    swap = outer(ids)
    return jnp.where(swap, mine[...], got[...]).astype(F32), jnp.where(swap, got[...], mine[...]).astype(F32)


def finish_ffn_kernel(ids, mine, got, out_w, up_w, down_w, both):
    share, width = out_w.shape
    size = mine.shape[0]
    both[0:size], both[size:] = halves(ids, mine, got)
    out_w[...] = both[0:share]
    for c in range(4):
        up_w[:, c * width : (c + 1) * width] = both[(1 + c) * share : (2 + c) * share]
    down_w[...] = both[5 * share :]


def finish_ffn_call(ids, mine, got, share):
    width = mine.shape[1]
    outs = (
        jax.ShapeDtypeStruct((share, width), F32),
        jax.ShapeDtypeStruct((share, 4 * width), F32),
        jax.ShapeDtypeStruct((4 * share, width), F32),
    )
    return pl.pallas_call(
        finish_ffn_kernel,
        out_shape=outs,
        grid=(1,),
        in_specs=[pl.BlockSpec(memory_space=pltpu.SMEM), whole_spec(mine), whole_spec(got)],
        out_specs=[whole_spec(a) for a in outs],
        scratch_shapes=[pltpu.VMEM((2 * mine.shape[0], width), F32)],
        compiler_params=params(),
        cost_estimate=cost(0, 6e6),
        name="finish_ffn",
    )(ids, mine, got)


def finish_proj_kernel(ids, mine, got, q_w, k_w, v_w, *rest):
    *vectors, bias, both = rest
    share, width = q_w.shape
    size = mine.shape[0]
    both[0:size], both[size:] = halves(ids, mine, got)
    for j, out in enumerate((q_w, k_w, v_w)):
        out[...] = both[j * share : (j + 1) * share]
    me = ids[0, 3]
    row = lax.broadcasted_iota(jnp.int32, (width, LANES), 0)
    column = lax.broadcasted_iota(jnp.int32, (width, LANES), 1)
    pick = jnp.where(row == column + me * share, 1.0, 0.0).astype(BF16)
    picked = nn(both[3 * share : 3 * share + 16].astype(BF16), pick)
    for out, j in zip(vectors, (8, 9, 10, 11, 2, 0, 1, 3)):
        out[...] = picked[j : j + 1, 0:share]
    line = both[pl.ds(3 * share + 4 + me // 2, 1), :]
    bias[...] = jnp.where(me % 2 == 0, line[:, 0 : 4 * share], line[:, 4 * share :])


def finish_proj_call(ids, mine, got, share):
    width = mine.shape[1]
    outs = (
        [jax.ShapeDtypeStruct((share, width), F32)] * 3
        + [jax.ShapeDtypeStruct((1, share), F32)] * 8
        + [jax.ShapeDtypeStruct((1, 4 * share), F32)]
    )
    return pl.pallas_call(
        finish_proj_kernel,
        out_shape=outs,
        grid=(1,),
        in_specs=[pl.BlockSpec(memory_space=pltpu.SMEM), whole_spec(mine), whole_spec(got)],
        out_specs=[whole_spec(a) for a in outs],
        scratch_shapes=[pltpu.VMEM((2 * mine.shape[0], width), F32)],
        compiler_params=params(),
        cost_estimate=cost(0, 2e6),
        name="finish_proj",
    )(ids, mine, got)


RIGHT = [(0, 1), (1, 2), (2, 3)]
LEFT = [(1, 0), (2, 1), (3, 2)]
RIGHT_AGAIN = [(1, 2), (2, 3)]
LEFT_AGAIN = [(2, 1), (1, 0)]


def shifted(array, pairs):
    return lax.ppermute(array, "seq", pairs)


def crossed(array, distance):
    return lax.ppermute(array, "dp", [(i, i ^ distance) for i in range(8)])


def neighbours(array):
    left, right = shifted(array, RIGHT), shifted(array, LEFT)
    return left, right, shifted(left, RIGHT_AGAIN), shifted(right, LEFT_AGAIN)


def after(value, *others):
    return lax.optimization_barrier((value, *others))[0]


def add(*arrays):
    return sum(array.astype(F32) for array in arrays).astype(BF16)


PAIRS = [(0, 1), (1, 0), (2, 3), (3, 2)]
ACROSS = [(0, 3), (3, 0), (1, 2), (2, 1)]


class Reduction:
    def __init__(self, keep, send, place):
        self.keep, self.place, self.cut = keep, place, keep.shape[1] // 2
        self.got = crossed(send, 1)

    def second(self, *order):
        keep, got, cut = self.keep, after(self.got, *order), self.cut
        self.got = got
        one = add(keep[2:4, :cut], got[2:4, :cut])
        two = add(keep[1::2, cut:], got[1::2, cut:])
        self.more = crossed(one, 2), crossed(two, 4)
        return one, two

    def third(self, *order):
        keep, got, cut = self.keep, self.got, self.cut
        more = self.more = tuple(after(m, *order) for m in self.more)
        one = add(keep[1, :cut], got[1, :cut], more[0][1])
        two = add(keep[2, cut:], got[2, cut:], more[1][1])
        self.last = crossed(one, 4), crossed(two, 2)
        return one, two

    def fourth(self, *order):
        keep, got, cut = self.keep, self.got, self.cut
        last = tuple(after(m, *order) for m in self.last)
        one = add(keep[0, :cut], got[0, :cut], self.more[0][0], last[0])
        two = add(keep[0, cut:], got[0, cut:], self.more[1][0], last[1])
        return self.over_seq(one, two)

    def over_seq(self, one, two):
        outside = (self.place == 0) | (self.place == 3)
        self.mine = jnp.where(outside, one, two)
        other = jnp.where(outside, two, one)
        self.got = shifted(other, PAIRS)
        return self.mine, other

    def fifth(self, *order):
        self.mine = add(self.mine, after(self.got, *order))
        self.got = shifted(self.mine, ACROSS)
        return (self.mine,)

    def sixth(self, *order):
        self.mine = add(self.mine, after(self.got, *order))
        self.got = shifted(self.mine, PAIRS)
        return (self.mine,)

    def result(self):
        return self.mine, self.got


def windows(slots, place, me):
    seqs, _, rows = slots.shape
    whole = slots.reshape(seqs, 5 * rows)
    first, last = slots[:, 2, :1], slots[:, 2, -1:]
    low = jnp.sum((whole < first).astype(jnp.int32), axis=1)
    high = jnp.sum((whole <= last).astype(jnp.int32), axis=1)
    begin = (low // LANES) * LANES
    chunks = jnp.maximum((high - begin + rows - 1) // rows, 2)
    begin = jnp.minimum(begin, rows * (jnp.minimum(5, 6 - place) - chunks))
    other = jnp.zeros_like(begin)
    return jnp.stack([begin, chunks, other + place, other + me], axis=1)


def per_device(
    inputs,
    segment_ids,
    norm1_gain,
    norm1_shift,
    query_weight,
    query_bias,
    key_weight,
    value_weight,
    value_bias,
    out_weight,
    out_bias,
    norm2_gain,
    norm2_shift,
    fc1_weight,
    fc1_bias,
    fc2_weight,
    fc2_bias,
    grad_output,
):
    seqs, rows, width = inputs.shape
    devices = lax.axis_size("dp")
    share = query_weight.shape[0]
    place, me = lax.axis_index("seq"), lax.axis_index("dp")
    direct = devices == 8
    parts = 8 if direct else 1
    zero = jnp.zeros((), jnp.int32)
    ids = jnp.stack([zero, zero, place, me])[None]

    vectors = (
        norm1_gain, norm1_shift, query_bias, value_bias,
        out_bias, norm2_gain, norm2_shift, fc2_bias, fc1_bias,
    )
    tokens = tokens_call(inputs, segment_ids)
    query_bias = after(query_bias, tokens)
    vectors = vectors[:2] + (query_bias,) + vectors[3:]
    packed_one, packed_two = pack_call(
        (query_weight, key_weight, value_weight, out_weight, fc1_weight, fc2_weight), vectors
    )
    left, right = shifted(tokens, RIGHT), shifted(tokens, LEFT)
    if direct:
        near = jnp.stack(
            [after(packed_one, left, right)] + [crossed(packed_one, d) for d in (2, 4, 6)]
        )
        first = near, crossed(near, 1)
        vec = unpack_call(*first, ids)
        second = (lax.all_gather(after(packed_two, near), "dp", axis=0),)
    else:
        one = lax.all_gather(packed_one, "dp", axis=0)
        two = lax.all_gather(packed_two, "dp", axis=0)
        small = one[:, 3 * share :]
        vec = jnp.concatenate(
            [
                small[:, :8, :share].transpose(1, 0, 2).reshape(8, width),
                small[:, 8, : 4 * share].reshape(4, width),
                jnp.zeros((4, width), BF16),
            ]
        ).astype(F32)
        first = (
            jnp.concatenate(
                [one[:, j * share : (j + 1) * share].reshape(width, width) for j in range(3)]
                + [jnp.zeros((16, width), BF16)]
            )[None],
        )
        second = (
            jnp.concatenate(
                [two[:, j * share : (j + 1) * share].reshape(width, width) for j in range(5)]
                + [two[:, 5 * share :].reshape(4 * width, width)]
            )[None],
        )
    far_left, far_right = shifted(left, RIGHT_AGAIN), shifted(right, LEFT_AGAIN)

    qkv = project_call(ids, (inputs, left, right), vec, first, None, seqs, rows)
    far_left, far_right, *qkv = lax.optimization_barrier((far_left, far_right, *qkv))
    late_ids = after(segment_ids, qkv[0])

    def ids_of(message):
        return message[:, rows, :rows].astype(jnp.int32)

    before, beyond = jnp.full_like(late_ids, -1), jnp.full_like(late_ids, 99)
    slots = jnp.stack(
        [
            jnp.where(place >= 2, ids_of(far_left), before),
            jnp.where(place >= 1, ids_of(left), before),
            late_ids,
            jnp.where(place <= 2, ids_of(right), beyond),
            jnp.where(place <= 1, ids_of(far_right), beyond),
        ],
        axis=1,
    )
    scal = windows(slots, place, me)
    lane = lax.broadcasted_iota(jnp.int32, (1, 1, LANES), 2)
    seg = ((slots.reshape(seqs, 5 * rows)[:, :, None] == lane) | (lane >= 16)).astype(BF16)
    qf = jnp.where((lane < 4) & (lane != late_ids[:, :, None]), -BIG, 0.0).astype(BF16)
    qkv = list(project_call(scal, (far_left, far_right), vec, first, qkv, seqs, rows))

    attn, features = attend_call(0, seqs, scal, *qkv, seg, qf, None)

    split = ((0, 1), (1, seqs - 1))

    def middle(at, count, before):
        *shared, msg = middle_call(
            at, count, scal, inputs, attn, grad_output, features, second, vec, before
        )
        return shared, msg

    shared, msg_a = middle(*split[0], None)
    left_a, right_a = shifted(msg_a, RIGHT), shifted(msg_a, LEFT)
    far_a = shifted(msg_a, [(0, 2), (1, 3), (2, 0), (3, 1)])
    shared, msg_b = middle(*split[1], shared)
    left_a, right_a, far_a, msg_b = lax.optimization_barrier((left_a, right_a, far_a, msg_b))
    left_b, right_b = shifted(msg_b, RIGHT), shifted(msg_b, LEFT)
    out, hid, gpre, act2, branch, gmid, sums = shared
    ffn = ffn_grads_call(
        after(scal, msg_b), parts, hid, gpre, act2, attn, branch, grad_output
    )
    left_b, right_b, *ffn = lax.optimization_barrier((left_b, right_b, *ffn))
    all_a = msg_a, left_a, right_a, far_a, far_a
    far_left_b, far_right_b = shifted(left_b, RIGHT_AGAIN), shifted(right_b, LEFT_AGAIN)
    all_b = msg_b, left_b, right_b, far_left_b, far_right_b
    dq = query_grads_call(0, 1, after(scal, ffn[0]), *qkv, msg_a, seg, None)
    if direct:
        reduction = Reduction(*ffn, place)
        order = reduction.second(dq)
        dq = query_grads_call(1, 2, after(scal, *order), *qkv, msg_b, seg, dq)
        order = reduction.third(dq)
        dkv = key_grads_call(1, 1, after(scal, *order), *qkv, seg, all_b, None)
        order = reduction.fourth(dkv[0])
        dkv = key_grads_call(2, 1, after(scal, *order), *qkv, seg, all_b, tuple(dkv), 1)
        order = reduction.fifth(dkv[0])
        dkv = key_grads_call(0, 1, after(scal, *order), *qkv, seg, all_a, tuple(dkv))
        grad_inputs, *proj = last_call(
            after(scal, dkv[0]), inputs, gmid, dq, *dkv, vec, sums, first
        )
        order = reduction.sixth(grad_inputs)
        tail = Reduction(proj[0], after(proj[1], *order), place)
        tail.second()
        tail.third()
        out_w, up_w, down_w = finish_ffn_call(ids, *reduction.result(), share)
        tail.fourth(out_w)
        tail.fifth()
        tail.sixth()
        q_w, k_w, v_w, *small, up_b = finish_proj_call(ids, *tail.result(), share)
        small = [s.reshape(share) for s in small]
        return (
            out, grad_inputs, small[0], small[1], q_w, small[2], k_w, v_w, small[3], out_w,
            small[4], small[5], small[6], up_w, up_b.reshape(4 * share), down_w, small[7],
        )

    dq = query_grads_call(1, 2, scal, *qkv, msg_b, seg, dq)
    dkv = key_grads_call(0, 1, scal, *qkv, seg, all_a, None)
    dkv = key_grads_call(1, seqs - 1, scal, *qkv, seg, all_b, tuple(dkv))
    grad_inputs, proj = last_call(scal, inputs, gmid, dq, *dkv, vec, sums, first)

    def reduced(array, count):
        cut = array.reshape(count, devices, -1, width).transpose(1, 0, 2, 3)
        cut = cut.reshape(devices, -1, width)
        part = lax.psum_scatter(cut, "dp", scatter_dimension=0, tiled=True)[0]
        return lax.psum(part, "seq").astype(F32)

    ffn_one, ffn_two = reduced(ffn[0], 5), reduced(ffn[1], 1)
    proj_w = reduced(proj[: 3 * width], 3)
    vectors = lax.psum(proj[3 * width : 3 * width + 16].astype(F32), ("dp", "seq"))
    mine = lax.dynamic_slice(vectors, (0, me * share), (16, share))
    up_grad = ffn_one[share:].reshape(4, share, width).transpose(1, 0, 2)
    up_bias = lax.dynamic_slice(vectors[4:8].reshape(4 * width), (me * 4 * share,), (4 * share,))
    return (
        out, grad_inputs, mine[8], mine[9], proj_w[:share], mine[10], proj_w[share : 2 * share],
        proj_w[2 * share :], mine[11], ffn_one[:share], mine[2], mine[0], mine[1],
        up_grad.reshape(share, 4 * width), up_bias, ffn_two, mine[3],
    )


def solution(mesh):
    token, matrix, vector = P("dp", "seq", None), P("dp", None), P("dp")
    return jax.shard_map(
        per_device,
        mesh=mesh,
        in_specs=(
            token, P("dp", "seq"), vector, vector, matrix, vector, matrix, matrix, vector,
            matrix, vector, vector, vector, matrix, vector, matrix, vector, token,
        ),
        out_specs=(
            token, token, vector, vector, matrix, vector, matrix, matrix, vector,
            matrix, vector, vector, vector, matrix, vector, matrix, vector,
        ),
        check_vma=False,
    )
```

```python
import functools

import jax
import jax.numpy as jnp
from jax import lax
from jax.experimental import pallas as pl
from jax.experimental.pallas import tpu as pltpu
from jax.sharding import PartitionSpec as P

F32 = jnp.float32
BF16 = jnp.bfloat16
HD = 64
LANES = 128
ROWS = 16
BIG = 1e30
EPSILON = 1e-05
MIB = 1 << 20

ANY = pl.BlockSpec(memory_space=pl.ANY)
VMEM = pl.BlockSpec(memory_space=pltpu.VMEM)


def nn(left, right):
    return lax.dot_general(left, right, (((1,), (0,)), ((), ())), preferred_element_type=F32)


def nt(left, right):
    return lax.dot_general(left, right, (((1,), (1,)), ((), ())), preferred_element_type=F32)


def tn(left, right):
    return lax.dot_general(left, right, (((0,), (0,)), ((), ())), preferred_element_type=F32)


def unit_of(values):
    center = values - jnp.mean(values, axis=-1, keepdims=True)
    inverse = lax.rsqrt(jnp.mean(center * center, axis=-1, keepdims=True) + EPSILON)
    return center * inverse, inverse


def norm_back(scaled, unit, inverse):
    return inverse * (
        scaled
        - jnp.mean(scaled, axis=-1, keepdims=True)
        - unit * jnp.mean(scaled * unit, axis=-1, keepdims=True)
    )


def column_sum(values):
    return jnp.sum(values, axis=0, keepdims=True)


def cost(flops, moved, transcendentals=0):
    return pl.CostEstimate(flops=int(flops / 4), bytes_accessed=int(moved / 4), transcendentals=0)


def params(limit=56, grid=1):
    return pltpu.CompilerParams(dimension_semantics=("arbitrary",) * grid, vmem_limit_bytes=limit * MIB)


def bits(rel):
    return (rel >> 1) & 1, (rel >> 2) & 1


def tokens_kernel(x, seg, tokens):
    count, rows, width = x.shape
    tokens[:, 0:rows] = x[...]
    tokens[:, rows:] = jnp.zeros((count, 16, width), BF16)
    for s in range(count):
        tokens[s, rows : rows + 1, 0:rows] = seg[s : s + 1].astype(F32).astype(BF16)


def tokens_call(x, seg):
    out = jax.ShapeDtypeStruct((x.shape[0], x.shape[1] + 16, x.shape[2]), BF16)
    return pl.pallas_call(
        tokens_kernel,
        out_shape=out,
        grid=(1,),
        in_specs=[whole_spec(x), whole_spec(seg)],
        out_specs=whole_spec(out),
        compiler_params=params(),
        cost_estimate=cost(0, 3e6),
        name="tokens",
    )(x, seg)


def pack_kernel(wq, wk, wv, wo, up, down, *rest):
    *vectors, first, second = rest
    share, width = wq.shape
    first[0:share] = wq[...]
    first[share : 2 * share] = wk[...]
    first[2 * share : 3 * share] = wv[...]
    first[3 * share :] = jnp.zeros((16, width), BF16)
    for j, vector in enumerate(vectors):
        size = vector.shape[1]
        first[3 * share + j : 3 * share + j + 1, 0:size] = vector[...]
    second[0:share] = wo[...]
    for c in range(4):
        second[(1 + c) * share : (2 + c) * share] = up[:, c * width : (c + 1) * width]
    second[5 * share :] = down[...]


def whole_spec(array):
    zeros = (0,) * len(array.shape)
    return pl.BlockSpec(array.shape, lambda i: zeros)


def pack_call(matrices, vectors):
    share, width = matrices[0].shape
    args = (*matrices, *[v.reshape(1, -1) for v in vectors])
    outs = (
        jax.ShapeDtypeStruct((3 * share + 16, width), BF16),
        jax.ShapeDtypeStruct((9 * share, width), BF16),
    )
    return pl.pallas_call(
        pack_kernel,
        out_shape=outs,
        grid=(1,),
        in_specs=[whole_spec(a) for a in args],
        out_specs=[whole_spec(a) for a in outs],
        compiler_params=params(),
        cost_estimate=cost(0, 6e6),
        name="pack",
    )(*args)


def piece_copies(scal, pieces, low, size, target, sems):
    if len(pieces) == 1:
        return [pltpu.make_async_copy(pieces[0][0].at[:, pl.ds(low, size)], target, sems.at[0])]
    me, copies = scal[0, 3], []
    for ref, index, rel, start, stop in pieces:
        if start <= low and low + size <= stop:
            source = ref if index is None else ref.at[index]
            copies.append(
                pltpu.make_async_copy(
                    source.at[pl.ds(low - start, size)], target.at[me ^ rel], sems.at[rel]
                )
            )
    return copies


def first_pieces(refs):
    if len(refs) == 1:
        return [(refs[0],)]
    near, far = refs
    return [(near, j, 2 * j, 0, near.shape[1]) for j in range(4)] + [
        (far, j, 2 * j + 1, 0, far.shape[1]) for j in range(4)
    ]


def second_pieces(refs):
    if len(refs) == 1:
        return [(refs[0],)]
    full = refs[0].shape[0]
    split = refs[3].shape[0]
    pieces = []
    for core in range(2):
        own, x, y, xy_low, xy_high = refs[5 * core : 5 * core + 5]
        pieces += [(own, None, core, 0, full), (x, None, 2 + core, 0, full), (y, None, 4 + core, 0, full)]
        pieces += [(xy_low, None, 6 + core, 0, split), (xy_high, None, 6 + core, split, full)]
    return pieces


def start(copies):
    for copy in copies:
        copy.start()


def wait(copies):
    for copy in copies:
        copy.wait()


def unpack_kernel(near, far, scal, vec):
    me = scal[0, 3]
    share = 96
    width = vec.shape[1]
    total = jnp.zeros((16, width), F32)
    row = lax.broadcasted_iota(jnp.int32, (LANES, width), 0)
    column = lax.broadcasted_iota(jnp.int32, (LANES, width), 1)
    for rel in range(8):
        device = me ^ rel
        block = (near if rel % 2 == 0 else far)[rel // 2]
        pick = jnp.where((row < share) & (column == row + device * share), 1.0, 0.0).astype(BF16)
        total = total + nn(block[:, 0:LANES], pick)
        bias = block[8:9, 0 : 4 * share].astype(F32)
        vec[pl.ds(8 + device // 2, 1), pl.ds(pl.multiple_of((device % 2) * 4 * share, LANES), 4 * share)] = bias
    vec[0:8] = total[0:8]
    vec[12:16] = jnp.zeros((4, width), F32)


def unpack_call(near, far, ids):
    width = near.shape[2]
    out = jax.ShapeDtypeStruct((16, width), F32)
    tail = pl.BlockSpec((4, 16, width), lambda i: (0, near.shape[1] // 16 - 1, 0))
    return pl.pallas_call(
        unpack_kernel,
        out_shape=out,
        grid=(1,),
        in_specs=[tail, tail, pl.BlockSpec(memory_space=pltpu.SMEM)],
        out_specs=whole_spec(out),
        compiler_params=params(),
        cost_estimate=cost(1e6, 4e6),
        name="unpack",
    )(near, far, ids)


def needed(scal, seq, slot, rows):
    low, high = scal[seq, 0], scal[seq, 0] + scal[seq, 1] * rows
    return (slot * rows < high) & ((slot + 1) * rows > low)


def project_kernel(far, pieces, scal, vec, *rest):
    sources = rest[: 2 if far else 3]
    rest = rest[len(sources) :]
    refs, (*outs, buf, weights, made, sems, wsems, out_sems) = rest[:pieces], rest[-9:]
    i = pl.program_id(0)
    steps = 1 if far else 3
    count, rows, width = buf.shape[1:]
    share = width // weights.shape[0]
    after = scal[0, 2] >= 2
    copies = piece_copies(scal, first_pieces(refs), 0, weights.shape[1], weights, wsems)
    if far:
        slot = jnp.where(after, 0, 4)
        used = needed(scal, 0, slot, rows)
        for s in range(1, count):
            used = used | needed(scal, s, slot, rows)
    else:
        slot = jnp.where(i == 0, 2, jnp.where(i == 1, 1, 3))
        used = True

    def load(step, act):
        for j, ref in enumerate(sources):
            when = (after == (j == 0)) if far else (step == j)

            @pl.when(when)
            def _():
                source = ref.at[:, pl.ds(0, rows)]
                act(pltpu.make_async_copy(source, buf.at[step % 2], sems.at[step % 2]))

    def stores(step, where):
        return [
            pltpu.make_async_copy(
                made.at[step % 2, t], outs[t].at[:, pl.ds(where * rows, rows)], out_sems.at[step % 2, t]
            )
            for t in range(3)
        ]

    @pl.when(i == 0)
    def _():
        load(0, lambda copy: copy.start())
        start(copies)

    @pl.when(i + 1 < steps)
    def _():
        load(i + 1, lambda copy: copy.start())

    load(i, lambda copy: copy.wait())

    @pl.when(i == 0)
    def _():
        wait(copies)

    @pl.when(i >= 2)
    def _():
        wait(stores(i, 0))

    def work():
        unit, _ = unit_of(buf[i % 2].reshape(count * rows, width).astype(F32))
        act = (unit * vec[0:1] + vec[1:2]).astype(BF16)
        for t in range(3):
            weight = weights[:, t * share : (t + 1) * share, :].reshape(width, width)
            result = nn(act, weight)
            if t == 0:
                result = (result + vec[2:3]).astype(BF16) * jnp.asarray(HD**-0.5, BF16)
            if t == 2:
                result = result + vec[3:4]
            made[i % 2, t] = result.astype(BF16).reshape(count, rows, width)
        start(stores(i, slot))

    if far:

        @pl.when(used)
        def _():
            work()
            wait(stores(0, 0))
    else:
        work()

        @pl.when(i == steps - 1)
        def _():
            wait(stores(i, 0))
            wait(stores(i - 1, 0))


def project_call(scal, sources, vec, first, before, seqs, rows):
    far = before is not None
    width = vec.shape[1]
    out = jax.ShapeDtypeStruct((seqs, 5 * rows, width), BF16)
    parts, depth = (8, first[0].shape[1]) if len(first) > 1 else first[0].shape[:2]
    steps = 1 if far else 3
    at = 2 + len(sources) + len(first)
    return pl.pallas_call(
        functools.partial(project_kernel, far, len(first)),
        out_shape=(out, out, out),
        grid=(steps,),
        in_specs=[pl.BlockSpec(memory_space=pltpu.SMEM), whole_spec(vec)]
        + [ANY] * (len(sources) + len(first) + (3 if far else 0)),
        out_specs=[ANY] * 3,
        scratch_shapes=[
            pltpu.VMEM((2, seqs, rows, width), BF16),
            pltpu.VMEM((parts, depth, width), BF16),
            pltpu.VMEM((2, 3, seqs, rows, width), BF16),
            pltpu.SemaphoreType.DMA((2,)),
            pltpu.SemaphoreType.DMA((8,)),
            pltpu.SemaphoreType.DMA((2, 3)),
        ],
        input_output_aliases={at: 0, at + 1: 1, at + 2: 2} if far else {},
        compiler_params=params(),
        cost_estimate=cost(6 * steps * seqs * rows * width * width, 8e6 * steps),
        name="far" if far else "near",
    )(scal, vec, *sources, *first, *(before or ()))


def lane_is(*wanted):
    lane = lax.broadcasted_iota(jnp.int32, (1, LANES), 1)
    hit = lane == wanted[0]
    for other in wanted[1:]:
        hit = hit | (lane == other)
    return hit


def head_mask(which):
    lane = lax.broadcasted_iota(jnp.int32, (1, LANES), 1)
    return (lane < HD) if which == 0 else (lane >= HD)


def half(pair, which):
    return jnp.where(head_mask(which), pair, jnp.zeros_like(pair))


def ones_at(rows, *wanted):
    return jnp.broadcast_to(jnp.where(lane_is(*wanted), 1.0, 0.0).astype(BF16), (rows, LANES))


def lanes(pair):
    return pl.ds(pl.multiple_of(pair * LANES, LANES), LANES)


def windowed(at, count, scal, arrays, rows):
    i = pl.program_id(0)

    def each(step, act):
        for c in range(4):

            @pl.when(c < scal[at + step, 1])
            def _():
                begin = pl.multiple_of(scal[at + step, 0] + c * rows, ROWS)
                for ref, buf, sems in arrays:
                    source = ref.at[at + step, pl.ds(begin, rows)]
                    target = buf.at[step % 2, pl.ds(c * rows, rows)]
                    act(pltpu.make_async_copy(source, target, sems.at[step % 2, c]))

    @pl.when(i == 0)
    def _():
        each(i, lambda copy: copy.start())

    @pl.when(i + 1 < count)
    def _():
        each(i + 1, lambda copy: copy.start())

    each(i, lambda copy: copy.wait())


def by_chunks(chunks, pairs, body):
    for c in range(2, 5):

        @pl.when(chunks == c)
        def _():
            lax.fori_loop(0, pairs, lambda p, _: body(c, p), None, unroll=3)


def window_scratch(rows, widths):
    return [pltpu.VMEM((2, 4 * rows, w), BF16) for w in widths] + [
        pltpu.SemaphoreType.DMA((2, 4)) for _ in widths
    ]


def attend_kernel(at, count, scal, q, qf, k, v, seg, *rest):
    o_out, qf_out, kbuf, vbuf, sbuf, ksem, vsem, ssem, feats = rest[-9:]
    i = pl.program_id(0)
    slot = i % 2
    rows, width = q.shape[1:]
    windowed(at, count, scal, ((k, kbuf, ksem), (v, vbuf, vsem), (seg, sbuf, ssem)), rows)
    feats[...] = qf[0].astype(F32)

    def body(chunks, pair):
        size = chunks * rows
        q_pair, features = q[0, :, lanes(pair)], qf[0]
        q_aug = jnp.concatenate(
            [
                jnp.concatenate([half(q_pair, 0), half(q_pair, 1)], axis=0),
                jnp.concatenate([features, features], axis=0),
            ],
            axis=1,
        )
        k_aug = jnp.concatenate([kbuf[slot, :size, lanes(pair)], sbuf[slot, :size, :]], axis=1)
        v_aug = jnp.concatenate(
            [vbuf[slot, :size, lanes(pair)], jnp.ones((size, LANES), BF16)], axis=1
        )
        scores = nt(q_aug, k_aug)
        highest = jnp.max(scores, axis=-1, keepdims=True)
        both = nn(jnp.exp(scores - highest).astype(BF16), v_aug)
        totals = both[:, LANES:]
        result = both[:, :LANES] / totals
        o_out[0, :, lanes(pair)] = jnp.where(head_mask(0), result[:rows], result[rows:]).astype(BF16)
        lse = highest + jnp.log(totals)
        top = lse.astype(BF16).astype(F32)
        rest_of = top - lse
        lane = 16 + 8 * pair
        new = jnp.where(lane_is(lane), -top[:rows], feats[...])
        new = jnp.where(lane_is(lane + 1), rest_of[:rows], new)
        new = jnp.where(lane_is(lane + 4), -top[rows:], new)
        feats[...] = jnp.where(lane_is(lane + 5), rest_of[rows:], new)

    by_chunks(scal[at + i, 1], width // LANES, body)
    qf_out[0] = feats[...].astype(BF16)


def attend_call(at, count, scal, q, k, v, seg, qf, before):
    seqs, total, width = q.shape
    rows = qf.shape[1]
    flat = pl.BlockSpec((1, rows, width), lambda s, c: (at + s, 0, 0))
    narrow = pl.BlockSpec((1, rows, LANES), lambda s, c: (at + s, 0, 0))
    return pl.pallas_call(
        functools.partial(attend_kernel, at, count),
        out_shape=(
            jax.ShapeDtypeStruct((seqs, rows, width), BF16),
            jax.ShapeDtypeStruct((seqs, rows, LANES), BF16),
        ),
        grid_spec=pltpu.PrefetchScalarGridSpec(
            num_scalar_prefetch=1,
            grid=(count,),
            in_specs=[pl.BlockSpec((1, rows, width), lambda s, c: (at + s, 2, 0)), narrow]
            + [ANY] * (5 if before else 3),
            out_specs=[flat, narrow],
            scratch_shapes=window_scratch(rows, (width, width, LANES))
            + [pltpu.VMEM((rows, LANES), F32)],
        ),
        input_output_aliases={6: 0, 7: 1} if before else {},
        compiler_params=params(),
        cost_estimate=cost(16 * count * rows * total * width, 15e6),
        name="attend",
    )(scal, q, qf, k, v, seg, *(before or ()))


def query_grads_kernel(at, count, scal, q, grad, k, v, seg, *rest):
    dq_out, kbuf, vbuf, sbuf, ksem, vsem, ssem = rest[-7:]
    i = pl.program_id(0)
    slot = i % 2
    rows, width = q.shape[1:]
    windowed(at, count, scal, ((k, kbuf, ksem), (v, vbuf, vsem), (seg, sbuf, ssem)), rows)

    def body(chunks, pair):
        size = chunks * rows
        q_pair, g_pair, features = q[0, :, lanes(pair)], grad[0, :, lanes(pair)], grad[0, :, width:]
        k_pair, v_pair = kbuf[slot, :size, lanes(pair)], vbuf[slot, :size, lanes(pair)]
        lane = 16 + 8 * pair
        for_scores, for_probs = [], []
        for which in range(2):
            own = lane + 4 * which
            kept = (lane_is(own, own + 1)) | (lane_is(0, 1, 2, 3))
            masked = jnp.where(kept, features, jnp.zeros_like(features))
            for_scores.append(jnp.concatenate([half(q_pair, which), masked], axis=1))
            masked = jnp.where(lane_is(own + 2, own + 3), features, jnp.zeros_like(features))
            for_probs.append(jnp.concatenate([half(g_pair, which), masked], axis=1))
        q_aug, g_aug = jnp.concatenate(for_scores, axis=0), jnp.concatenate(for_probs, axis=0)
        probs = jnp.exp(nt(q_aug, jnp.concatenate([k_pair, sbuf[slot, :size, :]], axis=1)))
        ones = jnp.ones((size, LANES), BF16)
        grad_probs = nt(g_aug, jnp.concatenate([v_pair, ones], axis=1))
        total = nn((probs * grad_probs).astype(BF16), k_pair)
        total = jnp.where(head_mask(0), total[:rows], total[rows:])
        dq_out[0, :, lanes(pair)] = (total * HD**-0.5).astype(BF16)

    by_chunks(scal[at + i, 1], width // LANES, body)


def query_grads_call(at, count, scal, q, k, v, msg, seg, before, skip=0):
    seqs, total, width = q.shape
    rows = msg.shape[1]
    return pl.pallas_call(
        functools.partial(query_grads_kernel, at, count),
        out_shape=jax.ShapeDtypeStruct((seqs, rows, width), BF16),
        grid_spec=pltpu.PrefetchScalarGridSpec(
            num_scalar_prefetch=1,
            grid=(count,),
            in_specs=[
                pl.BlockSpec((1, rows, width), lambda s, c: (at + s, 2, 0)),
                pl.BlockSpec((1, rows, width + LANES), lambda s, c: (skip + s, 0, 0)),
            ]
            + [ANY] * (3 if before is None else 4),
            out_specs=pl.BlockSpec((1, rows, width), lambda s, c: (at + s, 0, 0)),
            scratch_shapes=window_scratch(rows, (width, width, LANES)),
        ),
        input_output_aliases={} if before is None else {6: 0},
        compiler_params=params(),
        cost_estimate=cost(24 * count * rows * total * width, 5e6 * count),
        name="query_grads",
    )(scal, q, msg, k, v, seg, *(() if before is None else (before,)))


def key_grads_kernel(at, skip, count, scal, k, v, seg, q, g0, gl, gr, gll, grr, *rest):
    dk_out, dv_out, qbuf, qsem, grads, sems = rest[-6:]
    i = pl.program_id(0)
    slot = i % 2
    rows, width = k.shape[1:]

    def each(step, act):
        for place, ref in enumerate((gll, gl, g0, gr, grr)):

            @pl.when(needed(scal, at + step, place, rows))
            def _():
                target = grads.at[step % 2, pl.ds(place * rows, rows)]
                act(pltpu.make_async_copy(ref.at[step + skip], target, sems.at[step % 2, place]))

    @pl.when(i == 0)
    def _():
        each(i, lambda copy: copy.start())

    @pl.when(i + 1 < count)
    def _():
        each(i + 1, lambda copy: copy.start())

    windowed(at, count, scal, ((q, qbuf, qsem),), rows)
    each(i, lambda copy: copy.wait())
    begin = pl.multiple_of(scal[at + i, 0], ROWS)

    def body(chunks, pair):
        size = chunks * rows
        queries = pl.ds(begin, size)
        q_pair = qbuf[slot, :size, lanes(pair)]
        g_pair = grads[slot, queries, lanes(pair)]
        features = grads[slot, queries, width:]
        k_pair, v_pair = k[0, :, lanes(pair)], v[0, :, lanes(pair)]
        lane = 16 + 8 * pair
        for_scores, for_probs = [], []
        for which in range(2):
            own = lane + 4 * which
            kept = (lane_is(own, own + 1)) | (lane_is(0, 1, 2, 3))
            masked = jnp.where(kept, seg[0], jnp.zeros_like(seg[0]))
            for_scores.append(jnp.concatenate([half(k_pair, which), masked], axis=1))
            for_probs.append(
                jnp.concatenate([half(v_pair, which), ones_at(rows, own + 2, own + 3)], axis=1)
            )
        k_aug, v_aug = jnp.concatenate(for_scores, axis=0), jnp.concatenate(for_probs, axis=0)
        probs = jnp.exp(nt(k_aug, jnp.concatenate([q_pair, features], axis=1)))
        grad_probs = nt(v_aug, jnp.concatenate([g_pair, features], axis=1))
        grad_scores = (probs * grad_probs).astype(BF16)
        dv, dk = nn(probs.astype(BF16), g_pair), nn(grad_scores, q_pair)
        dk_out[0, :, lanes(pair)] = jnp.where(head_mask(0), dk[:rows], dk[rows:]).astype(BF16)
        dv_out[0, :, lanes(pair)] = jnp.where(head_mask(0), dv[:rows], dv[rows:]).astype(BF16)

    by_chunks(scal[at + i, 1], width // LANES, body)


def key_grads_call(at, count, scal, q, k, v, seg, msgs, before, skip=0):
    seqs, total, width = q.shape
    rows = msgs[0].shape[1]
    own = pl.BlockSpec((1, rows, width), lambda s, c: (at + s, 2, 0))
    out = pl.BlockSpec((1, rows, width), lambda s, c: (at + s, 0, 0))
    return pl.pallas_call(
        functools.partial(key_grads_kernel, at, skip, count),
        out_shape=(jax.ShapeDtypeStruct((seqs, rows, width), BF16),) * 2,
        grid_spec=pltpu.PrefetchScalarGridSpec(
            num_scalar_prefetch=1,
            grid=(count,),
            in_specs=[own, own, pl.BlockSpec((1, rows, LANES), lambda s, c: (at + s, 2, 0))]
            + [ANY] * (6 + (2 if before else 0)),
            out_specs=[out, out],
            scratch_shapes=window_scratch(rows, (width,))
            + [
                pltpu.VMEM((2, total, width + LANES), BF16),
                pltpu.SemaphoreType.DMA((2, 5)),
            ],
        ),
        input_output_aliases={10: 0, 11: 1} if before else {},
        compiler_params=params(),
        cost_estimate=cost(32 * count * rows * total * width, 6e6 * count),
        name="key_grads",
    )(scal, k, v, seg, q, *msgs, *(before or ()))


def middle_kernel(at, count, carried, pieces, scal, x, attn, grad, qf, vec, *rest):
    refs = rest[:pieces]
    outs = rest[pieces + (7 if carried else 0) :]
    out, hid, gpre, act2, branch, gmid, sums, msg = outs[:8]
    x_s, attn_s, grad_s, qf_s, wo, up_first, up_rest, down = outs[8:16]
    out_s, act2_s, branch_s, gmid_s, sums_s, msg_s = outs[16:22]
    hid_s, gpre_s = outs[22:26], outs[26:30]
    in_sems, w_sems, sems = outs[30:]
    parts, share, width = wo.shape
    rows = count * x.shape[1]
    group = pl.ds(at, count)
    second = second_pieces(refs)
    loads_out = piece_copies(scal, second, 0, share, wo, w_sems.at[0])
    loads_up = piece_copies(scal, second, share, share, up_first, w_sems.at[1])
    loads_rest = piece_copies(scal, second, 2 * share, 3 * share, up_rest, w_sems.at[3])
    loads_down = piece_copies(scal, second, 5 * share, 4 * share, down, w_sems.at[2])
    inputs = [
        pltpu.make_async_copy(ref.at[group], buf, in_sems.at[j])
        for j, (ref, buf) in enumerate(((attn, attn_s), (x, x_s), (grad, grad_s), (qf, qf_s)))
    ]
    start(inputs[:2])
    start(loads_out)
    start(inputs[2:])
    start(loads_up)
    start(loads_down)
    start(loads_rest)
    wait(inputs[:2])
    wait(loads_out)
    w_out = wo[...].reshape(width, width)
    attended = attn_s[...].reshape(rows, width)
    middle = x_s[...].reshape(rows, width).astype(F32) + nn(attended, w_out) + vec[4:5]
    unit, inverse = unit_of(middle)
    normed = (unit * vec[5:6] + vec[6:7]).astype(BF16)
    stores = []

    def store(j, value, buf, ref):
        buf[...] = value.reshape(buf.shape)
        stores.append(pltpu.make_async_copy(buf, ref, sems.at[j]))
        stores[-1].start()

    store(0, normed, act2_s, act2.at[group])
    wait(inputs[2:])
    g = grad_s[...].reshape(rows, width)
    g_full = g.astype(F32)
    result = middle + vec[7:8]
    grad_two = jnp.zeros((rows, width), F32)
    wait(loads_up)
    for c in range(4):
        w_up = up_first[...] if c == 0 else up_rest[:, (c - 1) * share : c * share, :]
        w_up = w_up.reshape(width, width)
        pre = nn(normed, w_up) + vec[8 + c : 9 + c]
        if c == 0:
            wait(loads_down)
            wait(loads_rest)
        if parts >= 4:
            step = parts // 4
            w_down = down[c * step : (c + 1) * step].reshape(width, width)
        else:
            w_down = down[0, c * width : (c + 1) * width]
        whole = 0.5 * (1.0 + lax.erf(pre * 0.7071067811865476))
        slope = whole + pre * jnp.exp(-0.5 * pre * pre) * 0.3989422804014327
        hidden = (pre * whole).astype(BF16)
        store(8 + c, hidden, hid_s[c], hid.at[group, c])
        result = result + nn(hidden, w_down)
        grad_pre = (nt(g, w_down) * slope).astype(BF16)
        store(12 + c, grad_pre, gpre_s[c], gpre.at[group, c])
        grad_two = grad_two + nt(grad_pre, w_up)
        sums_s[4 + c : 5 + c] = column_sum(grad_pre.astype(F32))
    store(1, result.astype(BF16), out_s, out.at[group])
    sums_s[0:1] = column_sum(grad_two * unit)
    sums_s[1:2] = column_sum(grad_two)
    grad_middle = g_full + norm_back(grad_two * vec[5:6], unit, inverse)
    store(2, grad_middle, gmid_s, gmid.at[group])
    grad_branch = grad_middle.astype(BF16)
    store(3, grad_branch, branch_s, branch.at[group])
    sums_s[2:3] = column_sum(grad_branch.astype(F32))
    sums_s[3:4] = column_sum(g_full)
    stores.append(pltpu.make_async_copy(sums_s, sums.at[1 if carried else 0], sems.at[4]))
    stores[-1].start()
    grad_attn = nt(grad_branch, w_out).astype(BF16)
    product = grad_attn.astype(F32) * attended.astype(F32)
    high = product.astype(BF16)
    low = (product - high.astype(F32)).astype(BF16)
    head = lax.broadcasted_iota(jnp.int32, (width, LANES), 0) // HD
    lane = lax.broadcasted_iota(jnp.int32, (width, LANES), 1) - 16 - 4 * head
    pick = jnp.where((lane == 2) | (lane == 3), 1.0, 0.0).astype(BF16)
    delta = nn(high, pick) + nn(low, pick)
    top = delta.astype(BF16).astype(F32)
    column = lax.broadcasted_iota(jnp.int32, (1, LANES), 1)
    in_heads = (column >= 16) & (column < 16 + 4 * (width // HD))
    features = jnp.where(
        in_heads & (column % 4 == 2),
        -top,
        jnp.where(
            in_heads & (column % 4 == 3),
            top - delta,
            qf_s[...].reshape(rows, LANES).astype(F32),
        ),
    )
    msg_s[:, :, :width] = grad_attn.reshape(count, rows // count, width)
    msg_s[:, :, width:] = features.astype(BF16).reshape(count, rows // count, LANES)
    stores.append(pltpu.make_async_copy(msg_s, msg, sems.at[5]))
    stores[-1].start()
    wait(stores)


def middle_call(at, count, scal, x, attn, grad, qf, second, vec, before):
    seqs, rows, width = x.shape
    parts = second[0].shape[0]
    share = width // parts
    flat = jax.ShapeDtypeStruct((seqs, rows, width), BF16)
    chunked = jax.ShapeDtypeStruct((seqs, 4, rows, width), BF16)
    outs = (
        flat,
        chunked,
        chunked,
        flat,
        flat,
        jax.ShapeDtypeStruct((seqs, rows, width), F32),
        jax.ShapeDtypeStruct((2, 8, width), F32),
    )
    base = 6 + len(second)
    return pl.pallas_call(
        functools.partial(middle_kernel, at, count, before is not None, len(second)),
        out_shape=outs + (jax.ShapeDtypeStruct((count, rows, width + LANES), BF16),),
        in_specs=[pl.BlockSpec(memory_space=pltpu.SMEM)]
        + [ANY] * 4
        + [VMEM]
        + [ANY] * (len(second) + (7 if before else 0)),
        out_specs=[ANY] * 8,
        scratch_shapes=[
            pltpu.VMEM((count, rows, width), BF16),
            pltpu.VMEM((count, rows, width), BF16),
            pltpu.VMEM((count, rows, width), BF16),
            pltpu.VMEM((count, rows, LANES), BF16),
            pltpu.VMEM((parts, share, width), BF16),
            pltpu.VMEM((parts, share, width), BF16),
            pltpu.VMEM((parts, 3 * share, width), BF16),
            pltpu.VMEM((parts, 4 * share, width), BF16),
            pltpu.VMEM((count, rows, width), BF16),
            pltpu.VMEM((count, rows, width), BF16),
            pltpu.VMEM((count, rows, width), BF16),
            pltpu.VMEM((count, rows, width), F32),
            pltpu.VMEM((8, width), F32),
            pltpu.VMEM((count, rows, width + LANES), BF16),
        ]
        + [pltpu.VMEM((count, rows, width), BF16)] * 8
        + [
            pltpu.SemaphoreType.DMA((4,)),
            pltpu.SemaphoreType.DMA((4, 8)),
            pltpu.SemaphoreType.DMA((16,)),
        ],
        input_output_aliases={base + j: j for j in range(7)} if before else {},
        compiler_params=pltpu.CompilerParams(vmem_limit_bytes=60 * MIB),
        cost_estimate=cost(36 * count * rows * width * width, 12e6 + 8e6 * count, 8 * count * rows * width),
        name="middle",
    )(scal, x, attn, grad, qf, vec, *second, *(before or ()))


def spread_copies(scal, source, row, keep, send, sems):
    share = source.shape[0] // 8
    copies = []
    for rel in range(8):
        x, y = bits(rel)
        ref = send if rel & 1 else keep
        block = source.at[pl.ds(pl.multiple_of((scal[0, 3] ^ rel) * share, 16), share)]
        copies.append(
            pltpu.make_async_copy(block, ref.at[2 * x + y, pl.ds(row, share)], sems.at[rel])
        )
    return copies


def ffn_grads_kernel(parts, scal, hid, gpre, act2, attn, branch, grad, *rest):
    outs, (one, two, sems_one, sems_two) = rest[:2], rest[-4:]
    i = pl.program_id(0)
    slot = i % 2
    count, rows, width = grad.shape
    tokens = count * rows
    share = width // parts

    def flat(ref):
        return ref[...].reshape(tokens, width)

    def copies_one(step):
        source = one.at[step % 2]
        if parts == 1:
            return [pltpu.make_async_copy(source, outs[0].at[pl.ds(step * width, width)], sems_one.at[step % 2, 0])]
        row = pl.multiple_of(step * share, 16)
        return spread_copies(scal, source, row, *outs, sems_one.at[step % 2])

    def copies_two(step):
        c = step - 1
        source = two.at[step % 2]
        if parts == 1:
            target = outs[1].at[pl.ds(c * width, width)]
            return [pltpu.make_async_copy(source, target, sems_two.at[step % 2, 0])]
        core, size = scal[0, 3] & 1, 4 * share
        where = c ^ (scal[0, 3] >> 1)
        where = 2 * (where & 1) + (where >> 1)
        return [
            pltpu.make_async_copy(
                source.at[pl.ds(pl.multiple_of(half_at * size, 16), size)],
                ref.at[where, pl.ds(5 * share, size)],
                sems_two.at[step % 2, j],
            )
            for j, (half_at, ref) in enumerate(((core, outs[0]), (1 - core, outs[1])))
        ]

    @pl.when(i >= 2)
    def _():
        wait(copies_one(i - 2))

    @pl.when(i >= 3)
    def _():
        wait(copies_two(i - 2))

    @pl.when(i == 0)
    def _():
        one[slot] = tn(flat(attn), flat(branch)).astype(BF16)

    @pl.when(i > 0)
    def _():
        one[slot] = tn(flat(act2), flat(gpre)).astype(BF16)
        two[slot] = tn(flat(hid), flat(grad)).astype(BF16)
        start(copies_two(i))

    start(copies_one(i))

    @pl.when(i == 4)
    def _():
        for step in (3, 4):
            wait(copies_one(step))
            wait(copies_two(step))


def ffn_grads_call(scal, parts, hid, gpre, act2, attn, branch, grad):
    count, rows, width = grad.shape
    share = width // parts
    chunk = pl.BlockSpec((count, 1, rows, width), lambda i: (0, jnp.maximum(i - 1, 0), 0, 0))
    if parts == 8:
        outs = (jax.ShapeDtypeStruct((4, 9 * share, width), BF16),) * 2
    else:
        outs = (
            jax.ShapeDtypeStruct((5 * width, width), BF16),
            jax.ShapeDtypeStruct((4 * width, width), BF16),
        )
    return pl.pallas_call(
        functools.partial(ffn_grads_kernel, parts),
        out_shape=outs,
        grid=(5,),
        in_specs=[pl.BlockSpec(memory_space=pltpu.SMEM), chunk, chunk]
        + [whole_spec(a) for a in (act2, attn, branch, grad)],
        out_specs=[ANY, ANY],
        scratch_shapes=[
            pltpu.VMEM((2, width, width), BF16),
            pltpu.VMEM((2, width, width), BF16),
            pltpu.SemaphoreType.DMA((2, 8)),
            pltpu.SemaphoreType.DMA((2, 2)),
        ],
        compiler_params=params(),
        cost_estimate=cost(18 * count * rows * width * width, 25e6),
        name="ffn_grads",
    )(scal, hid, gpre, act2, attn, branch, grad)


def last_kernel(parts, pieces, scal, vec, sums, x_in, gmid_in, dq_in, dk_in, dv_in, *rest):
    refs, rest = rest[:pieces], rest[pieces:]
    gin_out, outs = rest[0], rest[1:-13]
    weights, work, total, wsems, sems, x, gmid, dq, dk, dv, gin, in_sems, gin_sem = rest[-13:]
    count, rows, width = x.shape
    loads = [
        pltpu.make_async_copy(ref, buf, in_sems.at[j])
        for j, (ref, buf) in enumerate(
            ((x_in, x), (dq_in, dq), (dk_in, dk), (dv_in, dv), (gmid_in, gmid))
        )
    ]
    start(loads[:4])
    tokens = count * rows
    depth = weights.shape[1]
    share = width // parts
    copies = piece_copies(scal, first_pieces(refs), 0, depth, weights, wsems)
    start(copies)
    start(loads[4:])
    wait(loads[:1])
    unit, inverse = unit_of(x[...].reshape(tokens, width).astype(F32))
    act = (unit * vec[0:1] + vec[1:2]).astype(BF16)
    given, stores = [], []
    for j, ref in enumerate((dq, dk, dv)):
        wait(loads[1 + j : 2 + j])
        given.append(ref[...].reshape(tokens, width))
        work[j] = tn(act, given[j]).astype(BF16)
        if parts == 1:
            target = outs[0].at[pl.ds(j * width, width)]
            stores.append(pltpu.make_async_copy(work.at[j], target, sems.at[j, 0]))
            stores[-1].start()
        else:
            stores += spread_copies(scal, work.at[j], j * share, *outs, sems.at[j])
            start(stores[-8:])
    wait(copies)
    grad_one = jnp.zeros(unit.shape, F32)
    for j in range(3):
        weight = weights[:, j * share : (j + 1) * share, :].reshape(width, width)
        grad_one = grad_one + nt(given[j], weight)
    back = norm_back(grad_one * vec[0:1], unit, inverse)
    wait(loads[4:])
    gin[...] = (gmid[...].reshape(tokens, width) + back).astype(BF16).reshape(gin.shape)
    stores.append(pltpu.make_async_copy(gin, gin_out, gin_sem.at[0]))
    stores[-1].start()
    total[0:8] = (sums[0] + sums[1]).astype(BF16)
    total[8:32] = jnp.zeros((24, width), BF16)
    rows_now = [
        column_sum(grad_one * unit),
        column_sum(grad_one),
        column_sum(given[0].astype(F32)),
        column_sum(given[2].astype(F32)),
    ]
    for j, row in enumerate(rows_now):
        total[8 + j : 9 + j] = row.astype(BF16)
    if parts == 1:
        stores.append(
            pltpu.make_async_copy(total, outs[0].at[pl.ds(3 * width, 32)], sems.at[3, 0])
        )
        stores[-1].start()
    else:
        for rel in range(8):
            x_bit, y_bit = bits(rel)
            target = outs[rel & 1].at[2 * x_bit + y_bit, pl.ds(3 * share, 32)]
            stores.append(pltpu.make_async_copy(total, target, sems.at[3, rel]))
            stores[-1].start()
    wait(stores)


def last_call(scal, x, gmid, dq, dk, dv, vec, sums, first):
    parts, depth = (8, first[0].shape[1]) if len(first) > 1 else first[0].shape[:2]
    width = x.shape[2]
    share = width // parts
    gin = jax.ShapeDtypeStruct(x.shape, BF16)
    if parts == 1:
        outs = (jax.ShapeDtypeStruct((3 * width + 32, width), BF16),)
    else:
        outs = (jax.ShapeDtypeStruct((4, 3 * share + 32, width), BF16),) * 2
    return pl.pallas_call(
        functools.partial(last_kernel, parts, len(first)),
        out_shape=(gin, *outs),
        grid=(1,),
        in_specs=[pl.BlockSpec(memory_space=pltpu.SMEM), whole_spec(vec), whole_spec(sums)]
        + [ANY] * (5 + len(first)),
        out_specs=[ANY] * (1 + len(outs)),
        scratch_shapes=[
            pltpu.VMEM((parts, depth, width), BF16),
            pltpu.VMEM((3, width, width), BF16),
            pltpu.VMEM((32, width), BF16),
            pltpu.SemaphoreType.DMA((8,)),
            pltpu.SemaphoreType.DMA((4, 8)),
            pltpu.VMEM(x.shape, BF16),
            pltpu.VMEM(x.shape, F32),
            pltpu.VMEM(x.shape, BF16),
            pltpu.VMEM(x.shape, BF16),
            pltpu.VMEM(x.shape, BF16),
            pltpu.VMEM(x.shape, BF16),
            pltpu.SemaphoreType.DMA((5,)),
            pltpu.SemaphoreType.DMA((1,)),
        ],
        compiler_params=params(),
        cost_estimate=cost(12 * x.shape[0] * x.shape[1] * width * width, 20e6),
        name="last",
    )(scal, vec, sums, x, gmid, dq, dk, dv, *first)


def outer(ids):
    return (ids[0, 2] == 0) | (ids[0, 2] == 3)


def halves(ids, mine, got):
    swap = outer(ids)
    return jnp.where(swap, mine[...], got[...]).astype(F32), jnp.where(swap, got[...], mine[...]).astype(F32)


def finish_ffn_kernel(ids, mine, got, out_w, up_w, down_w, both):
    share, width = out_w.shape
    size = mine.shape[0]
    both[0:size], both[size:] = halves(ids, mine, got)
    out_w[...] = both[0:share]
    for c in range(4):
        up_w[:, c * width : (c + 1) * width] = both[(1 + c) * share : (2 + c) * share]
    down_w[...] = both[5 * share :]


def finish_ffn_call(ids, mine, got, share):
    width = mine.shape[1]
    outs = (
        jax.ShapeDtypeStruct((share, width), F32),
        jax.ShapeDtypeStruct((share, 4 * width), F32),
        jax.ShapeDtypeStruct((4 * share, width), F32),
    )
    return pl.pallas_call(
        finish_ffn_kernel,
        out_shape=outs,
        grid=(1,),
        in_specs=[pl.BlockSpec(memory_space=pltpu.SMEM), whole_spec(mine), whole_spec(got)],
        out_specs=[whole_spec(a) for a in outs],
        scratch_shapes=[pltpu.VMEM((2 * mine.shape[0], width), F32)],
        compiler_params=params(),
        cost_estimate=cost(0, 6e6),
        name="finish_ffn",
    )(ids, mine, got)


def finish_proj_kernel(ids, mine, got, q_w, k_w, v_w, *rest):
    *vectors, bias, both = rest
    share, width = q_w.shape
    size = mine.shape[0]
    both[0:size], both[size:] = halves(ids, mine, got)
    for j, out in enumerate((q_w, k_w, v_w)):
        out[...] = both[j * share : (j + 1) * share]
    me = ids[0, 3]
    row = lax.broadcasted_iota(jnp.int32, (width, LANES), 0)
    column = lax.broadcasted_iota(jnp.int32, (width, LANES), 1)
    pick = jnp.where(row == column + me * share, 1.0, 0.0).astype(BF16)
    picked = nn(both[3 * share : 3 * share + 16].astype(BF16), pick)
    for out, j in zip(vectors, (8, 9, 10, 11, 2, 0, 1, 3)):
        out[...] = picked[j : j + 1, 0:share]
    line = both[pl.ds(3 * share + 4 + me // 2, 1), :]
    bias[...] = jnp.where(me % 2 == 0, line[:, 0 : 4 * share], line[:, 4 * share :])


def finish_proj_call(ids, mine, got, share):
    width = mine.shape[1]
    outs = (
        [jax.ShapeDtypeStruct((share, width), F32)] * 3
        + [jax.ShapeDtypeStruct((1, share), F32)] * 8
        + [jax.ShapeDtypeStruct((1, 4 * share), F32)]
    )
    return pl.pallas_call(
        finish_proj_kernel,
        out_shape=outs,
        grid=(1,),
        in_specs=[pl.BlockSpec(memory_space=pltpu.SMEM), whole_spec(mine), whole_spec(got)],
        out_specs=[whole_spec(a) for a in outs],
        scratch_shapes=[pltpu.VMEM((2 * mine.shape[0], width), F32)],
        compiler_params=params(),
        cost_estimate=cost(0, 2e6),
        name="finish_proj",
    )(ids, mine, got)


RIGHT = [(0, 1), (1, 2), (2, 3)]
LEFT = [(1, 0), (2, 1), (3, 2)]
RIGHT_AGAIN = [(1, 2), (2, 3)]
LEFT_AGAIN = [(2, 1), (1, 0)]


def shifted(array, pairs):
    return lax.ppermute(array, "seq", pairs)


def crossed(array, distance):
    return lax.ppermute(array, "dp", [(i, i ^ distance) for i in range(8)])


def neighbours(array):
    left, right = shifted(array, RIGHT), shifted(array, LEFT)
    return left, right, shifted(left, RIGHT_AGAIN), shifted(right, LEFT_AGAIN)


def after(value, *others):
    return lax.optimization_barrier((value, *others))[0]


def add(*arrays):
    return sum(array.astype(F32) for array in arrays).astype(BF16)


PAIRS = [(0, 1), (1, 0), (2, 3), (3, 2)]
ACROSS = [(0, 3), (3, 0), (1, 2), (2, 1)]


class Reduction:
    def __init__(self, keep, send, place):
        self.keep, self.place, self.cut = keep, place, keep.shape[1] // 2
        self.got = crossed(send, 1)

    def second(self, *order):
        keep, got, cut = self.keep, after(self.got, *order), self.cut
        self.got = got
        one = add(keep[2:4, :cut], got[2:4, :cut])
        two = add(keep[1::2, cut:], got[1::2, cut:])
        self.more = crossed(one, 2), crossed(two, 4)
        return one, two

    def third(self, *order):
        keep, got, cut = self.keep, self.got, self.cut
        more = self.more = tuple(after(m, *order) for m in self.more)
        one = add(keep[1, :cut], got[1, :cut], more[0][1])
        two = add(keep[2, cut:], got[2, cut:], more[1][1])
        self.last = crossed(one, 4), crossed(two, 2)
        return one, two

    def fourth(self, *order):
        keep, got, cut = self.keep, self.got, self.cut
        last = tuple(after(m, *order) for m in self.last)
        one = add(keep[0, :cut], got[0, :cut], self.more[0][0], last[0])
        two = add(keep[0, cut:], got[0, cut:], self.more[1][0], last[1])
        return self.over_seq(one, two)

    def over_seq(self, one, two):
        outside = (self.place == 0) | (self.place == 3)
        self.mine = jnp.where(outside, one, two)
        other = jnp.where(outside, two, one)
        self.got = shifted(other, PAIRS)
        return self.mine, other

    def fifth(self, *order):
        self.mine = add(self.mine, after(self.got, *order))
        self.got = shifted(self.mine, ACROSS)
        return (self.mine,)

    def sixth(self, *order):
        self.mine = add(self.mine, after(self.got, *order))
        self.got = shifted(self.mine, PAIRS)
        return (self.mine,)

    def result(self):
        return self.mine, self.got


def windows(slots, place, me):
    seqs, _, rows = slots.shape
    whole = slots.reshape(seqs, 5 * rows)
    first, last = slots[:, 2, :1], slots[:, 2, -1:]
    low = jnp.sum((whole < first).astype(jnp.int32), axis=1)
    high = jnp.sum((whole <= last).astype(jnp.int32), axis=1)
    begin = (low // ROWS) * ROWS
    chunks = jnp.maximum((high - begin + rows - 1) // rows, 2)
    begin = jnp.minimum(begin, rows * (jnp.minimum(5, 6 - place) - chunks))
    other = jnp.zeros_like(begin)
    return jnp.stack([begin, chunks, other + place, other + me], axis=1)


def per_device(
    inputs,
    segment_ids,
    norm1_gain,
    norm1_shift,
    query_weight,
    query_bias,
    key_weight,
    value_weight,
    value_bias,
    out_weight,
    out_bias,
    norm2_gain,
    norm2_shift,
    fc1_weight,
    fc1_bias,
    fc2_weight,
    fc2_bias,
    grad_output,
):
    seqs, rows, width = inputs.shape
    devices = lax.axis_size("dp")
    share = query_weight.shape[0]
    place, me = lax.axis_index("seq"), lax.axis_index("dp")
    direct = devices == 8
    parts = 8 if direct else 1
    zero = jnp.zeros((), jnp.int32)
    ids = jnp.stack([zero, zero, place, me])[None]

    vectors = (
        norm1_gain, norm1_shift, query_bias, value_bias,
        out_bias, norm2_gain, norm2_shift, fc2_bias, fc1_bias,
    )
    tokens = tokens_call(inputs, segment_ids)
    query_bias = after(query_bias, tokens)
    vectors = vectors[:2] + (query_bias,) + vectors[3:]
    packed_one, packed_two = pack_call(
        (query_weight, key_weight, value_weight, out_weight, fc1_weight, fc2_weight), vectors
    )
    left, right = shifted(tokens, RIGHT), shifted(tokens, LEFT)
    if direct:
        near = jnp.stack(
            [after(packed_one, left, right)] + [crossed(packed_one, d) for d in (2, 4, 6)]
        )
        first = near, crossed(near, 1)
        vec = unpack_call(*first, ids)
        second = (lax.all_gather(after(packed_two, near), "dp", axis=0),)
    else:
        one = lax.all_gather(packed_one, "dp", axis=0)
        two = lax.all_gather(packed_two, "dp", axis=0)
        small = one[:, 3 * share :]
        vec = jnp.concatenate(
            [
                small[:, :8, :share].transpose(1, 0, 2).reshape(8, width),
                small[:, 8, : 4 * share].reshape(4, width),
                jnp.zeros((4, width), BF16),
            ]
        ).astype(F32)
        first = (
            jnp.concatenate(
                [one[:, j * share : (j + 1) * share].reshape(width, width) for j in range(3)]
                + [jnp.zeros((16, width), BF16)]
            )[None],
        )
        second = (
            jnp.concatenate(
                [two[:, j * share : (j + 1) * share].reshape(width, width) for j in range(5)]
                + [two[:, 5 * share :].reshape(4 * width, width)]
            )[None],
        )
    far_left, far_right = shifted(left, RIGHT_AGAIN), shifted(right, LEFT_AGAIN)

    qkv = project_call(ids, (inputs, left, right), vec, first, None, seqs, rows)
    far_left, far_right, *qkv = lax.optimization_barrier((far_left, far_right, *qkv))
    late_ids = after(segment_ids, qkv[0])

    def ids_of(message):
        return message[:, rows, :rows].astype(jnp.int32)

    before, beyond = jnp.full_like(late_ids, -1), jnp.full_like(late_ids, 99)
    slots = jnp.stack(
        [
            jnp.where(place >= 2, ids_of(far_left), before),
            jnp.where(place >= 1, ids_of(left), before),
            late_ids,
            jnp.where(place <= 2, ids_of(right), beyond),
            jnp.where(place <= 1, ids_of(far_right), beyond),
        ],
        axis=1,
    )
    scal = windows(slots, place, me)
    lane = lax.broadcasted_iota(jnp.int32, (1, 1, LANES), 2)
    seg = ((slots.reshape(seqs, 5 * rows)[:, :, None] == lane) | (lane >= 16)).astype(BF16)
    qf = jnp.where((lane < 4) & (lane != late_ids[:, :, None]), -BIG, 0.0).astype(BF16)
    qkv = list(project_call(scal, (far_left, far_right), vec, first, qkv, seqs, rows))

    attn, features = attend_call(0, seqs, scal, *qkv, seg, qf, None)

    split = ((0, 1), (1, seqs - 1))

    def middle(at, count, before):
        *shared, msg = middle_call(
            at, count, scal, inputs, attn, grad_output, features, second, vec, before
        )
        return shared, msg

    shared, msg_a = middle(*split[0], None)
    left_a, right_a = shifted(msg_a, RIGHT), shifted(msg_a, LEFT)
    far_a = shifted(msg_a, [(0, 2), (1, 3), (2, 0), (3, 1)])
    shared, msg_b = middle(*split[1], shared)
    left_a, right_a, far_a, msg_b = lax.optimization_barrier((left_a, right_a, far_a, msg_b))
    left_b, right_b = shifted(msg_b, RIGHT), shifted(msg_b, LEFT)
    out, hid, gpre, act2, branch, gmid, sums = shared
    ffn = ffn_grads_call(scal, parts, hid, gpre, act2, attn, branch, after(grad_output, msg_b))
    left_b, right_b, *ffn = lax.optimization_barrier((left_b, right_b, *ffn))
    all_a = msg_a, left_a, right_a, far_a, far_a
    far_left_b, far_right_b = shifted(left_b, RIGHT_AGAIN), shifted(right_b, LEFT_AGAIN)
    all_b = msg_b, left_b, right_b, far_left_b, far_right_b
    dq = query_grads_call(0, 1, scal, *qkv, msg_a, after(seg, ffn[0]), None)
    if direct:
        reduction = Reduction(*ffn, place)
        order = reduction.second(dq)
        dq = query_grads_call(1, 2, scal, *qkv, msg_b, after(seg, *order), dq)
        order = reduction.third(dq)
        dkv = key_grads_call(1, 1, scal, *qkv, after(seg, *order), all_b, None)
        order = reduction.fourth(dkv[0])
        dkv = key_grads_call(2, 1, scal, *qkv, after(seg, *order), all_b, tuple(dkv), 1)
        order = reduction.fifth(dkv[0])
        dkv = key_grads_call(0, 1, scal, *qkv, after(seg, *order), all_a, tuple(dkv))
        grad_inputs, *proj = last_call(
            scal, inputs, gmid, dq, *dkv, vec, sums, first
        )
        order = reduction.sixth(grad_inputs)
        tail = Reduction(proj[0], after(proj[1], *order), place)
        tail.second()
        tail.third()
        out_w, up_w, down_w = finish_ffn_call(ids, *reduction.result(), share)
        tail.fourth(out_w)
        tail.fifth()
        tail.sixth()
        q_w, k_w, v_w, *small, up_b = finish_proj_call(ids, *tail.result(), share)
        small = [s.reshape(share) for s in small]
        return (
            out, grad_inputs, small[0], small[1], q_w, small[2], k_w, v_w, small[3], out_w,
            small[4], small[5], small[6], up_w, up_b.reshape(4 * share), down_w, small[7],
        )

    dq = query_grads_call(1, 2, scal, *qkv, msg_b, seg, dq)
    dkv = key_grads_call(0, 1, scal, *qkv, seg, all_a, None)
    dkv = key_grads_call(1, seqs - 1, scal, *qkv, seg, all_b, tuple(dkv))
    grad_inputs, proj = last_call(scal, inputs, gmid, dq, *dkv, vec, sums, first)

    def reduced(array, count):
        cut = array.reshape(count, devices, -1, width).transpose(1, 0, 2, 3)
        cut = cut.reshape(devices, -1, width)
        part = lax.psum_scatter(cut, "dp", scatter_dimension=0, tiled=True)[0]
        return lax.psum(part, "seq").astype(F32)

    ffn_one, ffn_two = reduced(ffn[0], 5), reduced(ffn[1], 1)
    proj_w = reduced(proj[: 3 * width], 3)
    vectors = lax.psum(proj[3 * width : 3 * width + 16].astype(F32), ("dp", "seq"))
    mine = lax.dynamic_slice(vectors, (0, me * share), (16, share))
    up_grad = ffn_one[share:].reshape(4, share, width).transpose(1, 0, 2)
    up_bias = lax.dynamic_slice(vectors[4:8].reshape(4 * width), (me * 4 * share,), (4 * share,))
    return (
        out, grad_inputs, mine[8], mine[9], proj_w[:share], mine[10], proj_w[share : 2 * share],
        proj_w[2 * share :], mine[11], ffn_one[:share], mine[2], mine[0], mine[1],
        up_grad.reshape(share, 4 * width), up_bias, ffn_two, mine[3],
    )


def solution(mesh):
    token, matrix, vector = P("dp", "seq", None), P("dp", None), P("dp")
    return jax.shard_map(
        per_device,
        mesh=mesh,
        in_specs=(
            token, P("dp", "seq"), vector, vector, matrix, vector, matrix, matrix, vector,
            matrix, vector, vector, vector, matrix, vector, matrix, vector, token,
        ),
        out_specs=(
            token, token, vector, vector, matrix, vector, matrix, matrix, vector,
            matrix, vector, vector, vector, matrix, vector, matrix, vector,
        ),
        check_vma=False,
    )
```

```python
import functools

import jax
import jax.numpy as jnp
from jax import lax
from jax.experimental import pallas as pl
from jax.experimental.pallas import tpu as pltpu
from jax.sharding import PartitionSpec as P

F32 = jnp.float32
BF16 = jnp.bfloat16
HD = 64
LANES = 128
ROWS = 16
BIG = 1e30
EPSILON = 1e-05
MIB = 1 << 20

ANY = pl.BlockSpec(memory_space=pl.ANY)
VMEM = pl.BlockSpec(memory_space=pltpu.VMEM)


def nn(left, right):
    return lax.dot_general(left, right, (((1,), (0,)), ((), ())), preferred_element_type=F32)


def nt(left, right):
    return lax.dot_general(left, right, (((1,), (1,)), ((), ())), preferred_element_type=F32)


def tn(left, right):
    return lax.dot_general(left, right, (((0,), (0,)), ((), ())), preferred_element_type=F32)


def unit_of(values):
    center = values - jnp.mean(values, axis=-1, keepdims=True)
    inverse = lax.rsqrt(jnp.mean(center * center, axis=-1, keepdims=True) + EPSILON)
    return center * inverse, inverse


def norm_back(scaled, unit, inverse):
    return inverse * (
        scaled
        - jnp.mean(scaled, axis=-1, keepdims=True)
        - unit * jnp.mean(scaled * unit, axis=-1, keepdims=True)
    )


def column_sum(values):
    return jnp.sum(values, axis=0, keepdims=True)


def cost(flops, moved, transcendentals=0):
    return pl.CostEstimate(flops=int(flops / 4), bytes_accessed=int(moved / 4), transcendentals=0)


def params(limit=56, grid=1):
    return pltpu.CompilerParams(dimension_semantics=("arbitrary",) * grid, vmem_limit_bytes=limit * MIB)


def bits(rel):
    return (rel >> 1) & 1, (rel >> 2) & 1


def tokens_kernel(x, seg, tokens):
    count, rows, width = x.shape
    tokens[:, 0:rows] = x[...]
    tokens[:, rows:] = jnp.zeros((count, 16, width), BF16)
    for s in range(count):
        tokens[s, rows : rows + 1, 0:rows] = seg[s : s + 1].astype(F32).astype(BF16)


def tokens_call(x, seg):
    out = jax.ShapeDtypeStruct((x.shape[0], x.shape[1] + 16, x.shape[2]), BF16)
    return pl.pallas_call(
        tokens_kernel,
        out_shape=out,
        grid=(1,),
        in_specs=[whole_spec(x), whole_spec(seg)],
        out_specs=whole_spec(out),
        compiler_params=params(),
        cost_estimate=cost(0, 3e6),
        name="tokens",
    )(x, seg)


def pack_kernel(wq, wk, wv, wo, up, down, *rest):
    *vectors, first, second = rest
    share, width = wq.shape
    first[0:share] = wq[...]
    first[share : 2 * share] = wk[...]
    first[2 * share : 3 * share] = wv[...]
    first[3 * share :] = jnp.zeros((16, width), BF16)
    for j, vector in enumerate(vectors):
        size = vector.shape[1]
        first[3 * share + j : 3 * share + j + 1, 0:size] = vector[...]
    second[0:share] = wo[...]
    for c in range(4):
        second[(1 + c) * share : (2 + c) * share] = up[:, c * width : (c + 1) * width]
    second[5 * share :] = down[...]


def whole_spec(array):
    zeros = (0,) * len(array.shape)
    return pl.BlockSpec(array.shape, lambda i: zeros)


def pack_call(matrices, vectors):
    share, width = matrices[0].shape
    args = (*matrices, *[v.reshape(1, -1) for v in vectors])
    outs = (
        jax.ShapeDtypeStruct((3 * share + 16, width), BF16),
        jax.ShapeDtypeStruct((9 * share, width), BF16),
    )
    return pl.pallas_call(
        pack_kernel,
        out_shape=outs,
        grid=(1,),
        in_specs=[whole_spec(a) for a in args],
        out_specs=[whole_spec(a) for a in outs],
        compiler_params=params(),
        cost_estimate=cost(0, 6e6),
        name="pack",
    )(*args)


def piece_copies(scal, pieces, low, size, target, sems):
    if len(pieces) == 1:
        return [pltpu.make_async_copy(pieces[0][0].at[:, pl.ds(low, size)], target, sems.at[0])]
    me, copies = scal[0, 3], []
    for ref, index, rel, start, stop in pieces:
        if start <= low and low + size <= stop:
            source = ref if index is None else ref.at[index]
            copies.append(
                pltpu.make_async_copy(
                    source.at[pl.ds(low - start, size)], target.at[me ^ rel], sems.at[rel]
                )
            )
    return copies


def first_pieces(refs):
    if len(refs) == 1:
        return [(refs[0],)]
    near, far = refs
    return [(near, j, 2 * j, 0, near.shape[1]) for j in range(4)] + [
        (far, j, 2 * j + 1, 0, far.shape[1]) for j in range(4)
    ]


def second_pieces(refs):
    if len(refs) == 1:
        return [(refs[0],)]
    full = refs[0].shape[0]
    split = refs[3].shape[0]
    pieces = []
    for core in range(2):
        own, x, y, xy_low, xy_high = refs[5 * core : 5 * core + 5]
        pieces += [(own, None, core, 0, full), (x, None, 2 + core, 0, full), (y, None, 4 + core, 0, full)]
        pieces += [(xy_low, None, 6 + core, 0, split), (xy_high, None, 6 + core, split, full)]
    return pieces


def start(copies):
    for copy in copies:
        copy.start()


def wait(copies):
    for copy in copies:
        copy.wait()


def unpack_kernel(near, far, scal, vec):
    me = scal[0, 3]
    share = 96
    width = vec.shape[1]
    total = jnp.zeros((16, width), F32)
    row = lax.broadcasted_iota(jnp.int32, (LANES, width), 0)
    column = lax.broadcasted_iota(jnp.int32, (LANES, width), 1)
    for rel in range(8):
        device = me ^ rel
        block = (near if rel % 2 == 0 else far)[rel // 2]
        pick = jnp.where((row < share) & (column == row + device * share), 1.0, 0.0).astype(BF16)
        total = total + nn(block[:, 0:LANES], pick)
        bias = block[8:9, 0 : 4 * share].astype(F32)
        vec[pl.ds(8 + device // 2, 1), pl.ds(pl.multiple_of((device % 2) * 4 * share, LANES), 4 * share)] = bias
    vec[0:8] = total[0:8]
    vec[12:16] = jnp.zeros((4, width), F32)


def unpack_call(near, far, ids):
    width = near.shape[2]
    out = jax.ShapeDtypeStruct((16, width), F32)
    tail = pl.BlockSpec((4, 16, width), lambda i: (0, near.shape[1] // 16 - 1, 0))
    return pl.pallas_call(
        unpack_kernel,
        out_shape=out,
        grid=(1,),
        in_specs=[tail, tail, pl.BlockSpec(memory_space=pltpu.SMEM)],
        out_specs=whole_spec(out),
        compiler_params=params(),
        cost_estimate=cost(1e6, 4e6),
        name="unpack",
    )(near, far, ids)


def needed(scal, seq, slot, rows):
    low, high = scal[seq, 0], scal[seq, 0] + scal[seq, 1] * rows
    return (slot * rows < high) & ((slot + 1) * rows > low)


def project_kernel(far, pieces, scal, vec, *rest):
    sources = rest[: 2 if far else 3]
    rest = rest[len(sources) :]
    refs, (*outs, buf, weights, made, sems, wsems, out_sems) = rest[:pieces], rest[-9:]
    i = pl.program_id(0)
    steps = 1 if far else 3
    count, rows, width = buf.shape[1:]
    share = width // weights.shape[0]
    after = scal[0, 2] >= 2
    copies = piece_copies(scal, first_pieces(refs), 0, weights.shape[1], weights, wsems)
    if far:
        slot = jnp.where(after, 0, 4)
        used = needed(scal, 0, slot, rows)
        for s in range(1, count):
            used = used | needed(scal, s, slot, rows)
    else:
        slot = jnp.where(i == 0, 2, jnp.where(i == 1, 1, 3))
        used = True

    def load(step, act):
        for j, ref in enumerate(sources):
            when = (after == (j == 0)) if far else (step == j)

            @pl.when(when)
            def _():
                source = ref.at[:, pl.ds(0, rows)]
                act(pltpu.make_async_copy(source, buf.at[step % 2], sems.at[step % 2]))

    def stores(step, where):
        return [
            pltpu.make_async_copy(
                made.at[step % 2, t], outs[t].at[:, pl.ds(where * rows, rows)], out_sems.at[step % 2, t]
            )
            for t in range(3)
        ]

    @pl.when(i == 0)
    def _():
        load(0, lambda copy: copy.start())
        start(copies)

    @pl.when(i + 1 < steps)
    def _():
        load(i + 1, lambda copy: copy.start())

    load(i, lambda copy: copy.wait())

    @pl.when(i == 0)
    def _():
        wait(copies)

    @pl.when(i >= 2)
    def _():
        wait(stores(i, 0))

    def work():
        unit, _ = unit_of(buf[i % 2].reshape(count * rows, width).astype(F32))
        act = (unit * vec[0:1] + vec[1:2]).astype(BF16)
        for t in range(3):
            weight = weights[:, t * share : (t + 1) * share, :].reshape(width, width)
            result = nn(act, weight)
            if t == 0:
                result = (result + vec[2:3]).astype(BF16) * jnp.asarray(HD**-0.5, BF16)
            if t == 2:
                result = result + vec[3:4]
            made[i % 2, t] = result.astype(BF16).reshape(count, rows, width)
        start(stores(i, slot))

    if far:

        @pl.when(used)
        def _():
            work()
            wait(stores(0, 0))
    else:
        work()

        @pl.when(i == steps - 1)
        def _():
            wait(stores(i, 0))
            wait(stores(i - 1, 0))


def project_call(scal, sources, vec, first, before, seqs, rows):
    far = before is not None
    width = vec.shape[1]
    out = jax.ShapeDtypeStruct((seqs, 5 * rows, width), BF16)
    parts, depth = (8, first[0].shape[1]) if len(first) > 1 else first[0].shape[:2]
    steps = 1 if far else 3
    at = 2 + len(sources) + len(first)
    return pl.pallas_call(
        functools.partial(project_kernel, far, len(first)),
        out_shape=(out, out, out),
        grid=(steps,),
        in_specs=[pl.BlockSpec(memory_space=pltpu.SMEM), whole_spec(vec)]
        + [ANY] * (len(sources) + len(first) + (3 if far else 0)),
        out_specs=[ANY] * 3,
        scratch_shapes=[
            pltpu.VMEM((2, seqs, rows, width), BF16),
            pltpu.VMEM((parts, depth, width), BF16),
            pltpu.VMEM((2, 3, seqs, rows, width), BF16),
            pltpu.SemaphoreType.DMA((2,)),
            pltpu.SemaphoreType.DMA((8,)),
            pltpu.SemaphoreType.DMA((2, 3)),
        ],
        input_output_aliases={at: 0, at + 1: 1, at + 2: 2} if far else {},
        compiler_params=params(),
        cost_estimate=cost(6 * steps * seqs * rows * width * width, 8e6 * steps),
        name="far" if far else "near",
    )(scal, vec, *sources, *first, *(before or ()))


def lane_is(*wanted):
    lane = lax.broadcasted_iota(jnp.int32, (1, LANES), 1)
    hit = lane == wanted[0]
    for other in wanted[1:]:
        hit = hit | (lane == other)
    return hit


def head_mask(which):
    lane = lax.broadcasted_iota(jnp.int32, (1, LANES), 1)
    return (lane < HD) if which == 0 else (lane >= HD)


def half(pair, which):
    return jnp.where(head_mask(which), pair, jnp.zeros_like(pair))


def ones_at(rows, *wanted):
    return jnp.broadcast_to(jnp.where(lane_is(*wanted), 1.0, 0.0).astype(BF16), (rows, LANES))


def lanes(pair):
    return pl.ds(pl.multiple_of(pair * LANES, LANES), LANES)


def windowed(at, count, scal, arrays, rows):
    i = pl.program_id(0)

    def each(step, act):
        for c in range(4):

            @pl.when(c < scal[at + step, 1])
            def _():
                begin = pl.multiple_of(scal[at + step, 0] + c * rows, ROWS)
                for ref, buf, sems in arrays:
                    source = ref.at[at + step, pl.ds(begin, rows)]
                    target = buf.at[step % 2, pl.ds(c * rows, rows)]
                    act(pltpu.make_async_copy(source, target, sems.at[step % 2, c]))

    @pl.when(i == 0)
    def _():
        each(i, lambda copy: copy.start())

    @pl.when(i + 1 < count)
    def _():
        each(i + 1, lambda copy: copy.start())

    each(i, lambda copy: copy.wait())


def by_chunks(chunks, pairs, body):
    for c in range(2, 5):

        @pl.when(chunks == c)
        def _():
            lax.fori_loop(0, pairs, lambda p, _: body(c, p), None, unroll=2)


def window_scratch(rows, widths):
    return [pltpu.VMEM((2, 4 * rows, w), BF16) for w in widths] + [
        pltpu.SemaphoreType.DMA((2, 4)) for _ in widths
    ]


def attend_kernel(at, count, scal, q, qf, k, v, seg, *rest):
    o_out, qf_out, kbuf, vbuf, sbuf, ksem, vsem, ssem, feats = rest[-9:]
    i = pl.program_id(0)
    slot = i % 2
    rows, width = q.shape[1:]
    windowed(at, count, scal, ((k, kbuf, ksem), (v, vbuf, vsem), (seg, sbuf, ssem)), rows)
    feats[...] = qf[0].astype(F32)

    def body(chunks, pair):
        size = chunks * rows
        q_pair, features = q[0, :, lanes(pair)], qf[0]
        q_aug = jnp.concatenate(
            [
                jnp.concatenate([half(q_pair, 0), half(q_pair, 1)], axis=0),
                jnp.concatenate([features, features], axis=0),
            ],
            axis=1,
        )
        k_aug = jnp.concatenate([kbuf[slot, :size, lanes(pair)], sbuf[slot, :size, :]], axis=1)
        v_aug = jnp.concatenate(
            [vbuf[slot, :size, lanes(pair)], jnp.ones((size, LANES), BF16)], axis=1
        )
        scores = nt(q_aug, k_aug)
        highest = jnp.max(scores, axis=-1, keepdims=True)
        both = nn(jnp.exp(scores - highest).astype(BF16), v_aug)
        totals = both[:, LANES:]
        result = both[:, :LANES] / totals
        o_out[0, :, lanes(pair)] = jnp.where(head_mask(0), result[:rows], result[rows:]).astype(BF16)
        lse = highest + jnp.log(totals)
        top = lse.astype(BF16).astype(F32)
        rest_of = top - lse
        lane = 16 + 8 * pair
        new = jnp.where(lane_is(lane), -top[:rows], feats[...])
        new = jnp.where(lane_is(lane + 1), rest_of[:rows], new)
        new = jnp.where(lane_is(lane + 4), -top[rows:], new)
        feats[...] = jnp.where(lane_is(lane + 5), rest_of[rows:], new)

    by_chunks(scal[at + i, 1], width // LANES, body)
    qf_out[0] = feats[...].astype(BF16)


def attend_call(at, count, scal, q, k, v, seg, qf, before):
    seqs, total, width = q.shape
    rows = qf.shape[1]
    flat = pl.BlockSpec((1, rows, width), lambda s, c: (at + s, 0, 0))
    narrow = pl.BlockSpec((1, rows, LANES), lambda s, c: (at + s, 0, 0))
    return pl.pallas_call(
        functools.partial(attend_kernel, at, count),
        out_shape=(
            jax.ShapeDtypeStruct((seqs, rows, width), BF16),
            jax.ShapeDtypeStruct((seqs, rows, LANES), BF16),
        ),
        grid_spec=pltpu.PrefetchScalarGridSpec(
            num_scalar_prefetch=1,
            grid=(count,),
            in_specs=[pl.BlockSpec((1, rows, width), lambda s, c: (at + s, 2, 0)), narrow]
            + [ANY] * (5 if before else 3),
            out_specs=[flat, narrow],
            scratch_shapes=window_scratch(rows, (width, width, LANES))
            + [pltpu.VMEM((rows, LANES), F32)],
        ),
        input_output_aliases={6: 0, 7: 1} if before else {},
        compiler_params=params(),
        cost_estimate=cost(16 * count * rows * total * width, 15e6),
        name="attend",
    )(scal, q, qf, k, v, seg, *(before or ()))


def query_grads_kernel(at, count, scal, q, grad, k, v, seg, *rest):
    dq_out, kbuf, vbuf, sbuf, ksem, vsem, ssem = rest[-7:]
    i = pl.program_id(0)
    slot = i % 2
    rows, width = q.shape[1:]
    windowed(at, count, scal, ((k, kbuf, ksem), (v, vbuf, vsem), (seg, sbuf, ssem)), rows)

    def body(chunks, pair):
        size = chunks * rows
        q_pair, g_pair, features = q[0, :, lanes(pair)], grad[0, :, lanes(pair)], grad[0, :, width:]
        k_pair, v_pair = kbuf[slot, :size, lanes(pair)], vbuf[slot, :size, lanes(pair)]
        lane = 16 + 8 * pair
        for_scores, for_probs = [], []
        for which in range(2):
            own = lane + 4 * which
            kept = (lane_is(own, own + 1)) | (lane_is(0, 1, 2, 3))
            masked = jnp.where(kept, features, jnp.zeros_like(features))
            for_scores.append(jnp.concatenate([half(q_pair, which), masked], axis=1))
            masked = jnp.where(lane_is(own + 2, own + 3), features, jnp.zeros_like(features))
            for_probs.append(jnp.concatenate([half(g_pair, which), masked], axis=1))
        q_aug, g_aug = jnp.concatenate(for_scores, axis=0), jnp.concatenate(for_probs, axis=0)
        probs = jnp.exp(nt(q_aug, jnp.concatenate([k_pair, sbuf[slot, :size, :]], axis=1)))
        ones = jnp.ones((size, LANES), BF16)
        grad_probs = nt(g_aug, jnp.concatenate([v_pair, ones], axis=1))
        total = nn((probs * grad_probs).astype(BF16), k_pair)
        total = jnp.where(head_mask(0), total[:rows], total[rows:])
        dq_out[0, :, lanes(pair)] = (total * HD**-0.5).astype(BF16)

    by_chunks(scal[at + i, 1], width // LANES, body)


def query_grads_call(at, count, scal, q, k, v, msg, seg, before, skip=0):
    seqs, total, width = q.shape
    rows = msg.shape[1]
    return pl.pallas_call(
        functools.partial(query_grads_kernel, at, count),
        out_shape=jax.ShapeDtypeStruct((seqs, rows, width), BF16),
        grid_spec=pltpu.PrefetchScalarGridSpec(
            num_scalar_prefetch=1,
            grid=(count,),
            in_specs=[
                pl.BlockSpec((1, rows, width), lambda s, c: (at + s, 2, 0)),
                pl.BlockSpec((1, rows, width + LANES), lambda s, c: (skip + s, 0, 0)),
            ]
            + [ANY] * (3 if before is None else 4),
            out_specs=pl.BlockSpec((1, rows, width), lambda s, c: (at + s, 0, 0)),
            scratch_shapes=window_scratch(rows, (width, width, LANES)),
        ),
        input_output_aliases={} if before is None else {6: 0},
        compiler_params=params(),
        cost_estimate=cost(24 * count * rows * total * width, 5e6 * count),
        name="query_grads",
    )(scal, q, msg, k, v, seg, *(() if before is None else (before,)))


def key_grads_kernel(at, skip, count, scal, k, v, seg, q, g0, gl, gr, gll, grr, *rest):
    dk_out, dv_out, qbuf, qsem, grads, sems = rest[-6:]
    i = pl.program_id(0)
    slot = i % 2
    rows, width = k.shape[1:]

    def each(step, act):
        for place, ref in enumerate((gll, gl, g0, gr, grr)):

            @pl.when(needed(scal, at + step, place, rows))
            def _():
                target = grads.at[step % 2, pl.ds(place * rows, rows)]
                act(pltpu.make_async_copy(ref.at[step + skip], target, sems.at[step % 2, place]))

    @pl.when(i == 0)
    def _():
        each(i, lambda copy: copy.start())

    @pl.when(i + 1 < count)
    def _():
        each(i + 1, lambda copy: copy.start())

    windowed(at, count, scal, ((q, qbuf, qsem),), rows)
    each(i, lambda copy: copy.wait())
    begin = pl.multiple_of(scal[at + i, 0], ROWS)

    def body(chunks, pair):
        size = chunks * rows
        queries = pl.ds(begin, size)
        q_pair = qbuf[slot, :size, lanes(pair)]
        g_pair = grads[slot, queries, lanes(pair)]
        features = grads[slot, queries, width:]
        k_pair, v_pair = k[0, :, lanes(pair)], v[0, :, lanes(pair)]
        lane = 16 + 8 * pair
        for_scores, for_probs = [], []
        for which in range(2):
            own = lane + 4 * which
            kept = (lane_is(own, own + 1)) | (lane_is(0, 1, 2, 3))
            masked = jnp.where(kept, seg[0], jnp.zeros_like(seg[0]))
            for_scores.append(jnp.concatenate([half(k_pair, which), masked], axis=1))
            for_probs.append(
                jnp.concatenate([half(v_pair, which), ones_at(rows, own + 2, own + 3)], axis=1)
            )
        k_aug, v_aug = jnp.concatenate(for_scores, axis=0), jnp.concatenate(for_probs, axis=0)
        probs = jnp.exp(nt(k_aug, jnp.concatenate([q_pair, features], axis=1)))
        grad_probs = nt(v_aug, jnp.concatenate([g_pair, features], axis=1))
        grad_scores = (probs * grad_probs).astype(BF16)
        dv, dk = nn(probs.astype(BF16), g_pair), nn(grad_scores, q_pair)
        dk_out[0, :, lanes(pair)] = jnp.where(head_mask(0), dk[:rows], dk[rows:]).astype(BF16)
        dv_out[0, :, lanes(pair)] = jnp.where(head_mask(0), dv[:rows], dv[rows:]).astype(BF16)

    by_chunks(scal[at + i, 1], width // LANES, body)


def key_grads_call(at, count, scal, q, k, v, seg, msgs, before, skip=0):
    seqs, total, width = q.shape
    rows = msgs[0].shape[1]
    own = pl.BlockSpec((1, rows, width), lambda s, c: (at + s, 2, 0))
    out = pl.BlockSpec((1, rows, width), lambda s, c: (at + s, 0, 0))
    return pl.pallas_call(
        functools.partial(key_grads_kernel, at, skip, count),
        out_shape=(jax.ShapeDtypeStruct((seqs, rows, width), BF16),) * 2,
        grid_spec=pltpu.PrefetchScalarGridSpec(
            num_scalar_prefetch=1,
            grid=(count,),
            in_specs=[own, own, pl.BlockSpec((1, rows, LANES), lambda s, c: (at + s, 2, 0))]
            + [ANY] * (6 + (2 if before else 0)),
            out_specs=[out, out],
            scratch_shapes=window_scratch(rows, (width,))
            + [
                pltpu.VMEM((2, total, width + LANES), BF16),
                pltpu.SemaphoreType.DMA((2, 5)),
            ],
        ),
        input_output_aliases={10: 0, 11: 1} if before else {},
        compiler_params=params(),
        cost_estimate=cost(32 * count * rows * total * width, 6e6 * count),
        name="key_grads",
    )(scal, k, v, seg, q, *msgs, *(before or ()))


def middle_kernel(at, count, carried, pieces, scal, x, attn, grad, qf, vec, *rest):
    refs = rest[:pieces]
    outs = rest[pieces + (7 if carried else 0) :]
    out, hid, gpre, act2, branch, gmid, sums, msg = outs[:8]
    x_s, attn_s, grad_s, qf_s, wo, up_first, up_rest, down = outs[8:16]
    out_s, act2_s, branch_s, gmid_s, sums_s, msg_s = outs[16:22]
    hid_s, gpre_s = outs[22:26], outs[26:30]
    in_sems, w_sems, sems = outs[30:]
    parts, share, width = wo.shape
    rows = count * x.shape[1]
    group = pl.ds(at, count)
    second = second_pieces(refs)
    loads_out = piece_copies(scal, second, 0, share, wo, w_sems.at[0])
    loads_up = piece_copies(scal, second, share, share, up_first, w_sems.at[1])
    loads_rest = piece_copies(scal, second, 2 * share, 3 * share, up_rest, w_sems.at[3])
    loads_down = piece_copies(scal, second, 5 * share, 4 * share, down, w_sems.at[2])
    inputs = [
        pltpu.make_async_copy(ref.at[group], buf, in_sems.at[j])
        for j, (ref, buf) in enumerate(((attn, attn_s), (x, x_s), (grad, grad_s), (qf, qf_s)))
    ]
    start(inputs[:2])
    start(loads_out)
    start(inputs[2:])
    start(loads_up)
    start(loads_down)
    start(loads_rest)
    wait(inputs[:2])
    wait(loads_out)
    w_out = wo[...].reshape(width, width)
    attended = attn_s[...].reshape(rows, width)
    middle = x_s[...].reshape(rows, width).astype(F32) + nn(attended, w_out) + vec[4:5]
    unit, inverse = unit_of(middle)
    normed = (unit * vec[5:6] + vec[6:7]).astype(BF16)
    stores = []

    def store(j, value, buf, ref):
        buf[...] = value.reshape(buf.shape)
        stores.append(pltpu.make_async_copy(buf, ref, sems.at[j]))
        stores[-1].start()

    store(0, normed, act2_s, act2.at[group])
    wait(inputs[2:])
    g = grad_s[...].reshape(rows, width)
    g_full = g.astype(F32)
    result = middle + vec[7:8]
    grad_two = jnp.zeros((rows, width), F32)
    wait(loads_up)
    for c in range(4):
        w_up = up_first[...] if c == 0 else up_rest[:, (c - 1) * share : c * share, :]
        w_up = w_up.reshape(width, width)
        pre = nn(normed, w_up) + vec[8 + c : 9 + c]
        if c == 0:
            wait(loads_down)
            wait(loads_rest)
        if parts >= 4:
            step = parts // 4
            w_down = down[c * step : (c + 1) * step].reshape(width, width)
        else:
            w_down = down[0, c * width : (c + 1) * width]
        whole = 0.5 * (1.0 + lax.erf(pre * 0.7071067811865476))
        slope = whole + pre * jnp.exp(-0.5 * pre * pre) * 0.3989422804014327
        hidden = (pre * whole).astype(BF16)
        store(8 + c, hidden, hid_s[c], hid.at[group, c])
        result = result + nn(hidden, w_down)
        grad_pre = (nt(g, w_down) * slope).astype(BF16)
        store(12 + c, grad_pre, gpre_s[c], gpre.at[group, c])
        grad_two = grad_two + nt(grad_pre, w_up)
        sums_s[4 + c : 5 + c] = column_sum(grad_pre.astype(F32))
    store(1, result.astype(BF16), out_s, out.at[group])
    sums_s[0:1] = column_sum(grad_two * unit)
    sums_s[1:2] = column_sum(grad_two)
    grad_middle = g_full + norm_back(grad_two * vec[5:6], unit, inverse)
    store(2, grad_middle, gmid_s, gmid.at[group])
    grad_branch = grad_middle.astype(BF16)
    store(3, grad_branch, branch_s, branch.at[group])
    sums_s[2:3] = column_sum(grad_branch.astype(F32))
    sums_s[3:4] = column_sum(g_full)
    stores.append(pltpu.make_async_copy(sums_s, sums.at[1 if carried else 0], sems.at[4]))
    stores[-1].start()
    grad_attn = nt(grad_branch, w_out).astype(BF16)
    product = grad_attn.astype(F32) * attended.astype(F32)
    high = product.astype(BF16)
    low = (product - high.astype(F32)).astype(BF16)
    head = lax.broadcasted_iota(jnp.int32, (width, LANES), 0) // HD
    lane = lax.broadcasted_iota(jnp.int32, (width, LANES), 1) - 16 - 4 * head
    pick = jnp.where((lane == 2) | (lane == 3), 1.0, 0.0).astype(BF16)
    delta = nn(high, pick) + nn(low, pick)
    top = delta.astype(BF16).astype(F32)
    column = lax.broadcasted_iota(jnp.int32, (1, LANES), 1)
    in_heads = (column >= 16) & (column < 16 + 4 * (width // HD))
    features = jnp.where(
        in_heads & (column % 4 == 2),
        -top,
        jnp.where(
            in_heads & (column % 4 == 3),
            top - delta,
            qf_s[...].reshape(rows, LANES).astype(F32),
        ),
    )
    msg_s[:, :, :width] = grad_attn.reshape(count, rows // count, width)
    msg_s[:, :, width:] = features.astype(BF16).reshape(count, rows // count, LANES)
    stores.append(pltpu.make_async_copy(msg_s, msg, sems.at[5]))
    stores[-1].start()
    wait(stores)


def middle_call(at, count, scal, x, attn, grad, qf, second, vec, before):
    seqs, rows, width = x.shape
    parts = second[0].shape[0]
    share = width // parts
    flat = jax.ShapeDtypeStruct((seqs, rows, width), BF16)
    chunked = jax.ShapeDtypeStruct((seqs, 4, rows, width), BF16)
    outs = (
        flat,
        chunked,
        chunked,
        flat,
        flat,
        jax.ShapeDtypeStruct((seqs, rows, width), F32),
        jax.ShapeDtypeStruct((2, 8, width), F32),
    )
    base = 6 + len(second)
    return pl.pallas_call(
        functools.partial(middle_kernel, at, count, before is not None, len(second)),
        out_shape=outs + (jax.ShapeDtypeStruct((count, rows, width + LANES), BF16),),
        in_specs=[pl.BlockSpec(memory_space=pltpu.SMEM)]
        + [ANY] * 4
        + [VMEM]
        + [ANY] * (len(second) + (7 if before else 0)),
        out_specs=[ANY] * 8,
        scratch_shapes=[
            pltpu.VMEM((count, rows, width), BF16),
            pltpu.VMEM((count, rows, width), BF16),
            pltpu.VMEM((count, rows, width), BF16),
            pltpu.VMEM((count, rows, LANES), BF16),
            pltpu.VMEM((parts, share, width), BF16),
            pltpu.VMEM((parts, share, width), BF16),
            pltpu.VMEM((parts, 3 * share, width), BF16),
            pltpu.VMEM((parts, 4 * share, width), BF16),
            pltpu.VMEM((count, rows, width), BF16),
            pltpu.VMEM((count, rows, width), BF16),
            pltpu.VMEM((count, rows, width), BF16),
            pltpu.VMEM((count, rows, width), F32),
            pltpu.VMEM((8, width), F32),
            pltpu.VMEM((count, rows, width + LANES), BF16),
        ]
        + [pltpu.VMEM((count, rows, width), BF16)] * 8
        + [
            pltpu.SemaphoreType.DMA((4,)),
            pltpu.SemaphoreType.DMA((4, 8)),
            pltpu.SemaphoreType.DMA((16,)),
        ],
        input_output_aliases={base + j: j for j in range(7)} if before else {},
        compiler_params=pltpu.CompilerParams(vmem_limit_bytes=60 * MIB),
        cost_estimate=cost(36 * count * rows * width * width, 12e6 + 8e6 * count, 8 * count * rows * width),
        name="middle",
    )(scal, x, attn, grad, qf, vec, *second, *(before or ()))


def spread_copies(scal, source, row, keep, send, sems):
    share = source.shape[0] // 8
    copies = []
    for rel in range(8):
        x, y = bits(rel)
        ref = send if rel & 1 else keep
        block = source.at[pl.ds(pl.multiple_of((scal[0, 3] ^ rel) * share, 16), share)]
        copies.append(
            pltpu.make_async_copy(block, ref.at[2 * x + y, pl.ds(row, share)], sems.at[rel])
        )
    return copies


def ffn_grads_kernel(parts, scal, hid, gpre, act2, attn, branch, grad, *rest):
    outs, (one, two, sems_one, sems_two) = rest[:2], rest[-4:]
    i = pl.program_id(0)
    slot = i % 2
    count, rows, width = grad.shape
    tokens = count * rows
    share = width // parts

    def flat(ref):
        return ref[...].reshape(tokens, width)

    def copies_one(step):
        source = one.at[step % 2]
        if parts == 1:
            return [pltpu.make_async_copy(source, outs[0].at[pl.ds(step * width, width)], sems_one.at[step % 2, 0])]
        row = pl.multiple_of(step * share, 16)
        return spread_copies(scal, source, row, *outs, sems_one.at[step % 2])

    def copies_two(step):
        c = step - 1
        source = two.at[step % 2]
        if parts == 1:
            target = outs[1].at[pl.ds(c * width, width)]
            return [pltpu.make_async_copy(source, target, sems_two.at[step % 2, 0])]
        core, size = scal[0, 3] & 1, 4 * share
        where = c ^ (scal[0, 3] >> 1)
        where = 2 * (where & 1) + (where >> 1)
        return [
            pltpu.make_async_copy(
                source.at[pl.ds(pl.multiple_of(half_at * size, 16), size)],
                ref.at[where, pl.ds(5 * share, size)],
                sems_two.at[step % 2, j],
            )
            for j, (half_at, ref) in enumerate(((core, outs[0]), (1 - core, outs[1])))
        ]

    @pl.when(i >= 2)
    def _():
        wait(copies_one(i - 2))

    @pl.when(i >= 3)
    def _():
        wait(copies_two(i - 2))

    @pl.when(i == 0)
    def _():
        one[slot] = tn(flat(attn), flat(branch)).astype(BF16)

    @pl.when(i > 0)
    def _():
        one[slot] = tn(flat(act2), flat(gpre)).astype(BF16)
        two[slot] = tn(flat(hid), flat(grad)).astype(BF16)
        start(copies_two(i))

    start(copies_one(i))

    @pl.when(i == 4)
    def _():
        for step in (3, 4):
            wait(copies_one(step))
            wait(copies_two(step))


def ffn_grads_call(scal, parts, hid, gpre, act2, attn, branch, grad):
    count, rows, width = grad.shape
    share = width // parts
    chunk = pl.BlockSpec((count, 1, rows, width), lambda i: (0, jnp.maximum(i - 1, 0), 0, 0))
    if parts == 8:
        outs = (jax.ShapeDtypeStruct((4, 9 * share, width), BF16),) * 2
    else:
        outs = (
            jax.ShapeDtypeStruct((5 * width, width), BF16),
            jax.ShapeDtypeStruct((4 * width, width), BF16),
        )
    return pl.pallas_call(
        functools.partial(ffn_grads_kernel, parts),
        out_shape=outs,
        grid=(5,),
        in_specs=[pl.BlockSpec(memory_space=pltpu.SMEM), chunk, chunk]
        + [whole_spec(a) for a in (act2, attn, branch, grad)],
        out_specs=[ANY, ANY],
        scratch_shapes=[
            pltpu.VMEM((2, width, width), BF16),
            pltpu.VMEM((2, width, width), BF16),
            pltpu.SemaphoreType.DMA((2, 8)),
            pltpu.SemaphoreType.DMA((2, 2)),
        ],
        compiler_params=params(),
        cost_estimate=cost(18 * count * rows * width * width, 25e6),
        name="ffn_grads",
    )(scal, hid, gpre, act2, attn, branch, grad)


def last_kernel(parts, pieces, scal, vec, sums, x_in, gmid_in, dq_in, dk_in, dv_in, *rest):
    refs, rest = rest[:pieces], rest[pieces:]
    gin_out, outs = rest[0], rest[1:-13]
    weights, work, total, wsems, sems, x, gmid, dq, dk, dv, gin, in_sems, gin_sem = rest[-13:]
    count, rows, width = x.shape
    loads = [
        pltpu.make_async_copy(ref, buf, in_sems.at[j])
        for j, (ref, buf) in enumerate(
            ((x_in, x), (dq_in, dq), (dk_in, dk), (dv_in, dv), (gmid_in, gmid))
        )
    ]
    start(loads[:4])
    tokens = count * rows
    depth = weights.shape[1]
    share = width // parts
    copies = piece_copies(scal, first_pieces(refs), 0, depth, weights, wsems)
    start(copies)
    start(loads[4:])
    wait(loads[:1])
    unit, inverse = unit_of(x[...].reshape(tokens, width).astype(F32))
    act = (unit * vec[0:1] + vec[1:2]).astype(BF16)
    given, stores = [], []
    for j, ref in enumerate((dq, dk, dv)):
        wait(loads[1 + j : 2 + j])
        given.append(ref[...].reshape(tokens, width))
        work[j] = tn(act, given[j]).astype(BF16)
        if parts == 1:
            target = outs[0].at[pl.ds(j * width, width)]
            stores.append(pltpu.make_async_copy(work.at[j], target, sems.at[j, 0]))
            stores[-1].start()
        else:
            stores += spread_copies(scal, work.at[j], j * share, *outs, sems.at[j])
            start(stores[-8:])
    wait(copies)
    grad_one = jnp.zeros(unit.shape, F32)
    for j in range(3):
        weight = weights[:, j * share : (j + 1) * share, :].reshape(width, width)
        grad_one = grad_one + nt(given[j], weight)
    back = norm_back(grad_one * vec[0:1], unit, inverse)
    wait(loads[4:])
    gin[...] = (gmid[...].reshape(tokens, width) + back).astype(BF16).reshape(gin.shape)
    stores.append(pltpu.make_async_copy(gin, gin_out, gin_sem.at[0]))
    stores[-1].start()
    total[0:8] = (sums[0] + sums[1]).astype(BF16)
    total[8:32] = jnp.zeros((24, width), BF16)
    rows_now = [
        column_sum(grad_one * unit),
        column_sum(grad_one),
        column_sum(given[0].astype(F32)),
        column_sum(given[2].astype(F32)),
    ]
    for j, row in enumerate(rows_now):
        total[8 + j : 9 + j] = row.astype(BF16)
    if parts == 1:
        stores.append(
            pltpu.make_async_copy(total, outs[0].at[pl.ds(3 * width, 32)], sems.at[3, 0])
        )
        stores[-1].start()
    else:
        for rel in range(8):
            x_bit, y_bit = bits(rel)
            target = outs[rel & 1].at[2 * x_bit + y_bit, pl.ds(3 * share, 32)]
            stores.append(pltpu.make_async_copy(total, target, sems.at[3, rel]))
            stores[-1].start()
    wait(stores)


def last_call(scal, x, gmid, dq, dk, dv, vec, sums, first):
    parts, depth = (8, first[0].shape[1]) if len(first) > 1 else first[0].shape[:2]
    width = x.shape[2]
    share = width // parts
    gin = jax.ShapeDtypeStruct(x.shape, BF16)
    if parts == 1:
        outs = (jax.ShapeDtypeStruct((3 * width + 32, width), BF16),)
    else:
        outs = (jax.ShapeDtypeStruct((4, 3 * share + 32, width), BF16),) * 2
    return pl.pallas_call(
        functools.partial(last_kernel, parts, len(first)),
        out_shape=(gin, *outs),
        grid=(1,),
        in_specs=[pl.BlockSpec(memory_space=pltpu.SMEM), whole_spec(vec), whole_spec(sums)]
        + [ANY] * (5 + len(first)),
        out_specs=[ANY] * (1 + len(outs)),
        scratch_shapes=[
            pltpu.VMEM((parts, depth, width), BF16),
            pltpu.VMEM((3, width, width), BF16),
            pltpu.VMEM((32, width), BF16),
            pltpu.SemaphoreType.DMA((8,)),
            pltpu.SemaphoreType.DMA((4, 8)),
            pltpu.VMEM(x.shape, BF16),
            pltpu.VMEM(x.shape, F32),
            pltpu.VMEM(x.shape, BF16),
            pltpu.VMEM(x.shape, BF16),
            pltpu.VMEM(x.shape, BF16),
            pltpu.VMEM(x.shape, BF16),
            pltpu.SemaphoreType.DMA((5,)),
            pltpu.SemaphoreType.DMA((1,)),
        ],
        compiler_params=params(),
        cost_estimate=cost(12 * x.shape[0] * x.shape[1] * width * width, 20e6),
        name="last",
    )(scal, vec, sums, x, gmid, dq, dk, dv, *first)


def outer(ids):
    return (ids[0, 2] == 0) | (ids[0, 2] == 3)


def halves(ids, mine, got):
    swap = outer(ids)
    return jnp.where(swap, mine[...], got[...]).astype(F32), jnp.where(swap, got[...], mine[...]).astype(F32)


def finish_ffn_kernel(ids, mine, got, out_w, up_w, down_w, both):
    share, width = out_w.shape
    size = mine.shape[0]
    both[0:size], both[size:] = halves(ids, mine, got)
    out_w[...] = both[0:share]
    for c in range(4):
        up_w[:, c * width : (c + 1) * width] = both[(1 + c) * share : (2 + c) * share]
    down_w[...] = both[5 * share :]


def finish_ffn_call(ids, mine, got, share):
    width = mine.shape[1]
    outs = (
        jax.ShapeDtypeStruct((share, width), F32),
        jax.ShapeDtypeStruct((share, 4 * width), F32),
        jax.ShapeDtypeStruct((4 * share, width), F32),
    )
    return pl.pallas_call(
        finish_ffn_kernel,
        out_shape=outs,
        grid=(1,),
        in_specs=[pl.BlockSpec(memory_space=pltpu.SMEM), whole_spec(mine), whole_spec(got)],
        out_specs=[whole_spec(a) for a in outs],
        scratch_shapes=[pltpu.VMEM((2 * mine.shape[0], width), F32)],
        compiler_params=params(),
        cost_estimate=cost(0, 6e6),
        name="finish_ffn",
    )(ids, mine, got)


def finish_proj_kernel(ids, mine, got, q_w, k_w, v_w, *rest):
    *vectors, bias, both = rest
    share, width = q_w.shape
    size = mine.shape[0]
    both[0:size], both[size:] = halves(ids, mine, got)
    for j, out in enumerate((q_w, k_w, v_w)):
        out[...] = both[j * share : (j + 1) * share]
    me = ids[0, 3]
    row = lax.broadcasted_iota(jnp.int32, (width, LANES), 0)
    column = lax.broadcasted_iota(jnp.int32, (width, LANES), 1)
    pick = jnp.where(row == column + me * share, 1.0, 0.0).astype(BF16)
    picked = nn(both[3 * share : 3 * share + 16].astype(BF16), pick)
    for out, j in zip(vectors, (8, 9, 10, 11, 2, 0, 1, 3)):
        out[...] = picked[j : j + 1, 0:share]
    line = both[pl.ds(3 * share + 4 + me // 2, 1), :]
    bias[...] = jnp.where(me % 2 == 0, line[:, 0 : 4 * share], line[:, 4 * share :])


def finish_proj_call(ids, mine, got, share):
    width = mine.shape[1]
    outs = (
        [jax.ShapeDtypeStruct((share, width), F32)] * 3
        + [jax.ShapeDtypeStruct((1, share), F32)] * 8
        + [jax.ShapeDtypeStruct((1, 4 * share), F32)]
    )
    return pl.pallas_call(
        finish_proj_kernel,
        out_shape=outs,
        grid=(1,),
        in_specs=[pl.BlockSpec(memory_space=pltpu.SMEM), whole_spec(mine), whole_spec(got)],
        out_specs=[whole_spec(a) for a in outs],
        scratch_shapes=[pltpu.VMEM((2 * mine.shape[0], width), F32)],
        compiler_params=params(),
        cost_estimate=cost(0, 2e6),
        name="finish_proj",
    )(ids, mine, got)


RIGHT = [(0, 1), (1, 2), (2, 3)]
LEFT = [(1, 0), (2, 1), (3, 2)]
RIGHT_AGAIN = [(1, 2), (2, 3)]
LEFT_AGAIN = [(2, 1), (1, 0)]


def shifted(array, pairs):
    return lax.ppermute(array, "seq", pairs)


def crossed(array, distance):
    return lax.ppermute(array, "dp", [(i, i ^ distance) for i in range(8)])


def neighbours(array):
    left, right = shifted(array, RIGHT), shifted(array, LEFT)
    return left, right, shifted(left, RIGHT_AGAIN), shifted(right, LEFT_AGAIN)


def after(value, *others):
    return lax.optimization_barrier((value, *others))[0]


def add(*arrays):
    return sum(array.astype(F32) for array in arrays).astype(BF16)


PAIRS = [(0, 1), (1, 0), (2, 3), (3, 2)]
ACROSS = [(0, 3), (3, 0), (1, 2), (2, 1)]


class Reduction:
    def __init__(self, keep, send, place):
        self.keep, self.place, self.cut = keep, place, keep.shape[1] // 2
        self.got = crossed(send, 1)

    def second(self, *order):
        keep, got, cut = self.keep, after(self.got, *order), self.cut
        self.got = got
        one = add(keep[2:4, :cut], got[2:4, :cut])
        two = add(keep[1::2, cut:], got[1::2, cut:])
        self.more = crossed(one, 2), crossed(two, 4)
        return one, two

    def third(self, *order):
        keep, got, cut = self.keep, self.got, self.cut
        more = self.more = tuple(after(m, *order) for m in self.more)
        one = add(keep[1, :cut], got[1, :cut], more[0][1])
        two = add(keep[2, cut:], got[2, cut:], more[1][1])
        self.last = crossed(one, 4), crossed(two, 2)
        return one, two

    def fourth(self, *order):
        keep, got, cut = self.keep, self.got, self.cut
        last = tuple(after(m, *order) for m in self.last)
        one = add(keep[0, :cut], got[0, :cut], self.more[0][0], last[0])
        two = add(keep[0, cut:], got[0, cut:], self.more[1][0], last[1])
        return self.over_seq(one, two)

    def over_seq(self, one, two):
        outside = (self.place == 0) | (self.place == 3)
        self.mine = jnp.where(outside, one, two)
        other = jnp.where(outside, two, one)
        self.got = shifted(other, PAIRS)
        return self.mine, other

    def fifth(self, *order):
        self.mine = add(self.mine, after(self.got, *order))
        self.got = shifted(self.mine, ACROSS)
        return (self.mine,)

    def sixth(self, *order):
        self.mine = add(self.mine, after(self.got, *order))
        self.got = shifted(self.mine, PAIRS)
        return (self.mine,)

    def result(self):
        return self.mine, self.got


def windows(slots, place, me):
    seqs, _, rows = slots.shape
    whole = slots.reshape(seqs, 5 * rows)
    first, last = slots[:, 2, :1], slots[:, 2, -1:]
    low = jnp.sum((whole < first).astype(jnp.int32), axis=1)
    high = jnp.sum((whole <= last).astype(jnp.int32), axis=1)
    begin = (low // ROWS) * ROWS
    chunks = jnp.maximum((high - begin + rows - 1) // rows, 2)
    begin = jnp.minimum(begin, rows * (jnp.minimum(5, 6 - place) - chunks))
    other = jnp.zeros_like(begin)
    return jnp.stack([begin, chunks, other + place, other + me], axis=1)


def per_device(
    inputs,
    segment_ids,
    norm1_gain,
    norm1_shift,
    query_weight,
    query_bias,
    key_weight,
    value_weight,
    value_bias,
    out_weight,
    out_bias,
    norm2_gain,
    norm2_shift,
    fc1_weight,
    fc1_bias,
    fc2_weight,
    fc2_bias,
    grad_output,
):
    seqs, rows, width = inputs.shape
    devices = lax.axis_size("dp")
    share = query_weight.shape[0]
    place, me = lax.axis_index("seq"), lax.axis_index("dp")
    direct = devices == 8
    parts = 8 if direct else 1
    zero = jnp.zeros((), jnp.int32)
    ids = jnp.stack([zero, zero, place, me])[None]

    vectors = (
        norm1_gain, norm1_shift, query_bias, value_bias,
        out_bias, norm2_gain, norm2_shift, fc2_bias, fc1_bias,
    )
    tokens = tokens_call(inputs, segment_ids)
    query_bias = after(query_bias, tokens)
    vectors = vectors[:2] + (query_bias,) + vectors[3:]
    packed_one, packed_two = pack_call(
        (query_weight, key_weight, value_weight, out_weight, fc1_weight, fc2_weight), vectors
    )
    left, right = shifted(tokens, RIGHT), shifted(tokens, LEFT)
    if direct:
        near = jnp.stack(
            [after(packed_one, left, right)] + [crossed(packed_one, d) for d in (2, 4, 6)]
        )
        first = near, crossed(near, 1)
        vec = unpack_call(*first, ids)
        second = (lax.all_gather(after(packed_two, near), "dp", axis=0),)
    else:
        one = lax.all_gather(packed_one, "dp", axis=0)
        two = lax.all_gather(packed_two, "dp", axis=0)
        small = one[:, 3 * share :]
        vec = jnp.concatenate(
            [
                small[:, :8, :share].transpose(1, 0, 2).reshape(8, width),
                small[:, 8, : 4 * share].reshape(4, width),
                jnp.zeros((4, width), BF16),
            ]
        ).astype(F32)
        first = (
            jnp.concatenate(
                [one[:, j * share : (j + 1) * share].reshape(width, width) for j in range(3)]
                + [jnp.zeros((16, width), BF16)]
            )[None],
        )
        second = (
            jnp.concatenate(
                [two[:, j * share : (j + 1) * share].reshape(width, width) for j in range(5)]
                + [two[:, 5 * share :].reshape(4 * width, width)]
            )[None],
        )
    far_left, far_right = shifted(left, RIGHT_AGAIN), shifted(right, LEFT_AGAIN)

    qkv = project_call(ids, (inputs, left, right), vec, first, None, seqs, rows)
    far_left, far_right, *qkv = lax.optimization_barrier((far_left, far_right, *qkv))
    late_ids = after(segment_ids, qkv[0])

    def ids_of(message):
        return message[:, rows, :rows].astype(jnp.int32)

    before, beyond = jnp.full_like(late_ids, -1), jnp.full_like(late_ids, 99)
    slots = jnp.stack(
        [
            jnp.where(place >= 2, ids_of(far_left), before),
            jnp.where(place >= 1, ids_of(left), before),
            late_ids,
            jnp.where(place <= 2, ids_of(right), beyond),
            jnp.where(place <= 1, ids_of(far_right), beyond),
        ],
        axis=1,
    )
    scal = windows(slots, place, me)
    lane = lax.broadcasted_iota(jnp.int32, (1, 1, LANES), 2)
    seg = ((slots.reshape(seqs, 5 * rows)[:, :, None] == lane) | (lane >= 16)).astype(BF16)
    qf = jnp.where((lane < 4) & (lane != late_ids[:, :, None]), -BIG, 0.0).astype(BF16)
    qkv = list(project_call(scal, (far_left, far_right), vec, first, qkv, seqs, rows))

    attn, features = attend_call(0, seqs, scal, *qkv, seg, qf, None)

    split = ((0, 1), (1, seqs - 1))

    def middle(at, count, before):
        *shared, msg = middle_call(
            at, count, scal, inputs, attn, grad_output, features, second, vec, before
        )
        return shared, msg

    shared, msg_a = middle(*split[0], None)
    left_a, right_a = shifted(msg_a, RIGHT), shifted(msg_a, LEFT)
    far_a = shifted(msg_a, [(0, 2), (1, 3), (2, 0), (3, 1)])
    shared, msg_b = middle(*split[1], shared)
    left_a, right_a, far_a, msg_b = lax.optimization_barrier((left_a, right_a, far_a, msg_b))
    left_b, right_b = shifted(msg_b, RIGHT), shifted(msg_b, LEFT)
    out, hid, gpre, act2, branch, gmid, sums = shared
    ffn = ffn_grads_call(scal, parts, hid, gpre, act2, attn, branch, after(grad_output, msg_b))
    left_b, right_b, *ffn = lax.optimization_barrier((left_b, right_b, *ffn))
    all_a = msg_a, left_a, right_a, far_a, far_a
    far_left_b, far_right_b = shifted(left_b, RIGHT_AGAIN), shifted(right_b, LEFT_AGAIN)
    all_b = msg_b, left_b, right_b, far_left_b, far_right_b
    dq = query_grads_call(0, 1, scal, *qkv, msg_a, after(seg, ffn[0]), None)
    if direct:
        reduction = Reduction(*ffn, place)
        order = reduction.second(dq)
        dq = query_grads_call(1, 2, scal, *qkv, msg_b, after(seg, *order), dq)
        order = reduction.third(dq)
        dkv = key_grads_call(1, 1, scal, *qkv, after(seg, *order), all_b, None)
        order = reduction.fourth(dkv[0])
        dkv = key_grads_call(2, 1, scal, *qkv, after(seg, *order), all_b, tuple(dkv), 1)
        order = reduction.fifth(dkv[0])
        dkv = key_grads_call(0, 1, scal, *qkv, after(seg, *order), all_a, tuple(dkv))
        grad_inputs, *proj = last_call(
            scal, inputs, gmid, dq, *dkv, vec, sums, first
        )
        order = reduction.sixth(grad_inputs)
        tail = Reduction(proj[0], after(proj[1], *order), place)
        tail.second()
        tail.third()
        out_w, up_w, down_w = finish_ffn_call(ids, *reduction.result(), share)
        tail.fourth(out_w)
        tail.fifth()
        tail.sixth()
        q_w, k_w, v_w, *small, up_b = finish_proj_call(ids, *tail.result(), share)
        small = [s.reshape(share) for s in small]
        return (
            out, grad_inputs, small[0], small[1], q_w, small[2], k_w, v_w, small[3], out_w,
            small[4], small[5], small[6], up_w, up_b.reshape(4 * share), down_w, small[7],
        )

    dq = query_grads_call(1, 2, scal, *qkv, msg_b, seg, dq)
    dkv = key_grads_call(0, 1, scal, *qkv, seg, all_a, None)
    dkv = key_grads_call(1, seqs - 1, scal, *qkv, seg, all_b, tuple(dkv))
    grad_inputs, proj = last_call(scal, inputs, gmid, dq, *dkv, vec, sums, first)

    def reduced(array, count):
        cut = array.reshape(count, devices, -1, width).transpose(1, 0, 2, 3)
        cut = cut.reshape(devices, -1, width)
        part = lax.psum_scatter(cut, "dp", scatter_dimension=0, tiled=True)[0]
        return lax.psum(part, "seq").astype(F32)

    ffn_one, ffn_two = reduced(ffn[0], 5), reduced(ffn[1], 1)
    proj_w = reduced(proj[: 3 * width], 3)
    vectors = lax.psum(proj[3 * width : 3 * width + 16].astype(F32), ("dp", "seq"))
    mine = lax.dynamic_slice(vectors, (0, me * share), (16, share))
    up_grad = ffn_one[share:].reshape(4, share, width).transpose(1, 0, 2)
    up_bias = lax.dynamic_slice(vectors[4:8].reshape(4 * width), (me * 4 * share,), (4 * share,))
    return (
        out, grad_inputs, mine[8], mine[9], proj_w[:share], mine[10], proj_w[share : 2 * share],
        proj_w[2 * share :], mine[11], ffn_one[:share], mine[2], mine[0], mine[1],
        up_grad.reshape(share, 4 * width), up_bias, ffn_two, mine[3],
    )


def solution(mesh):
    token, matrix, vector = P("dp", "seq", None), P("dp", None), P("dp")
    return jax.shard_map(
        per_device,
        mesh=mesh,
        in_specs=(
            token, P("dp", "seq"), vector, vector, matrix, vector, matrix, matrix, vector,
            matrix, vector, vector, vector, matrix, vector, matrix, vector, token,
        ),
        out_specs=(
            token, token, vector, vector, matrix, vector, matrix, matrix, vector,
            matrix, vector, vector, vector, matrix, vector, matrix, vector,
        ),
        check_vma=False,
    )
```
